32 devices in a mesh: cuts: 4 (over y, core), sub: 8 (over z, x).
Axes of the slice: x: 2, y: 2, z: 4, core: 2. Of those that a mesh axis runs over, the one named last changes fastest.
Arguments:
- start_states: float32 [4, 16, 512, 128], P('cuts', 'sub'), may hold values from -8 to 8
- source: bfloat16 [16, 512, 128], P('sub'), may hold values from -3 to 3
- block_inverse: bfloat16 [16, 512, 512], P('sub'), may hold values from -1 to 1
- face_map: int32 [16, 2, 128], P('sub'), may hold values from 0 to 127, each once within a row
- transmissibility: float32 [16, 2, 128], P('sub'), may hold values from 7 to 11
- partner: int32 [16], replicated, may hold values from 0 to 15
- fracture_cond: float32 [16], replicated, may hold values from 0.3 to 3
Outputs:
- new_starts: float32 [4, 16, 512, 128], P('cuts', 'sub')
The draws below stay inside these ranges and needn't reach their ends.
All inputs are finite; a program needn't handle non-finite values.
Results may differ from the reference program's by a relative error of at most 0.0024.
Values sent between devices are 32-bit elements; how exact they have to be, the bound alone decides.
No kernel may reach another device: no remote copies, remote signals or barrier semaphores. Data moves between devices by JAX's collectives and lax.ppermute only.
A program may use at most 64 MiB of HBM per device.

```python
import math
import jax
import jax.numpy as jnp
from jax import lax

BLOCK = 512
FACE = 128
SCENARIOS = 128
FINE_STEPS = 4
SWEEPS = 4
SLICES = 4
BLOCKS = 16


def draw_block_inverse(key, part):
    first, second = jax.random.split(jax.random.fold_in(key, 11))
    noise = jnp.clip(jax.random.normal(first, (BLOCKS, BLOCK, BLOCK), jnp.float32), -4.0, 4.0)
    diag_gain = jax.random.uniform(second, (BLOCKS, BLOCK), jnp.float32, 0.9, 1.1)
    places = jnp.arange(BLOCK, dtype=jnp.int32)
    on_face = jnp.logical_or(places < FACE, places >= BLOCK - FACE)
    diag_value = jnp.where(on_face[None, :], 0.07, 0.6) * diag_gain
    root = jnp.sqrt(diag_value)
    eye = jnp.eye(BLOCK, dtype=jnp.float32)
    inner = eye[None] + 0.25 * noise / jnp.sqrt(1.0 * BLOCK)
    matrix = root[:, :, None] * inner * root[:, None, :]
    return matrix.astype(jnp.bfloat16)


def draw_start_states(key, part):
    first, second = jax.random.split(jax.random.fold_in(key, 23), 2)
    offset = jax.random.normal(first, (SLICES, BLOCKS, 1, SCENARIOS), jnp.float32)
    noise = 0.5 * jax.random.normal(second, (SLICES, BLOCKS, BLOCK, SCENARIOS), jnp.float32)
    return jnp.clip(offset + noise, -8.0, 8.0)


def touch_ends(entries, rng, least, high):
    longest = entries.shape.index(max(entries.shape))
    spots = []
    for shift in (0, 1):
        where = [jax.random.randint(jax.random.fold_in(rng, axis), (), 0, length) for axis, length in enumerate(entries.shape)]
        where[longest] = (where[longest] + shift) % entries.shape[longest]
        spots.append(tuple(where))
    return entries.at[spots[0]].set(least).at[spots[1]].set(high)


def levels(own_key, extent, cuts, smallest, high):
    gain, own = 1.0, jax.random.fold_in(own_key, 6)
    for position, parts in cuts:
        draws = jnp.exp(jax.random.uniform(jax.random.fold_in(own, position), (parts,), jnp.float32, smallest / len(cuts), high / len(cuts)))
        gain = gain * jnp.repeat(draws, extent[position] // parts).reshape([-1 if axis == position else 1 for axis in range(len(extent))])
    return gain


def normal_values(own_key, extent, scale, limit, shards=(), held_as=jnp.bfloat16):
    entries = scale * jax.random.normal(own_key, extent, jnp.float32)
    if shards:
        entries = entries * levels(own_key, extent, shards, -0.22, 0.18)
    return jnp.clip(entries, -limit, limit).astype(held_as)


def setup_inputs(seed: int = 0) -> dict:
    seeds = jax.random.split(jax.random.key(seed), 8)
    start_states = draw_start_states(jax.random.fold_in(seeds[7], 71), 0)
    source = normal_values(seeds[1], (BLOCKS, BLOCK, SCENARIOS), 0.5, 3.0, ((0, 8),))
    block_inverse = draw_block_inverse(jax.random.fold_in(seeds[7], 71), 0)
    face_map = jax.vmap(lambda own: jax.random.permutation(own, FACE))(jax.random.split(seeds[3], BLOCKS * 2)).reshape((BLOCKS, 2, FACE)).astype(jnp.int32)
    transmissibility = jnp.clip(jnp.exp(math.log(11.0) - 0.45198512 * jax.random.uniform(seeds[4], (BLOCKS, 2, FACE), jnp.float32) ** levels(seeds[4], (BLOCKS, 2, FACE), ((0, 8),), -0.2, 0.2)), 7.0, 11.0)
    partner = touch_ends(jax.random.randint(seeds[5], (BLOCKS,), 0, BLOCKS), jax.random.fold_in(seeds[5], 1), 0, BLOCKS - 1).astype(jnp.int32)
    fracture_cond = jnp.clip(jnp.exp(jax.random.uniform(seeds[6], (BLOCKS,), jnp.float32, math.log(0.3), math.log(3.0))), 0.3, 3.0)
    return dict(start_states=start_states, source=source, block_inverse=block_inverse, face_map=face_map, transmissibility=transmissibility, partner=partner, fracture_cond=fracture_cond)


def face_terms(below, above, face_map, transmissibility):
    low_in = transmissibility[:, 0, :, None] * jnp.take_along_axis(below, face_map[:, 0, :, None], axis=1)
    up_in = transmissibility[:, 1, :, None] * jnp.take_along_axis(above, face_map[:, 1, :, None], axis=1)
    return (low_in, up_in)

def sweep(state, rhs, inverse_wide, face_map, transmissibility):
    lower = state[:, :FACE]
    upper = state[:, BLOCK - FACE:]
    zero = jnp.zeros_like(upper[:1])
    below = jnp.concatenate([zero, upper[:-1]], axis=0)
    above = jnp.concatenate([lower[1:], zero], axis=0)
    low_in, up_in = face_terms(below, above, face_map, transmissibility)
    full = jnp.concatenate([rhs[:, :FACE] + low_in, rhs[:, FACE:BLOCK - FACE], rhs[:, BLOCK - FACE:] + up_in], axis=1)
    full = full.astype(jnp.bfloat16).astype(jnp.float32)
    return jnp.einsum('bij,bjr->bir', inverse_wide, full)

def coarse_map(partner, fracture_cond):
    count = partner.shape[0]
    places = jnp.arange(count, dtype=jnp.int32)
    chain = (jnp.abs(places[:, None] - places[None, :]) == 1).astype(jnp.float32)
    onehot = (partner[:, None] == places[None, :]).astype(jnp.float32)
    linked = fracture_cond[:, None] * onehot
    weights = chain + linked + linked.T
    lapl = jnp.diag(jnp.sum(weights, axis=1)) - weights
    system = jnp.eye(count, dtype=jnp.float32) + lapl
    factor = jnp.linalg.cholesky(system)
    return jax.scipy.linalg.cho_solve((factor, True), jnp.eye(count, dtype=jnp.float32))

def reference(start_states, source, block_inverse, face_map, transmissibility, partner, fracture_cond):
    inverse_wide = block_inverse.astype(jnp.float32)
    source_wide = source.astype(jnp.float32)

    def propagate(start):
        state = start
        for step in range(FINE_STEPS):
            rhs = state + source_wide
            for turn in range(SWEEPS):
                state = sweep(state, rhs, inverse_wide, face_map, transmissibility)
        return (state, jnp.mean(start, axis=1), jnp.mean(state, axis=1))
    ends, coarse_start, coarse_end = lax.map(propagate, start_states)
    coarse_op = coarse_map(partner, fracture_cond)
    high = lax.Precision.HIGHEST

    def advance(current, items):
        end_prev, mean_prev, mean_now, start_now = items
        fresh = end_prev + (current - mean_prev)[:, None, :]
        nxt = jnp.dot(coarse_op, current, precision=high) + (mean_now - jnp.dot(coarse_op, start_now, precision=high))
        return (nxt, fresh)
    items = (ends[:-1], coarse_end[:-1], coarse_end[1:], coarse_start[1:])
    last, fresh = lax.scan(advance, coarse_end[0], items)
    return jnp.concatenate([start_states[:1], fresh], axis=0)
```

```python
import functools

import jax
import jax.numpy as jnp
from jax import lax
from jax.experimental import pallas as pl
from jax.experimental.pallas import tpu as pltpu
from jax.sharding import PartitionSpec as P

FINE_STEPS = 4
SWEEPS = 4
F32 = jnp.float32
BF16 = jnp.bfloat16
HIGH = lax.Precision.HIGHEST


def dot(a, b, dims=((1,), (0,)), precision=None):
    return lax.dot_general(a, b, (dims, ((), ())), precision=precision, preferred_element_type=F32)


def transpose(x):
    return jnp.transpose(x, (1, 0))


def iota(shape, axis):
    return lax.broadcasted_iota(jnp.int32, shape, axis)


def call(body, out_shape, args, flops=1 << 28):
    size = sum(a.size * a.dtype.itemsize for a in list(args) + list(out_shape))
    vmem = pl.BlockSpec(memory_space=pltpu.VMEM)
    return pl.pallas_call(
        body,
        out_shape=out_shape,
        in_specs=[vmem] * len(args),
        out_specs=[vmem] * len(out_shape),
        compiler_params=pltpu.CompilerParams(vmem_limit_bytes=24 << 20),
        cost_estimate=pl.CostEstimate(flops=flops, bytes_accessed=size, transcendentals=0),
    )(*args)


def face_vector(i, count, rhs_ref, link_ref, low, up, below, above):
    face = low[0].shape[0]
    under = below if i == 0 else up[i - 1]
    over = above if i == count - 1 else low[i + 1]
    v_low = rhs_ref[i, :face] + link_ref[2 * i] * under
    v_up = rhs_ref[i, face : 2 * face] + link_ref[2 * i + 1] * over
    return v_low.astype(BF16), v_up.astype(BF16)


def face_sweep(count, ff_ref, y_ref, rhs_ref, link_ref, low, up, below, above):
    face = low[0].shape[0]
    vectors, new_low, new_up = [], [], []
    for i in range(count):
        v = jnp.concatenate(face_vector(i, count, rhs_ref, link_ref, low, up, below, above), axis=0)
        x = y_ref[i] + dot(ff_ref[i], v)
        vectors.append(v)
        new_low.append(x[:face])
        new_up.append(x[face:])
    return vectors, new_low, new_up


def outgoing(count, ff_ref, y_ref, rhs_ref, link_ref, low, up):
    face = low[0].shape[0]
    last = count - 1
    zero = jnp.zeros_like(low[0])
    v = jnp.concatenate(face_vector(last, count, rhs_ref, link_ref, low, up, zero, zero), axis=0)
    next_up = y_ref[last, face:] + dot(ff_ref[last, face:], v)
    v = jnp.concatenate(face_vector(0, count, rhs_ref, link_ref, low, up, zero, zero), axis=0)
    next_low = y_ref[0, :face] + dot(ff_ref[0, :face], v)
    return (up[last], next_up), (low[0], next_low)


def store_messages(upward, downward, first_ref, second_ref):
    even = lax.rem(lax.axis_index("sub"), 2) == 0
    at = 0
    for one, other in zip(upward, downward):
        rows = pl.ds(at, one.shape[0])
        first_ref[rows] = jnp.where(even, one, other)
        second_ref[rows] = jnp.where(even, other, one)
        at += one.shape[0]


def received(first_ref, second_ref, rows):
    even = lax.rem(lax.axis_index("sub"), 2) == 0
    first, second = first_ref[rows], second_ref[rows]
    return jnp.where(even, second, first), jnp.where(even, first, second)


def prepare(count, start_ref, source_ref, inverse_ref, map_ref, trans_ref,
            ff_ref, fm_ref, rf_ref, rm_ref, rhs_ref, source_out, y_ref, link_ref, faces_ref,
            mean_ref, first_ref, second_ref):
    width = start_ref.shape[1]
    face = map_ref.shape[2]
    inner = slice(face, width - face)
    ends = (slice(0, face), slice(width - face, width))
    me, size = lax.axis_index("sub"), lax.axis_size("sub")
    low, up, middle, means = [], [], [], []
    for i in range(count):
        perms = []
        for side in range(2):
            linked = iota((face, face), 0) == map_ref[i, side : side + 1, :]
            perm = linked.astype(F32).astype(BF16)
            column = jnp.sum(
                jnp.where(linked, trans_ref[i, side : side + 1, :], 0.0), axis=1, keepdims=True
            )
            if i == 0 and side == 0:
                column = jnp.where(me == 0, 0.0, column)
            if i == count - 1 and side == 1:
                column = jnp.where(me == size - 1, 0.0, column)
            link_ref[2 * i + side] = jnp.broadcast_to(column, (face, start_ref.shape[2]))
            perms.append(perm)
            to = slice(side * face, (side + 1) * face)
            columns = dot(inverse_ref[i, :, ends[side]], perm, ((1,), (1,))).astype(BF16)
            ff_ref[i, :face, to] = columns[:face]
            ff_ref[i, face:, to] = columns[width - face :]
            rf_ref[i, 2 * face :, to] = columns[inner]
            value = start_ref[i, ends[side]]
            high = value.astype(BF16)
            rest = value - high.astype(F32)
            mid = rest.astype(BF16)
            tail = (rest - mid.astype(F32)).astype(BF16)
            permuted = dot(perm, high) + dot(perm, mid) + dot(perm, tail)
            wells = dot(perm, source_ref[i, ends[side]])
            rhs_ref[i, to] = permuted + wells
            source_out[i, to] = wells
        fm_ref[i, :face] = inverse_ref[i, :face, inner]
        fm_ref[i, face:] = inverse_ref[i, width - face :, inner]
        for side in range(2):
            to = slice(side * face, (side + 1) * face)
            rf_ref[i, to] = dot(perms[side], ff_ref[i, to]).astype(BF16)
            rm_ref[i, to] = dot(perms[side], fm_ref[i, to]).astype(BF16)
        rm_ref[i, 2 * face :] = inverse_ref[i, inner, inner]
        wells = source_ref[i, inner].astype(F32)
        rhs_ref[i, 2 * face :] = start_ref[i, inner] + wells
        source_out[i, 2 * face :] = wells
        low.append(start_ref[i, ends[0]])
        up.append(start_ref[i, ends[1]])
        faces_ref[i, :face] = low[i]
        faces_ref[i, face:] = up[i]
        mean_ref[i : i + 1] = jnp.sum(start_ref[i], axis=0, keepdims=True) / width
        y_ref[i] = dot(fm_ref[i], rhs_ref[i, 2 * face :].astype(BF16))
    upward, downward = outgoing(count, ff_ref, y_ref, rhs_ref, link_ref, low, up)
    last = count - 1
    upward += (ff_ref[last, face:, face:].astype(F32), transpose(link_ref[2 * last + 1])[:8])
    downward += (ff_ref[0, :face, :face].astype(F32), transpose(link_ref[0])[:8])
    store_messages(upward, downward, first_ref, second_ref)


def load_faces(count, faces_ref):
    face = faces_ref.shape[1] // 2
    return [faces_ref[i, :face] for i in range(count)], [faces_ref[i, face:] for i in range(count)]


def window(count, first_ref, second_ref, ff_ref, y_ref, rhs_ref, link_ref, faces_ref, near_ref, near_link_ref):
    low, up = load_faces(count, faces_ref)
    face = low[0].shape[0]
    below, above = received(first_ref, second_ref, slice(0, face))
    next_below, next_above = received(first_ref, second_ref, slice(face, 2 * face))
    next_below += dot(near_ref[0], (near_link_ref[0] * low[0]).astype(BF16))
    next_above += dot(near_ref[1], (near_link_ref[1] * up[count - 1]).astype(BF16))
    _, low, up = face_sweep(count, ff_ref, y_ref, rhs_ref, link_ref, low, up, below, above)
    return face_sweep(count, ff_ref, y_ref, rhs_ref, link_ref, low, up, next_below, next_above)


def middle_window(count, opening, *refs):
    if opening:
        (first_ref, second_ref, ff_ref, y_ref, rhs_ref, link_ref, faces_ref,
         new_faces, out_first, out_second, near_ref, near_link_ref) = refs
        face = faces_ref.shape[1] // 2
        for k, part in enumerate(received(first_ref, second_ref, slice(2 * face, 3 * face))):
            near_ref[k] = part.astype(BF16)
        for k, part in enumerate(received(first_ref, second_ref, slice(3 * face, 3 * face + 8))):
            near_link_ref[k] = transpose(jnp.broadcast_to(part[:1], (face, face)))
    else:
        (first_ref, second_ref, ff_ref, y_ref, rhs_ref, link_ref, faces_ref, near_ref, near_link_ref,
         new_faces, out_first, out_second) = refs
        face = faces_ref.shape[1] // 2
    _, low, up = window(
        count, first_ref, second_ref, ff_ref, y_ref, rhs_ref, link_ref, faces_ref, near_ref, near_link_ref
    )
    for i in range(count):
        new_faces[i, :face] = low[i]
        new_faces[i, face:] = up[i]
    store_messages(*outgoing(count, ff_ref, y_ref, rhs_ref, link_ref, low, up), out_first, out_second)


def step_window(count, first_ref, second_ref, ff_ref, y_ref, rhs_ref, link_ref, faces_ref, near_ref,
                near_link_ref, fm_ref, rf_ref, rm_ref, source_ref,
                new_faces, out_first, out_second, new_rhs, new_y):
    face = faces_ref.shape[1] // 2
    vectors, low, up = window(
        count, first_ref, second_ref, ff_ref, y_ref, rhs_ref, link_ref, faces_ref, near_ref, near_link_ref
    )
    for i in range(count):
        new_faces[i, :face] = low[i]
        new_faces[i, face:] = up[i]
        state = dot(rf_ref[i], vectors[i]) + dot(rm_ref[i], rhs_ref[i, 2 * face :].astype(BF16))
        rhs = state + source_ref[i]
        new_rhs[i] = rhs
        new_y[i] = dot(fm_ref[i], rhs[2 * face :].astype(BF16))
    store_messages(*outgoing(count, ff_ref, new_y, new_rhs, link_ref, low, up), out_first, out_second)


def last_window(count, first_ref, second_ref, ff_ref, y_ref, rhs_ref, link_ref, faces_ref, near_ref,
                near_link_ref, rf_ref, rm_ref, mean_ref, end_ref, means_ref):
    face = faces_ref.shape[1] // 2
    width = end_ref.shape[1]
    vectors, low, up = window(
        count, first_ref, second_ref, ff_ref, y_ref, rhs_ref, link_ref, faces_ref, near_ref, near_link_ref
    )
    rows = []
    for i in range(count):
        inner = dot(rf_ref[i, 2 * face :], vectors[i]) + dot(
            rm_ref[i, 2 * face :], rhs_ref[i, 2 * face :].astype(BF16)
        )
        end_ref[i, :face] = low[i]
        end_ref[i, face : width - face] = inner
        end_ref[i, width - face :] = up[i]
        total = jnp.sum(low[i], axis=0, keepdims=True) + jnp.sum(up[i], axis=0, keepdims=True)
        rows.append((total + jnp.sum(inner, axis=0, keepdims=True)) / width)
    rows += [mean_ref[i : i + 1] for i in range(count)]
    block = jnp.concatenate(rows, axis=0)
    for k in range(means_ref.shape[0] // (2 * count)):
        means_ref[2 * count * k : 2 * count * (k + 1)] = block


def coarse_operator(partner_row, partner_col, cond_row, cond_col, out_ref):
    n = out_ref.shape[0]
    row, col = iota((n, n), 0), iota((n, n), 1)
    chain = (jnp.abs(row - col) == 1).astype(F32)
    weights = (
        chain
        + jnp.where(partner_col[...] == col, cond_col[...], 0.0)
        + jnp.where(partner_row[...] == row, cond_row[...], 0.0)
    )
    eye = (row == col).astype(F32)
    m = eye + eye * jnp.sum(weights, axis=1, keepdims=True) - weights
    for i in range(n):
        pivot = 1.0 / m[i : i + 1, i : i + 1]
        line = m[i : i + 1, :] * pivot
        column = m[:, i : i + 1]
        inner = jnp.where(col == i, -column * pivot, m - column * line)
        m = jnp.where(row == i, jnp.where(col == i, pivot, line), inner)
    out_ref[...] = m


def correct(count, slices, means_ref, op_ref, previous_ref, start_ref, out_ref):
    here = lax.axis_index("cuts")
    me = lax.axis_index("sub")
    blocks = op_ref.shape[0]
    per = means_ref.shape[0] // slices
    shape = (blocks, per)
    block = iota(shape, 0)
    place = iota(shape, 1)
    unit, item = place // (2 * count), lax.rem(place, 2 * count)
    take_end = (unit * count + item == block) & (item < count)
    take_start = (unit * count + item - count == block) & (item >= count)
    take_end = take_end.astype(F32)
    take_start = take_start.astype(F32)
    op = op_ref[...]
    shift = jnp.zeros((blocks, means_ref.shape[1]), F32)
    for s in range(1, slices - 1):
        jump = dot(take_end, means_ref[(s - 1) * per : s * per], precision=HIGH) - dot(
            take_start, means_ref[s * per : (s + 1) * per], precision=HIGH
        )
        shift = jnp.where(s < here, dot(op, shift + jump, precision=HIGH), shift)
    chosen = (iota((8, blocks), 1) == me * count + iota((8, blocks), 0)).astype(F32)
    mine = dot(chosen, shift, precision=HIGH)
    later = here > 0
    for i in range(count):
        out_ref[i] = jnp.where(later, previous_ref[i] + mine[i : i + 1], start_ref[i])


def exchange(first, second):
    size = lax.axis_size("sub")
    pairs = [(i, i ^ 1) for i in range(size)]
    other = [(i, (i + (1 if i % 2 else -1)) % size) for i in range(size)]
    far = lax.ppermute(second, "sub", other)
    near = lax.ppermute(first, "sub", pairs)
    return near, far


def on_device(slices, start_states, source, block_inverse, face_map, transmissibility, partner, fracture_cond):
    start = start_states[0]
    count, width, scenarios = start.shape
    face = face_map.shape[-1]
    inner = width - 2 * face
    sub = lax.axis_size("sub")
    sds = jax.ShapeDtypeStruct
    message = sds((2 * face, scenarios), F32)
    opening = sds((3 * face + 8, scenarios), F32)
    faces_shape = sds((count, 2 * face, scenarios), F32)
    rhs_shape = sds((count, width, scenarios), F32)
    ff, fm, rf, rm, rhs, wells, y, link, faces, mean, first, second = call(
        functools.partial(prepare, count),
        [
            sds((count, 2 * face, 2 * face), BF16),
            sds((count, 2 * face, inner), BF16),
            sds((count, width, 2 * face), BF16),
            sds((count, width, inner), BF16),
            rhs_shape,
            rhs_shape,
            faces_shape,
            sds((2 * count, face, scenarios), F32),
            faces_shape,
            sds((count, scenarios), F32),
            opening,
            opening,
        ],
        (start, source, block_inverse, face_map, transmissibility),
    )
    blocks = partner.shape[0]
    (op,) = call(
        coarse_operator,
        [sds((blocks, blocks), F32)],
        (
            partner.reshape(1, blocks),
            partner.reshape(blocks, 1),
            fracture_cond.reshape(1, blocks),
            fracture_cond.reshape(blocks, 1),
        ),
    )
    near = near_link = None
    for step in range(FINE_STEPS):
        for turn in range(0, SWEEPS, 2):
            first, second = exchange(first, second)
            common = (first, second, ff, y, rhs, link, faces)
            if turn < SWEEPS - 2:
                outs = [faces_shape, message, message]
                if near is None:
                    outs += [sds((2, face, face), BF16), sds((2, face, scenarios), F32)]
                    faces, first, second, near, near_link = call(
                        functools.partial(middle_window, count, True), outs, common
                    )
                else:
                    faces, first, second = call(
                        functools.partial(middle_window, count, False), outs, common + (near, near_link)
                    )
            elif step < FINE_STEPS - 1:
                faces, first, second, rhs, y = call(
                    functools.partial(step_window, count),
                    [faces_shape, message, message, rhs_shape, faces_shape],
                    common + (near, near_link, fm, rf, rm, wells),
                )
            else:
                end, means = call(
                    functools.partial(last_window, count),
                    [rhs_shape, sds((slices * sub * 2 * count, scenarios), F32)],
                    common + (near, near_link, rf, rm, mean),
                )
    previous = lax.ppermute(end, "cuts", [(i, (i + 1) % slices) for i in range(slices)])
    means = lax.all_to_all(means, ("cuts", "sub"), 0, 0, tiled=True)
    (result,) = call(
        functools.partial(correct, count, slices), [rhs_shape], (means, op, previous, start)
    )
    return result[None]


def solution(mesh):
    slices = mesh.shape["cuts"]
    in_specs = (
        P("cuts", "sub", None, None),
        P("sub", None, None),
        P("sub", None, None),
        P("sub", None, None),
        P("sub", None, None),
        P(),
        P(),
    )
    return jax.shard_map(
        functools.partial(on_device, slices),
        mesh=mesh,
        in_specs=in_specs,
        out_specs=P("cuts", "sub", None, None),
        check_vma=False,
    )
```

```python
import functools

import jax
import jax.numpy as jnp
from jax import lax
from jax.experimental import pallas as pl
from jax.experimental.pallas import tpu as pltpu
from jax.sharding import PartitionSpec as P

FINE_STEPS = 4
SWEEPS = 4
F32 = jnp.float32
BF16 = jnp.bfloat16
HIGH = lax.Precision.HIGHEST


def dot(a, b, dims=((1,), (0,)), precision=None):
    return lax.dot_general(a, b, (dims, ((), ())), precision=precision, preferred_element_type=F32)


def transpose(x):
    return jnp.transpose(x, (1, 0))


def iota(shape, axis):
    return lax.broadcasted_iota(jnp.int32, shape, axis)


def call(body, out_shape, args, flops=1 << 28, stay=(), stay_out=(), scratch=()):
    size = sum(a.size * a.dtype.itemsize for a in list(args) + list(out_shape))
    vmem = pl.BlockSpec(memory_space=pltpu.VMEM)
    hbm = pl.BlockSpec(memory_space=pltpu.HBM)
    return pl.pallas_call(
        body,
        out_shape=out_shape,
        in_specs=[hbm if k in stay else vmem for k in range(len(args))],
        out_specs=[hbm if k in stay_out else vmem for k in range(len(out_shape))],
        scratch_shapes=list(scratch),
        compiler_params=pltpu.CompilerParams(vmem_limit_bytes=24 << 20),
        cost_estimate=pl.CostEstimate(flops=flops, bytes_accessed=size, transcendentals=0),
    )(*args)


def face_vector(i, count, rhs_ref, link_ref, low, up, below, above):
    face = low[0].shape[0]
    under = below if i == 0 else up[i - 1]
    over = above if i == count - 1 else low[i + 1]
    v_low = rhs_ref[i, :face] + link_ref[2 * i] * under
    v_up = rhs_ref[i, face : 2 * face] + link_ref[2 * i + 1] * over
    return v_low.astype(BF16), v_up.astype(BF16)


def face_sweep(count, ff_ref, y_ref, rhs_ref, link_ref, low, up, below, above):
    face = low[0].shape[0]
    vectors, new_low, new_up = [], [], []
    for i in range(count):
        v = jnp.concatenate(face_vector(i, count, rhs_ref, link_ref, low, up, below, above), axis=0)
        x = y_ref[i] + dot(ff_ref[i], v)
        vectors.append(v)
        new_low.append(x[:face])
        new_up.append(x[face:])
    return vectors, new_low, new_up


def outgoing(count, ff_ref, y_ref, rhs_ref, link_ref, low, up):
    face = low[0].shape[0]
    last = count - 1
    zero = jnp.zeros_like(low[0])
    v = jnp.concatenate(face_vector(last, count, rhs_ref, link_ref, low, up, zero, zero), axis=0)
    next_up = y_ref[last, face:] + dot(ff_ref[last, face:], v)
    v = jnp.concatenate(face_vector(0, count, rhs_ref, link_ref, low, up, zero, zero), axis=0)
    next_low = y_ref[0, :face] + dot(ff_ref[0, :face], v)
    return (up[last], next_up), (low[0], next_low)


def store_messages(upward, downward, first_ref, second_ref):
    even = lax.rem(lax.axis_index("sub"), 2) == 0
    at = 0
    for one, other in zip(upward, downward):
        rows = pl.ds(at, one.shape[0])
        first_ref[rows] = jnp.where(even, one, other)
        second_ref[rows] = jnp.where(even, other, one)
        at += one.shape[0]


def received(first_ref, second_ref, rows):
    even = lax.rem(lax.axis_index("sub"), 2) == 0
    first, second = first_ref[rows], second_ref[rows]
    return jnp.where(even, second, first), jnp.where(even, first, second)


def prepare(count, start_hbm, source_hbm, inverse_hbm, map_hbm, trans_hbm,
            ff_ref, fm_ref, rf_ref, rm_ref, rhs_ref, source_out, y_ref, link_ref, faces_ref,
            mean_ref, first_ref, second_ref,
            start_ref, source_ref, inverse_ref, map_ref, trans_ref, sems):
    copies = [
        pltpu.make_async_copy(map_hbm, map_ref, sems.at[0]),
        pltpu.make_async_copy(trans_hbm, trans_ref, sems.at[1]),
    ]
    for i in range(count):
        copies += [
            pltpu.make_async_copy(src.at[i], dst.at[i], sems.at[2 + 3 * i + k])
            for k, (src, dst) in enumerate(
                ((inverse_hbm, inverse_ref), (start_hbm, start_ref), (source_hbm, source_ref))
            )
        ]
    for copy in copies:
        copy.start()
    copies[0].wait()
    copies[1].wait()
    width = start_ref.shape[1]
    face = map_ref.shape[2]
    inner = slice(face, width - face)
    ends = (slice(0, face), slice(width - face, width))
    me, size = lax.axis_index("sub"), lax.axis_size("sub")
    low, up, middle, means = [], [], [], []
    for i in range(count):
        perms = []
        for copy in copies[2 + 3 * i : 5 + 3 * i]:
            copy.wait()
        for side in range(2):
            linked = iota((face, face), 0) == map_ref[i, side : side + 1, :]
            perm = linked.astype(F32).astype(BF16)
            column = jnp.sum(
                jnp.where(linked, trans_ref[i, side : side + 1, :], 0.0), axis=1, keepdims=True
            )
            if i == 0 and side == 0:
                column = jnp.where(me == 0, 0.0, column)
            if i == count - 1 and side == 1:
                column = jnp.where(me == size - 1, 0.0, column)
            link_ref[2 * i + side] = jnp.broadcast_to(column, (face, start_ref.shape[2]))
            perms.append(perm)
            to = slice(side * face, (side + 1) * face)
            columns = dot(inverse_ref[i, :, ends[side]], perm, ((1,), (1,))).astype(BF16)
            ff_ref[i, :face, to] = columns[:face]
            ff_ref[i, face:, to] = columns[width - face :]
            rf_ref[i, 2 * face :, to] = columns[inner]
            value = start_ref[i, ends[side]]
            high = value.astype(BF16)
            rest = value - high.astype(F32)
            mid = rest.astype(BF16)
            tail = (rest - mid.astype(F32)).astype(BF16)
            permuted = dot(perm, high) + dot(perm, mid) + dot(perm, tail)
            wells = dot(perm, source_ref[i, ends[side]])
            rhs_ref[i, to] = permuted + wells
            source_out[i, to] = wells
        fm_ref[i, :face] = inverse_ref[i, :face, inner]
        fm_ref[i, face:] = inverse_ref[i, width - face :, inner]
        for side in range(2):
            to = slice(side * face, (side + 1) * face)
            rf_ref[i, to] = dot(perms[side], ff_ref[i, to]).astype(BF16)
            rm_ref[i, to] = dot(perms[side], fm_ref[i, to]).astype(BF16)
        rm_ref[i, 2 * face :] = inverse_ref[i, inner, inner]
        wells = source_ref[i, inner].astype(F32)
        rhs_ref[i, 2 * face :] = start_ref[i, inner] + wells
        source_out[i, 2 * face :] = wells
        low.append(start_ref[i, ends[0]])
        up.append(start_ref[i, ends[1]])
        faces_ref[i, :face] = low[i]
        faces_ref[i, face:] = up[i]
        mean_ref[i : i + 1] = jnp.sum(start_ref[i], axis=0, keepdims=True) / width
        y_ref[i] = dot(fm_ref[i], rhs_ref[i, 2 * face :].astype(BF16))
    upward, downward = outgoing(count, ff_ref, y_ref, rhs_ref, link_ref, low, up)
    last = count - 1
    upward += (ff_ref[last, face:, face:].astype(F32), transpose(link_ref[2 * last + 1])[:8])
    downward += (ff_ref[0, :face, :face].astype(F32), transpose(link_ref[0])[:8])
    store_messages(upward, downward, first_ref, second_ref)


def load_faces(count, faces_ref):
    face = faces_ref.shape[1] // 2
    return [faces_ref[i, :face] for i in range(count)], [faces_ref[i, face:] for i in range(count)]


def window(count, first_ref, second_ref, ff_ref, y_ref, rhs_ref, link_ref, faces_ref, near_ref, near_link_ref):
    low, up = load_faces(count, faces_ref)
    face = low[0].shape[0]
    below, above = received(first_ref, second_ref, slice(0, face))
    next_below, next_above = received(first_ref, second_ref, slice(face, 2 * face))
    next_below += dot(near_ref[0], (near_link_ref[0] * low[0]).astype(BF16))
    next_above += dot(near_ref[1], (near_link_ref[1] * up[count - 1]).astype(BF16))
    _, low, up = face_sweep(count, ff_ref, y_ref, rhs_ref, link_ref, low, up, below, above)
    return face_sweep(count, ff_ref, y_ref, rhs_ref, link_ref, low, up, next_below, next_above)


def middle_window(count, opening, *refs):
    if opening:
        (first_ref, second_ref, ff_ref, y_ref, rhs_ref, link_ref, faces_ref,
         new_faces, out_first, out_second, near_ref, near_link_ref) = refs
        face = faces_ref.shape[1] // 2
        for k, part in enumerate(received(first_ref, second_ref, slice(2 * face, 3 * face))):
            near_ref[k] = part.astype(BF16)
        for k, part in enumerate(received(first_ref, second_ref, slice(3 * face, 3 * face + 8))):
            near_link_ref[k] = transpose(jnp.broadcast_to(part[:1], (face, face)))
    else:
        (first_ref, second_ref, ff_ref, y_ref, rhs_ref, link_ref, faces_ref, near_ref, near_link_ref,
         new_faces, out_first, out_second) = refs
        face = faces_ref.shape[1] // 2
    _, low, up = window(
        count, first_ref, second_ref, ff_ref, y_ref, rhs_ref, link_ref, faces_ref, near_ref, near_link_ref
    )
    for i in range(count):
        new_faces[i, :face] = low[i]
        new_faces[i, face:] = up[i]
    store_messages(*outgoing(count, ff_ref, y_ref, rhs_ref, link_ref, low, up), out_first, out_second)


def step_window(count, first_ref, second_ref, ff_ref, y_ref, rhs_ref, link_ref, faces_ref, near_ref,
                near_link_ref, fm_ref, rf_ref, base_ref, source_ref,
                new_faces, out_first, out_second, new_rhs, new_y):
    face = faces_ref.shape[1] // 2
    vectors, low, up = window(
        count, first_ref, second_ref, ff_ref, y_ref, rhs_ref, link_ref, faces_ref, near_ref, near_link_ref
    )
    for i in range(count):
        new_faces[i, :face] = low[i]
        new_faces[i, face:] = up[i]
        rhs = base_ref[i] + dot(rf_ref[i], vectors[i]) + source_ref[i]
        new_rhs[i] = rhs
        new_y[i] = dot(fm_ref[i], rhs[2 * face :].astype(BF16))
    store_messages(*outgoing(count, ff_ref, new_y, new_rhs, link_ref, low, up), out_first, out_second)


def inner_base(count, rhs_ref, rm_ref, base_ref):
    for i in range(count):
        face = (rhs_ref.shape[1] - rm_ref.shape[2]) // 2
        base_ref[i] = dot(rm_ref[i], rhs_ref[i, 2 * face :].astype(BF16))


def end_base(count, rhs_ref, rm_ref, y_ref, base_ref):
    face = y_ref.shape[1] // 2
    for i in range(count):
        base_ref[i, : 2 * face] = y_ref[i]
        base_ref[i, 2 * face :] = dot(rm_ref[i, 2 * face :], rhs_ref[i, 2 * face :].astype(BF16))


def last_window(count, first_ref, second_ref, ff_ref, y_ref, rhs_ref, link_ref, faces_ref, near_ref,
                near_link_ref, rf_ref, base_ref, mean_ref, vector_ref, means_ref):
    face = faces_ref.shape[1] // 2
    width = base_ref.shape[1]
    vectors, low, up = window(
        count, first_ref, second_ref, ff_ref, y_ref, rhs_ref, link_ref, faces_ref, near_ref, near_link_ref
    )
    rows = []
    for i in range(count):
        vector_ref[i] = vectors[i].astype(F32)
        inner = base_ref[i, 2 * face :] + dot(rf_ref[i, 2 * face :], vectors[i])
        total = jnp.sum(low[i], axis=0, keepdims=True) + jnp.sum(up[i], axis=0, keepdims=True)
        rows.append((total + jnp.sum(inner, axis=0, keepdims=True)) / width)
    rows += [mean_ref[i : i + 1] for i in range(count)]
    block = jnp.concatenate(rows, axis=0)
    for k in range(means_ref.shape[0] // (2 * count)):
        means_ref[2 * count * k : 2 * count * (k + 1)] = block


def previous_end(count, base_ref, vector_ref, ff_ref, rf_ref, end_ref):
    face = vector_ref.shape[1] // 2
    width = base_ref.shape[1]
    for i in range(count):
        v = vector_ref[i].astype(BF16)
        faces = base_ref[i, : 2 * face] + dot(ff_ref[i], v)
        end_ref[i, :face] = faces[:face]
        end_ref[i, face : width - face] = base_ref[i, 2 * face :] + dot(rf_ref[i, 2 * face :], v)
        end_ref[i, width - face :] = faces[face:]


def coarse_operator(count, slices, partner_row, partner_col, cond_row, cond_col, out_ref):
    n = partner_row.shape[1]
    row, col = iota((n, n), 0), iota((n, n), 1)
    chain = (jnp.abs(row - col) == 1).astype(F32)
    weights = (
        chain
        + jnp.where(partner_col[...] == col, cond_col[...], 0.0)
        + jnp.where(partner_row[...] == row, cond_row[...], 0.0)
    )
    eye = (row == col).astype(F32)
    m = eye + eye * jnp.sum(weights, axis=1, keepdims=True) - weights
    for i in range(n):
        pivot = 1.0 / m[i : i + 1, i : i + 1]
        line = m[i : i + 1, :] * pivot
        column = m[:, i : i + 1]
        inner = jnp.where(col == i, -column * pivot, m - column * line)
        m = jnp.where(row == i, jnp.where(col == i, pivot, line), inner)
    here, me = lax.axis_index("cuts"), lax.axis_index("sub")
    per = out_ref.shape[1] // slices
    shape = (n, per)
    block, place = iota(shape, 0), iota(shape, 1)
    unit, item = place // (2 * count), lax.rem(place, 2 * count)
    take_end = ((unit * count + item == block) & (item < count)).astype(F32)
    take_start = ((unit * count + item - count == block) & (item >= count)).astype(F32)
    power = (iota((8, n), 1) == me * count + iota((8, n), 0)).astype(F32)
    none = jnp.zeros_like(power)
    weight = [none] * slices
    for s in reversed(range(1, slices - 1)):
        power = jnp.where(s < here, dot(power, m, precision=HIGH), power)
        weight[s] = jnp.where(s < here, power, none)
    for s in range(slices):
        after = weight[s + 1] if s + 1 < slices else none
        out_ref[:, s * per : (s + 1) * per] = dot(after, take_end, precision=HIGH) - dot(
            weight[s], take_start, precision=HIGH
        )


def correct(count, means_ref, op_ref, previous_ref, start_ref, out_hbm, out_ref, sems):
    later = lax.axis_index("cuts") > 0
    mine = dot(op_ref[...], means_ref[...], precision=HIGH)
    copies = []
    for i in range(count):
        out_ref[i] = jnp.where(later, previous_ref[i] + mine[i : i + 1], start_ref[i])
        copies.append(pltpu.make_async_copy(out_ref.at[i], out_hbm.at[i], sems.at[i]))
        copies[i].start()
    for copy in copies:
        copy.wait()


def exchange(first, second):
    size, slices = lax.axis_size("sub"), lax.axis_size("cuts")
    pairs = [(i, i ^ 1) for i in range(size)]
    other = []
    for c in range(slices):
        for i in range(size):
            j = i + (1 if i % 2 else -1)
            d = c
            if not 0 <= j < size:
                d, j = (c ^ 1 if c ^ 1 < slices else c), i
            other.append((c * size + i, d * size + j))
    far = lax.ppermute(second, ("cuts", "sub"), other)
    near = lax.ppermute(first, "sub", pairs)
    return near, far


def on_device(slices, start_states, source, block_inverse, face_map, transmissibility, partner, fracture_cond):
    start = start_states[0]
    count, width, scenarios = start.shape
    face = face_map.shape[-1]
    inner = width - 2 * face
    sub = lax.axis_size("sub")
    sds = jax.ShapeDtypeStruct
    message = sds((2 * face, scenarios), F32)
    opening = sds((3 * face + 8, scenarios), F32)
    faces_shape = sds((count, 2 * face, scenarios), F32)
    rhs_shape = sds((count, width, scenarios), F32)
    ff, fm, rf, rm, rhs, wells, y, link, faces, mean, first, second = call(
        functools.partial(prepare, count),
        [
            sds((count, 2 * face, 2 * face), BF16),
            sds((count, 2 * face, inner), BF16),
            sds((count, width, 2 * face), BF16),
            sds((count, width, inner), BF16),
            rhs_shape,
            rhs_shape,
            faces_shape,
            sds((2 * count, face, scenarios), F32),
            faces_shape,
            sds((count, scenarios), F32),
            opening,
            opening,
        ],
        [pltpu.with_memory_space_constraint(a, pltpu.HBM) for a in (start, source, block_inverse, face_map, transmissibility)],
        stay=range(5),
        scratch=[pltpu.VMEM(a.shape, a.dtype) for a in (start, source, block_inverse, face_map, transmissibility)]
        + [pltpu.SemaphoreType.DMA((2 + 3 * count,))],
    )
    blocks = partner.shape[0]
    (op,) = call(
        functools.partial(coarse_operator, count, slices),
        [sds((8, slices * sub * 2 * count), F32)],
        (
            partner.reshape(1, blocks),
            partner.reshape(blocks, 1),
            fracture_cond.reshape(1, blocks),
            fracture_cond.reshape(blocks, 1),
        ),
    )
    near = near_link = None
    ring = [(i, (i + 1) % slices) for i in range(slices)]
    for step in range(FINE_STEPS):
        if step < FINE_STEPS - 1:
            (base,) = call(functools.partial(inner_base, count), [rhs_shape], (rhs, rm))
        else:
            (base,) = call(functools.partial(end_base, count), [rhs_shape], (rhs, rm, y))
            previous_base = lax.ppermute(base, "cuts", ring)
        for turn in range(0, SWEEPS, 2):
            first, second = exchange(first, second)
            common = (first, second, ff, y, rhs, link, faces)
            if turn < SWEEPS - 2:
                outs = [faces_shape, message, message]
                if near is None:
                    outs += [sds((2, face, face), BF16), sds((2, face, scenarios), F32)]
                    faces, first, second, near, near_link = call(
                        functools.partial(middle_window, count, True), outs, common
                    )
                else:
                    faces, first, second = call(
                        functools.partial(middle_window, count, False), outs, common + (near, near_link)
                    )
            elif step < FINE_STEPS - 1:
                faces, first, second, rhs, y = call(
                    functools.partial(step_window, count),
                    [faces_shape, message, message, rhs_shape, faces_shape],
                    common + (near, near_link, fm, rf, base, wells),
                )
            else:
                vector, means = call(
                    functools.partial(last_window, count),
                    [faces_shape, sds((slices * sub * 2 * count, scenarios), F32)],
                    common + (near, near_link, rf, base, mean),
                )
    previous_vector = lax.ppermute(vector, "cuts", ring)
    means = lax.all_to_all(means, ("cuts", "sub"), 0, 0, tiled=True)
    (previous,) = call(
        functools.partial(previous_end, count), [rhs_shape], (previous_base, previous_vector, ff, rf)
    )
    (result,) = call(
        functools.partial(correct, count),
        [rhs_shape],
        (means, op, previous, start),
        stay_out=(0,),
        scratch=[pltpu.VMEM(rhs_shape.shape, F32), pltpu.SemaphoreType.DMA((count,))],
    )
    return result[None]


def solution(mesh):
    slices = mesh.shape["cuts"]
    in_specs = (
        P("cuts", "sub", None, None),
        P("sub", None, None),
        P("sub", None, None),
        P("sub", None, None),
        P("sub", None, None),
        P(),
        P(),
    )
    return jax.shard_map(
        functools.partial(on_device, slices),
        mesh=mesh,
        in_specs=in_specs,
        out_specs=P("cuts", "sub", None, None),
        check_vma=False,
    )
```

```python
import functools

import jax
import jax.numpy as jnp
from jax import lax
from jax.experimental import pallas as pl
from jax.experimental.pallas import tpu as pltpu
from jax.sharding import PartitionSpec as P


FINE_STEPS = 4
SWEEPS = 4
F32 = jnp.float32
BF16 = jnp.bfloat16
HIGH = lax.Precision.HIGHEST


def dot(a, b, dims=((1,), (0,)), precision=None):
    return lax.dot_general(a, b, (dims, ((), ())), precision=precision, preferred_element_type=F32)


def transpose(x):
    return jnp.transpose(x, (1, 0))


def iota(shape, axis):
    return lax.broadcasted_iota(jnp.int32, shape, axis)


def call(body, out_shape, args, flops=1 << 28, stay=(), stay_out=(), scratch=()):
    size = sum(a.size * a.dtype.itemsize for a in list(args) + list(out_shape))
    vmem = pl.BlockSpec(memory_space=pltpu.VMEM)
    hbm = pl.BlockSpec(memory_space=pltpu.HBM)
    return pl.pallas_call(
        body,
        out_shape=out_shape,
        in_specs=[hbm if k in stay else vmem for k in range(len(args))],
        out_specs=[hbm if k in stay_out else vmem for k in range(len(out_shape))],
        scratch_shapes=list(scratch),
        compiler_params=pltpu.CompilerParams(vmem_limit_bytes=24 << 20),
        cost_estimate=pl.CostEstimate(flops=flops, bytes_accessed=size, transcendentals=0),
    )(*args)


def face_vector(i, count, rhs_ref, link_ref, low, up, below, above):
    face = low[0].shape[0]
    under = below if i == 0 else up[i - 1]
    over = above if i == count - 1 else low[i + 1]
    v_low = rhs_ref[i, :face] + link_ref[2 * i] * under
    v_up = rhs_ref[i, face : 2 * face] + link_ref[2 * i + 1] * over
    return v_low.astype(BF16), v_up.astype(BF16)


def face_sweep(count, ff_ref, y_ref, rhs_ref, link_ref, low, up, below, above):
    face = low[0].shape[0]
    vectors, new_low, new_up = [], [], []
    for i in range(count):
        v = jnp.concatenate(face_vector(i, count, rhs_ref, link_ref, low, up, below, above), axis=0)
        x = y_ref[i] + dot(ff_ref[i], v)
        vectors.append(v)
        new_low.append(x[:face])
        new_up.append(x[face:])
    return vectors, new_low, new_up


def outgoing(count, ff_ref, y_ref, rhs_ref, link_ref, low, up):
    face = low[0].shape[0]
    last = count - 1
    zero = jnp.zeros_like(low[0])
    v = jnp.concatenate(face_vector(last, count, rhs_ref, link_ref, low, up, zero, zero), axis=0)
    next_up = y_ref[last, face:] + dot(ff_ref[last, face:], v)
    v = jnp.concatenate(face_vector(0, count, rhs_ref, link_ref, low, up, zero, zero), axis=0)
    next_low = y_ref[0, :face] + dot(ff_ref[0, :face], v)
    return (up[last], next_up), (low[0], next_low)


def store_messages(upward, downward, first_ref, second_ref):
    even = lax.rem(lax.axis_index("sub"), 2) == 0
    at = 0
    for one, other in zip(upward, downward):
        rows = pl.ds(at, one.shape[0])
        first_ref[rows] = jnp.where(even, one, other)
        second_ref[rows] = jnp.where(even, other, one)
        at += one.shape[0]


def received(first_ref, second_ref, rows):
    even = lax.rem(lax.axis_index("sub"), 2) == 0
    first, second = first_ref[rows], second_ref[rows]
    return jnp.where(even, second, first), jnp.where(even, first, second)


def read_all(sources, targets, sems):
    copies = [pltpu.make_async_copy(a, b, sems.at[k]) for k, (a, b) in enumerate(zip(sources, targets))]
    for copy in copies:
        copy.start()
    return copies


def face_rows(side, face, width):
    return slice(0, face) if side == 0 else slice(width - face, width)


def permutation(i, side, map_ref):
    face = map_ref.shape[2]
    return iota((face, face), 0) == map_ref[i, side : side + 1, :]


def as_bf16(mask):
    return mask.astype(F32).astype(BF16)


def prepare(count, start_hbm, source_hbm, inverse_hbm, map_hbm, trans_hbm,
            rhs_ref, link_ref, faces_ref, first_ref, second_ref,
            start_ref, source_ref, low_ref, up_ref, map_ref, trans_ref, sems):
    width = start_ref.shape[1]
    face = map_ref.shape[2]
    last = count - 1
    copies = read_all(
        (map_hbm, trans_hbm, start_hbm, source_hbm,
         inverse_hbm.at[0, pl.ds(0, face)], inverse_hbm.at[last, pl.ds(width - face, face)]),
        (map_ref, trans_ref, start_ref, source_ref, low_ref, up_ref),
        sems,
    )
    me, size = lax.axis_index("sub"), lax.axis_size("sub")
    copies[0].wait()
    copies[1].wait()
    perms = []
    for i in range(count):
        for side in range(2):
            linked = permutation(i, side, map_ref)
            column = jnp.sum(
                jnp.where(linked, trans_ref[i, side : side + 1, :], 0.0), axis=1, keepdims=True
            )
            if i == 0 and side == 0:
                column = jnp.where(me == 0, 0.0, column)
            if i == last and side == 1:
                column = jnp.where(me == size - 1, 0.0, column)
            link_ref[2 * i + side] = jnp.broadcast_to(column, (face, start_ref.shape[2]))
            perms.append(as_bf16(linked))
    for copy in copies[2:]:
        copy.wait()
    low, up = [], []
    for i in range(count):
        for side in range(2):
            rows = face_rows(side, face, width)
            to = slice(side * face, (side + 1) * face)
            value = start_ref[i, rows]
            high = value.astype(BF16)
            rest = value - high.astype(F32)
            mid = rest.astype(BF16)
            tail = (rest - mid.astype(F32)).astype(BF16)
            perm = perms[2 * i + side]
            parts = dot(perm, jnp.concatenate([high, mid, tail, source_ref[i, rows]], axis=1))
            cut = value.shape[1]
            parts = [parts[:, k * cut : (k + 1) * cut] for k in range(4)]
            rhs_ref[i, to] = parts[0] + parts[1] + parts[2] + parts[3]
            faces_ref[i, to] = value
            (up if side else low).append(value)
    zero = jnp.zeros_like(low[0])
    inner = slice(face, width - face)
    ahead, operators = [], []
    for i, matrix, at in ((last, up_ref, 1), (0, low_ref, 0)):
        columns = [
            dot(matrix[:, face_rows(side, face, width)], perms[2 * i + side], ((1,), (1,))).astype(BF16)
            for side in range(2)
        ]
        middle = (start_ref[i, inner] + source_ref[i, inner].astype(F32)).astype(BF16)
        v = jnp.concatenate(face_vector(i, count, rhs_ref, link_ref, low, up, zero, zero), axis=0)
        ahead.append(dot(matrix[:, inner], middle) + dot(jnp.concatenate(columns, axis=1), v))
        operators.append(columns[at].astype(F32))
    upward = (up[last], ahead[0], operators[0], transpose(link_ref[2 * last + 1])[:8])
    downward = (low[0], ahead[1], operators[1], transpose(link_ref[0])[:8])
    store_messages(upward, downward, first_ref, second_ref)


def prepare_rest(count, start_hbm, source_hbm, inverse_hbm, map_hbm,
                 ff_ref, fm_ref, rf_ref, rm_ref, mid_ref, wells_ref, y_ref, mean_ref,
                 start_ref, source_ref, inverse_ref, map_ref, sems):
    for copy in read_all(
        (start_hbm, source_hbm, inverse_hbm, map_hbm), (start_ref, source_ref, inverse_ref, map_ref), sems
    ):
        copy.wait()
    width = start_ref.shape[1]
    face = map_ref.shape[2]
    inner = slice(face, width - face)
    for i in range(count):
        perms = [as_bf16(permutation(i, side, map_ref)) for side in range(2)]
        for side in range(2):
            to = slice(side * face, (side + 1) * face)
            rows = face_rows(side, face, width)
            columns = dot(inverse_ref[i, :, rows], perms[side], ((1,), (1,))).astype(BF16)
            ff_ref[i, :face, to] = columns[:face]
            ff_ref[i, face:, to] = columns[width - face :]
            rf_ref[i, 2 * face :, to] = columns[inner]
            wells_ref[i, to] = dot(perms[side], source_ref[i, rows])
            fm_ref[i, to] = inverse_ref[i, rows, inner]
        for side in range(2):
            to = slice(side * face, (side + 1) * face)
            rf_ref[i, to] = dot(perms[side], ff_ref[i, to]).astype(BF16)
            rm_ref[i, to] = dot(perms[side], fm_ref[i, to]).astype(BF16)
        rm_ref[i, 2 * face :] = inverse_ref[i, inner, inner]
        wells = source_ref[i, inner].astype(F32)
        mid_ref[i] = start_ref[i, inner] + wells
        wells_ref[i, 2 * face :] = wells
        mean_ref[i : i + 1] = jnp.sum(start_ref[i], axis=0, keepdims=True) / width
        y_ref[i] = dot(fm_ref[i], mid_ref[i].astype(BF16))


def load_faces(count, faces_ref):
    face = faces_ref.shape[1] // 2
    return [faces_ref[i, :face] for i in range(count)], [faces_ref[i, face:] for i in range(count)]


def window(count, first_ref, second_ref, ff_ref, y_ref, rhs_ref, link_ref, faces_ref, near_ref, near_link_ref):
    low, up = load_faces(count, faces_ref)
    face = low[0].shape[0]
    below, above = received(first_ref, second_ref, slice(0, face))
    next_below, next_above = received(first_ref, second_ref, slice(face, 2 * face))
    next_below += dot(near_ref[0], (near_link_ref[0] * low[0]).astype(BF16))
    next_above += dot(near_ref[1], (near_link_ref[1] * up[count - 1]).astype(BF16))
    _, low, up = face_sweep(count, ff_ref, y_ref, rhs_ref, link_ref, low, up, below, above)
    return face_sweep(count, ff_ref, y_ref, rhs_ref, link_ref, low, up, next_below, next_above)


def middle_window(count, opening, *refs):
    if opening:
        (first_ref, second_ref, ff_ref, y_ref, rhs_ref, link_ref, faces_ref, share_ref,
         new_faces, out_first, out_second, near_ref, near_link_ref) = refs
        face = faces_ref.shape[1] // 2
        for k, part in enumerate(received(first_ref, second_ref, slice(2 * face, 3 * face))):
            near_ref[k] = part.astype(BF16)
        for k, part in enumerate(received(first_ref, second_ref, slice(3 * face, 3 * face + 8))):
            near_link_ref[k] = transpose(jnp.broadcast_to(part[:1], (face, face)))
    else:
        (first_ref, second_ref, ff_ref, y_ref, rhs_ref, link_ref, faces_ref, near_ref, near_link_ref,
         new_faces, out_first, out_second) = refs
        face = faces_ref.shape[1] // 2
    _, low, up = window(
        count, first_ref, second_ref, ff_ref, y_ref, rhs_ref, link_ref, faces_ref, near_ref, near_link_ref
    )
    for i in range(count):
        new_faces[i, :face] = low[i]
        new_faces[i, face:] = up[i]
    upward, downward = outgoing(count, ff_ref, y_ref, rhs_ref, link_ref, low, up)
    if opening:
        upward += (share_ref[1],)
        downward += (share_ref[0],)
    store_messages(upward, downward, out_first, out_second)


def step_window(count, opening, first_ref, second_ref, ff_ref, y_ref, rhs_ref, link_ref, faces_ref, near_ref,
                near_link_ref, fm_ref, rf_ref, base_ref, source_ref,
                new_faces, out_first, out_second, new_rhs, new_mid, new_y, *near_share):
    face = faces_ref.shape[1] // 2
    if opening:
        for k, part in enumerate(received(first_ref, second_ref, slice(2 * face, 2 * face + 8))):
            near_share[0][k] = part
    vectors, low, up = window(
        count, first_ref, second_ref, ff_ref, y_ref, rhs_ref, link_ref, faces_ref, near_ref, near_link_ref
    )
    for i in range(count):
        new_faces[i, :face] = low[i]
        new_faces[i, face:] = up[i]
        rhs = base_ref[i] + dot(rf_ref[i], vectors[i]) + source_ref[i]
        new_rhs[i] = rhs[: 2 * face]
        new_mid[i] = rhs[2 * face :]
        new_y[i] = dot(fm_ref[i], rhs[2 * face :].astype(BF16))
    store_messages(*outgoing(count, ff_ref, new_y, new_rhs, link_ref, low, up), out_first, out_second)


def inner_base(count, mid_ref, rm_ref, base_ref):
    for i in range(count):
        base_ref[i] = dot(rm_ref[i], mid_ref[i].astype(BF16))


def shares(count, ff_ref, rf_ref, link_ref, mass_ref, share_ref):
    face = ff_ref.shape[1] // 2
    mass = []
    for i in range(count):
        total = jnp.sum(ff_ref[i].astype(F32), axis=0, keepdims=True)
        total += jnp.sum(rf_ref[i, 2 * face :].astype(F32), axis=0, keepdims=True)
        mass.append(jnp.broadcast_to(total / rf_ref.shape[1], (8, 2 * face)))
        for k in range(2):
            line = mass[i][:1, k * face : (k + 1) * face]
            mass_ref[i, k * face : (k + 1) * face] = transpose(jnp.broadcast_to(line, (face, face)))
    for k, (outer, other) in enumerate(((0, 1), (count - 1, count - 2))):
        here, there = slice(k * face, (k + 1) * face), pl.ds((1 - k) * face, face)
        line = transpose(link_ref[2 * outer + k])[:8]
        inner_line = transpose(link_ref[2 * other + k])[:8]
        one = mass[outer][:, here] * line
        operator = ff_ref[outer, there, here].astype(F32)
        two = dot(mass[other][:, here] * inner_line, operator, precision=HIGH) * line
        share_ref[k] = jnp.where(iota(one.shape, 0) == 0, one, two)


def end_mean(count, mid_ref, rm_ref, y_ref, near_share_ref, out_ref, column_ref):
    face = y_ref.shape[1] // 2
    for k in range(2):
        for j in range(2):
            line = jnp.broadcast_to(near_share_ref[k, j : j + 1], (face, face))
            column_ref[2 * k + j] = transpose(line)
    for i in range(count):
        inner = dot(rm_ref[i, 2 * face :], mid_ref[i].astype(BF16))
        total = jnp.sum(y_ref[i], axis=0, keepdims=True) + jnp.sum(inner, axis=0, keepdims=True)
        out_ref[i : i + 1] = total / rm_ref.shape[1]


def means_payload(count, ff_ref, y_ref, rhs_ref, link_ref, faces_ref, near_ref, near_link_ref,
                  column_ref, mass_ref, base_mean_ref, mean_ref, op_ref, parts_ref):
    low, up = load_faces(count, faces_ref)
    zero = jnp.zeros_like(low[0])
    last = count - 1
    next_below = dot(near_ref[0], (near_link_ref[0] * low[0]).astype(BF16))
    next_above = dot(near_ref[1], (near_link_ref[1] * up[last]).astype(BF16))
    _, next_low, next_up = face_sweep(count, ff_ref, y_ref, rhs_ref, link_ref, low, up, zero, zero)
    rows = []
    for i in range(count):
        v = jnp.concatenate(
            face_vector(i, count, rhs_ref, link_ref, next_low, next_up, next_below, next_above), axis=0
        )
        rows.append(base_mean_ref[i : i + 1] + weighted(mass_ref[i], v.astype(F32)))
    rows += [mean_ref[i : i + 1] for i in range(count)]
    for k, (two, one) in ((1, (up[last], next_up[last])), (0, (low[0], next_low[0]))):
        rows.append(weighted(column_ref[2 * k], one))
        rows.append(weighted(column_ref[2 * k + 1], two))
    rows += [zero[:1]] * (payload_rows(count) - len(rows))
    parts_ref[...] = dot(op_ref[...], jnp.concatenate(rows, axis=0), precision=HIGH)


def weighted(column, x):
    return jnp.sum(column * x, axis=0, keepdims=True)


def payload_rows(count):
    return -(-(2 * count + 4) // 8) * 8


def taken_base(count, mid_ref, fm_ref, rm_ref, y_ref, inner_ref):
    face = y_ref.shape[1] // 2
    for i in range(count):
        v = mid_ref[i].astype(BF16)
        y_ref[i] = dot(fm_ref[i], v)
        inner_ref[i] = dot(rm_ref[i, 2 * face :], v)


def last_window(count, first_ref, second_ref, ff_ref, y_ref, rhs_ref, link_ref, faces_ref, near_ref,
                near_link_ref, rf_ref, inner_ref, end_ref):
    face = faces_ref.shape[1] // 2
    width = end_ref.shape[1]
    vectors, low, up = window(
        count, first_ref, second_ref, ff_ref, y_ref, rhs_ref, link_ref, faces_ref, near_ref, near_link_ref
    )
    for i in range(count):
        end_ref[i, :face] = low[i]
        end_ref[i, face : width - face] = inner_ref[i] + dot(rf_ref[i, 2 * face :], vectors[i])
        end_ref[i, width - face :] = up[i]


def coarse_operator(count, slices, partner_hbm, cond_hbm, out_ref, partner_ref, cond_ref, sems):
    copies = [
        pltpu.make_async_copy(partner_hbm, partner_ref, sems.at[0]),
        pltpu.make_async_copy(cond_hbm, cond_ref, sems.at[1]),
    ]
    for copy in copies:
        copy.start()
    for copy in copies:
        copy.wait()
    n = partner_ref.shape[0]
    row, col = iota((n, n), 0), iota((n, n), 1)
    weights = (jnp.abs(row - col) == 1).astype(F32)
    for b in range(n):
        to, cond = partner_ref[b], cond_ref[b]
        weights += jnp.where((row == b) & (col == to), cond, 0.0)
        weights += jnp.where((col == b) & (row == to), cond, 0.0)
    eye = (row == col).astype(F32)
    m = eye + eye * jnp.sum(weights, axis=1, keepdims=True) - weights
    for i in range(n):
        pivot = 1.0 / m[i : i + 1, i : i + 1]
        line = m[i : i + 1, :] * pivot
        column = m[:, i : i + 1]
        inner = jnp.where(col == i, -column * pivot, m - column * line)
        m = jnp.where(row == i, jnp.where(col == i, pivot, line), inner)
    here, me = lax.axis_index("cuts"), lax.axis_index("sub")
    shape = (n, out_ref.shape[1])
    block, item = iota(shape, 0) - me * count, iota(shape, 1)
    own = (item < count) & (block == item)
    above = (item >= 2 * count) & (item < 2 * count + 2) & (block == item - count)
    below = (item >= 2 * count + 2) & (item < 2 * count + 4) & (block == 2 * count + 1 - item)
    end = (own | above | below).astype(F32)
    start = ((item >= count) & (item < 2 * count) & (block == item - count)).astype(F32)
    ends, starts = [], []
    for _ in range(1, slices - 1):
        end, start = dot(m, end, precision=HIGH), dot(m, start, precision=HIGH)
        ends.append(end)
        starts.append(start)
    for s in range(slices):
        total = jnp.zeros(shape, F32)
        for k in range(1, slices - 1):
            if s - 1 - k >= 0:
                total += jnp.where(here == s - 1 - k, ends[k - 1], 0.0)
            if s - k >= 1:
                total -= jnp.where(here == s - k, starts[k - 1], 0.0)
        out_ref[s * n : (s + 1) * n] = total


def correct(count, parts_ref, previous_ref, start_ref, out_hbm, out_ref, sems):
    later = lax.axis_index("cuts") > 0
    mine = jnp.sum(parts_ref[...], axis=0)
    copies = []
    for i in range(count):
        out_ref[i] = jnp.where(later, previous_ref[i] + mine[i : i + 1], start_ref[i])
        copies.append(pltpu.make_async_copy(out_ref.at[i], out_hbm.at[i], sems.at[i]))
        copies[i].start()
    for copy in copies:
        copy.wait()


def exchange(first, second, ahead=0):
    size, slices = lax.axis_size("sub"), lax.axis_size("cuts")
    pairs, other = [], []
    for c in range(slices):
        d = (c + ahead) % slices
        for i in range(size):
            pairs.append((c * size + i, d * size + (i ^ 1)))
            j = i + (1 if i % 2 else -1)
            if 0 <= j < size:
                other.append((c * size + i, d * size + j))
            elif ahead:
                other.append((c * size + i, d * size + i))
            else:
                other.append((c * size + i, (c ^ 1 if c ^ 1 < slices else c) * size + i))
    far = lax.ppermute(second, ("cuts", "sub"), other)
    near = lax.ppermute(first, ("cuts", "sub"), pairs)
    return near, far


def on_device(slices, start_states, source, block_inverse, face_map, transmissibility, partner, fracture_cond):
    start = start_states[0]
    count, width, scenarios = start.shape
    face = face_map.shape[-1]
    inner = width - 2 * face
    sub = lax.axis_size("sub")
    sds = jax.ShapeDtypeStruct
    message = sds((2 * face, scenarios), F32)
    opening = sds((3 * face + 8, scenarios), F32)
    sharing = sds((2 * face + 8, scenarios), F32)
    share_shape = sds((2, 8, face), F32)
    per = payload_rows(count)
    faces_shape = sds((count, 2 * face, scenarios), F32)
    rhs_shape = sds((count, width, scenarios), F32)
    held = [
        pltpu.with_memory_space_constraint(a, pltpu.HBM)
        for a in (start, source, block_inverse, face_map, transmissibility)
    ]
    buffers = [pltpu.VMEM(a.shape, a.dtype) for a in (start, source)]
    row = pltpu.VMEM((face, width), BF16)
    tables = [pltpu.VMEM(a.shape, a.dtype) for a in (face_map, transmissibility)]
    mid_shape = sds((count, inner, scenarios), F32)
    rhs, link, faces, first, second = call(
        functools.partial(prepare, count),
        [faces_shape, sds((2 * count, face, scenarios), F32), faces_shape, opening, opening],
        held,
        stay=range(5),
        scratch=buffers + [row, row] + tables + [pltpu.SemaphoreType.DMA((6,))],
    )
    ff, fm, rf, rm, mid, wells, y, mean = call(
        functools.partial(prepare_rest, count),
        [
            sds((count, 2 * face, 2 * face), BF16),
            sds((count, 2 * face, inner), BF16),
            sds((count, width, 2 * face), BF16),
            sds((count, width, inner), BF16),
            mid_shape,
            rhs_shape,
            faces_shape,
            sds((count, scenarios), F32),
        ],
        held[:4],
        stay=range(4),
        scratch=buffers
        + [pltpu.VMEM(block_inverse.shape, BF16), tables[0], pltpu.SemaphoreType.DMA((4,))],
    )
    blocks = partner.shape[0]
    (op,) = call(
        functools.partial(coarse_operator, count, slices),
        [sds((slices * blocks, per), F32)],
        [pltpu.with_memory_space_constraint(v, pltpu.HBM) for v in (partner, fracture_cond)],
        stay=range(2),
        scratch=[
            pltpu.SMEM((blocks,), jnp.int32),
            pltpu.SMEM((blocks,), F32),
            pltpu.SemaphoreType.DMA((2,)),
        ],
    )
    mass, share = call(
        functools.partial(shares, count),
        [faces_shape, share_shape],
        (ff, rf, link),
    )
    near = near_link = None
    ring = [(i, (i + 1) % slices) for i in range(slices)]
    for step in range(FINE_STEPS):
        final = step == FINE_STEPS - 1
        if final:
            taken_mid = lax.ppermute(mid, "cuts", ring)
            taken_rhs = lax.ppermute(rhs, "cuts", ring)
            base_mean, near_column = call(
                functools.partial(end_mean, count),
                [sds((count, scenarios), F32), sds((4, face, scenarios), F32)],
                (mid, rm, y, near_share),
            )
        else:
            (base,) = call(functools.partial(inner_base, count), [rhs_shape], (mid, rm))
        for turn in range(0, SWEEPS, 2):
            ending = final and turn == SWEEPS - 2
            first, second = exchange(first, second, 1 if ending else 0)
            common = (first, second, ff, y, rhs, link, faces)
            if turn < SWEEPS - 2:
                if near is None:
                    faces, first, second, near, near_link = call(
                        functools.partial(middle_window, count, True),
                        [faces_shape, sharing, sharing, sds((2, face, face), BF16), sds((2, face, scenarios), F32)],
                        common + (share,),
                    )
                else:
                    faces, first, second = call(
                        functools.partial(middle_window, count, False),
                        [faces_shape, message, message],
                        common + (near, near_link),
                    )
            elif not ending:
                outs = [faces_shape, message, message, faces_shape, mid_shape, faces_shape]
                outs = call(
                    functools.partial(step_window, count, step == 0),
                    outs + [share_shape] if step == 0 else outs,
                    common + (near, near_link, fm, rf, base, wells),
                )
                faces, first, second, rhs, mid, y = outs[:6]
                if step == 0:
                    near_share = outs[6]
    taken_faces = lax.ppermute(faces, "cuts", ring)
    taken_y, taken_inner = call(
        functools.partial(taken_base, count),
        [faces_shape, mid_shape],
        (taken_mid, fm, rm),
    )
    taken_y, parts_rhs = lax.optimization_barrier((taken_y, rhs))
    (parts,) = call(
        functools.partial(means_payload, count),
        [sds((slices * blocks, scenarios), F32)],
        (ff, y, parts_rhs, link, faces, near, near_link, near_column, mass, base_mean, mean, op),
    )
    parts = parts.reshape(slices * sub, count, scenarios)
    parts = lax.all_to_all(parts, ("cuts", "sub"), 0, 0, tiled=True)
    (previous,) = call(
        functools.partial(last_window, count),
        [rhs_shape],
        (first, second, ff, taken_y, taken_rhs, link, taken_faces, near, near_link, rf, taken_inner),
    )
    (result,) = call(
        functools.partial(correct, count),
        [rhs_shape],
        (parts, previous, start),
        stay_out=(0,),
        scratch=[pltpu.VMEM(rhs_shape.shape, F32), pltpu.SemaphoreType.DMA((count,))],
    )
    return result[None]


def solution(mesh):
    slices = mesh.shape["cuts"]

    def body(*args):
        return on_device(slices, *args)

    in_specs = (
        P("cuts", "sub", None, None),
        P("sub", None, None),
        P("sub", None, None),
        P("sub", None, None),
        P("sub", None, None),
        P(),
        P(),
    )
    return jax.shard_map(
        body,
        mesh=mesh,
        in_specs=in_specs,
        out_specs=P("cuts", "sub", None, None),
        check_vma=False,
    )
```

```python
import functools

import jax
import jax.numpy as jnp
from jax import lax
from jax.experimental import pallas as pl
from jax.experimental.pallas import tpu as pltpu
from jax.sharding import PartitionSpec as P


FINE_STEPS = 4
SWEEPS = 4
F32 = jnp.float32
BF16 = jnp.bfloat16
HIGH = lax.Precision.HIGHEST


def dot(a, b, dims=((1,), (0,)), precision=None):
    return lax.dot_general(a, b, (dims, ((), ())), precision=precision, preferred_element_type=F32)


def transpose(x):
    return jnp.transpose(x, (1, 0))


def iota(shape, axis):
    return lax.broadcasted_iota(jnp.int32, shape, axis)


def call(body, out_shape, args, flops=1 << 28, stay=(), stay_out=(), scratch=(), aliases=None):
    size = sum(a.size * a.dtype.itemsize for a in list(args) + list(out_shape))
    vmem = pl.BlockSpec(memory_space=pltpu.VMEM)
    hbm = pl.BlockSpec(memory_space=pltpu.HBM)
    return pl.pallas_call(
        body,
        out_shape=out_shape,
        in_specs=[hbm if k in stay else vmem for k in range(len(args))],
        out_specs=[hbm if k in stay_out else vmem for k in range(len(out_shape))],
        scratch_shapes=list(scratch),
        input_output_aliases=aliases or {},
        compiler_params=pltpu.CompilerParams(vmem_limit_bytes=24 << 20),
        cost_estimate=pl.CostEstimate(flops=flops, bytes_accessed=size, transcendentals=0),
    )(*args)


def face_vector(i, count, rhs_ref, link_ref, low, up, below, above):
    face = low[0].shape[0]
    under = below if i == 0 else up[i - 1]
    over = above if i == count - 1 else low[i + 1]
    v_low = rhs_ref[i, :face] + link_ref[2 * i] * under
    v_up = rhs_ref[i, face : 2 * face] + link_ref[2 * i + 1] * over
    return v_low.astype(BF16), v_up.astype(BF16)


def face_sweep(count, ff_ref, y_ref, rhs_ref, link_ref, low, up, below, above):
    face = low[0].shape[0]
    vectors, new_low, new_up = [], [], []
    for i in range(count):
        v = jnp.concatenate(face_vector(i, count, rhs_ref, link_ref, low, up, below, above), axis=0)
        x = y_ref[i] + dot(ff_ref[i], v)
        vectors.append(v)
        new_low.append(x[:face])
        new_up.append(x[face:])
    return vectors, new_low, new_up


def outgoing(count, ff_ref, y_ref, rhs_ref, link_ref, low, up):
    face = low[0].shape[0]
    last = count - 1
    zero = jnp.zeros_like(low[0])
    v = jnp.concatenate(face_vector(last, count, rhs_ref, link_ref, low, up, zero, zero), axis=0)
    next_up = y_ref[last, face:] + dot(ff_ref[last, face:], v)
    v = jnp.concatenate(face_vector(0, count, rhs_ref, link_ref, low, up, zero, zero), axis=0)
    next_low = y_ref[0, :face] + dot(ff_ref[0, :face], v)
    return (up[last], next_up), (low[0], next_low)


def store_messages(upward, downward, first_ref, second_ref):
    even = lax.rem(lax.axis_index("sub"), 2) == 0
    at = 0
    for one, other in zip(upward, downward):
        rows = pl.ds(at, one.shape[0])
        first_ref[rows] = jnp.where(even, one, other)
        second_ref[rows] = jnp.where(even, other, one)
        at += one.shape[0]


def received(first_ref, second_ref, rows):
    even = lax.rem(lax.axis_index("sub"), 2) == 0
    first, second = first_ref[rows], second_ref[rows]
    return jnp.where(even, second, first), jnp.where(even, first, second)


def read_all(sources, targets, sems):
    copies = [pltpu.make_async_copy(a, b, sems.at[k]) for k, (a, b) in enumerate(zip(sources, targets))]
    for copy in copies:
        copy.start()
    return copies


def face_rows(side, face, width):
    return slice(0, face) if side == 0 else slice(width - face, width)


def permutation(i, side, map_ref):
    face = map_ref.shape[2]
    return iota((face, face), 0) == map_ref[i, side : side + 1, :]


def as_bf16(mask):
    return mask.astype(F32).astype(BF16)


def prepare(count, start_hbm, source_hbm, inverse_hbm, map_hbm, trans_hbm,
            rhs_ref, link_ref, faces_ref, first_ref, second_ref,
            start_ref, source_ref, low_ref, up_ref, map_ref, trans_ref, sems):
    width = start_ref.shape[1]
    face = map_ref.shape[2]
    last = count - 1
    copies = read_all(
        (map_hbm, trans_hbm, start_hbm, source_hbm,
         inverse_hbm.at[0, pl.ds(0, face)], inverse_hbm.at[last, pl.ds(width - face, face)]),
        (map_ref, trans_ref, start_ref, source_ref, low_ref, up_ref),
        sems,
    )
    me, size = lax.axis_index("sub"), lax.axis_size("sub")
    copies[0].wait()
    copies[1].wait()
    perms = []
    for i in range(count):
        for side in range(2):
            linked = permutation(i, side, map_ref)
            column = jnp.sum(
                jnp.where(linked, trans_ref[i, side : side + 1, :], 0.0), axis=1, keepdims=True
            )
            if i == 0 and side == 0:
                column = jnp.where(me == 0, 0.0, column)
            if i == last and side == 1:
                column = jnp.where(me == size - 1, 0.0, column)
            link_ref[2 * i + side] = jnp.broadcast_to(column, (face, start_ref.shape[2]))
            perms.append(as_bf16(linked))
    for copy in copies[2:]:
        copy.wait()
    low, up = [], []
    for i in range(count):
        for side in range(2):
            rows = face_rows(side, face, width)
            to = slice(side * face, (side + 1) * face)
            value = start_ref[i, rows]
            high = value.astype(BF16)
            rest = value - high.astype(F32)
            mid = rest.astype(BF16)
            tail = (rest - mid.astype(F32)).astype(BF16)
            perm = perms[2 * i + side]
            parts = dot(perm, jnp.concatenate([high, mid, tail, source_ref[i, rows]], axis=1))
            cut = value.shape[1]
            parts = [parts[:, k * cut : (k + 1) * cut] for k in range(4)]
            rhs_ref[i, to] = parts[0] + parts[1] + parts[2] + parts[3]
            faces_ref[i, to] = value
            (up if side else low).append(value)
    zero = jnp.zeros_like(low[0])
    inner = slice(face, width - face)
    ahead, operators = [], []
    for i, matrix, at in ((last, up_ref, 1), (0, low_ref, 0)):
        columns = [
            dot(matrix[:, face_rows(side, face, width)], perms[2 * i + side], ((1,), (1,))).astype(BF16)
            for side in range(2)
        ]
        middle = (start_ref[i, inner] + source_ref[i, inner].astype(F32)).astype(BF16)
        v = jnp.concatenate(face_vector(i, count, rhs_ref, link_ref, low, up, zero, zero), axis=0)
        ahead.append(dot(matrix[:, inner], middle) + dot(jnp.concatenate(columns, axis=1), v))
        operators.append(columns[at].astype(F32))
    upward = (up[last], ahead[0], operators[0], transpose(link_ref[2 * last + 1])[:8])
    downward = (low[0], ahead[1], operators[1], transpose(link_ref[0])[:8])
    store_messages(upward, downward, first_ref, second_ref)


def prepare_rest(count, start_hbm, source_hbm, inverse_hbm, map_hbm,
                 ff_ref, fm_ref, pf_ref, rf_ref, pm_ref, rm_ref, mid_ref, wells_ref, y_ref, mean_ref,
                 start_ref, source_ref, inverse_ref, map_ref, sems):
    for copy in read_all(
        (start_hbm, source_hbm, inverse_hbm, map_hbm), (start_ref, source_ref, inverse_ref, map_ref), sems
    ):
        copy.wait()
    width = start_ref.shape[1]
    face = map_ref.shape[2]
    inner = slice(face, width - face)
    for i in range(count):
        perms = [as_bf16(permutation(i, side, map_ref)) for side in range(2)]
        for side in range(2):
            to = slice(side * face, (side + 1) * face)
            rows = face_rows(side, face, width)
            columns = dot(inverse_ref[i, :, rows], perms[side], ((1,), (1,))).astype(BF16)
            ff_ref[i, :face, to] = columns[:face]
            ff_ref[i, face:, to] = columns[width - face :]
            rf_ref[i, :, to] = columns[inner]
            wells_ref[i, to] = dot(perms[side], source_ref[i, rows])
            fm_ref[i, to] = inverse_ref[i, rows, inner]
        for side in range(2):
            to = slice(side * face, (side + 1) * face)
            pf_ref[i, to] = dot(perms[side], ff_ref[i, to]).astype(BF16)
            pm_ref[i, to] = dot(perms[side], fm_ref[i, to]).astype(BF16)
        rm_ref[i] = inverse_ref[i, inner, inner]
        wells = source_ref[i, inner].astype(F32)
        mid_ref[i] = start_ref[i, inner] + wells
        wells_ref[i, 2 * face :] = wells
        mean_ref[i : i + 1] = jnp.sum(start_ref[i], axis=0, keepdims=True) / width
        y_ref[i] = dot(fm_ref[i], mid_ref[i].astype(BF16))


def load_faces(count, faces_ref):
    face = faces_ref.shape[1] // 2
    return [faces_ref[i, :face] for i in range(count)], [faces_ref[i, face:] for i in range(count)]


def window(count, first_ref, second_ref, ff_ref, y_ref, rhs_ref, link_ref, faces_ref, near_ref, near_link_ref):
    low, up = load_faces(count, faces_ref)
    face = low[0].shape[0]
    below, above = received(first_ref, second_ref, slice(0, face))
    next_below, next_above = received(first_ref, second_ref, slice(face, 2 * face))
    next_below += dot(near_ref[0], (near_link_ref[0] * low[0]).astype(BF16))
    next_above += dot(near_ref[1], (near_link_ref[1] * up[count - 1]).astype(BF16))
    _, low, up = face_sweep(count, ff_ref, y_ref, rhs_ref, link_ref, low, up, below, above)
    return face_sweep(count, ff_ref, y_ref, rhs_ref, link_ref, low, up, next_below, next_above)


def middle_window(count, opening, *refs):
    if opening:
        (first_ref, second_ref, ff_ref, y_ref, rhs_ref, link_ref, faces_ref, share_ref,
         new_faces, out_first, out_second, near_ref, near_link_ref) = refs
        face = faces_ref.shape[1] // 2
        for k, part in enumerate(received(first_ref, second_ref, slice(2 * face, 3 * face))):
            near_ref[k] = part.astype(BF16)
        for k, part in enumerate(received(first_ref, second_ref, slice(3 * face, 3 * face + 8))):
            near_link_ref[k] = transpose(jnp.broadcast_to(part[:1], (face, face)))
    else:
        (first_ref, second_ref, ff_ref, y_ref, rhs_ref, link_ref, faces_ref, near_ref, near_link_ref,
         new_faces, out_first, out_second) = refs
        face = faces_ref.shape[1] // 2
    _, low, up = window(
        count, first_ref, second_ref, ff_ref, y_ref, rhs_ref, link_ref, faces_ref, near_ref, near_link_ref
    )
    for i in range(count):
        new_faces[i, :face] = low[i]
        new_faces[i, face:] = up[i]
    upward, downward = outgoing(count, ff_ref, y_ref, rhs_ref, link_ref, low, up)
    if opening:
        upward += (share_ref[1],)
        downward += (share_ref[0],)
    store_messages(upward, downward, out_first, out_second)


def step_window(count, opening, first_ref, second_ref, ff_ref, y_ref, rhs_ref, link_ref, faces_ref, near_ref,
                near_link_ref, fm_ref, pf_ref, rf_ref, base_ref, source_ref,
                new_faces, out_first, out_second, new_rhs, new_mid, new_y, *near_share):
    face = faces_ref.shape[1] // 2
    if opening:
        for k, part in enumerate(received(first_ref, second_ref, slice(2 * face, 2 * face + 8))):
            near_share[0][k] = part
    vectors, low, up = window(
        count, first_ref, second_ref, ff_ref, y_ref, rhs_ref, link_ref, faces_ref, near_ref, near_link_ref
    )
    for i in range(count):
        new_faces[i, :face] = low[i]
        new_faces[i, face:] = up[i]
        cut = 2 * face
        new_rhs[i] = base_ref[i, :cut] + dot(pf_ref[i], vectors[i]) + source_ref[i, :cut]
        rhs = base_ref[i, cut:] + dot(rf_ref[i], vectors[i]) + source_ref[i, cut:]
        new_mid[i] = rhs
        new_y[i] = dot(fm_ref[i], rhs.astype(BF16))
    store_messages(*outgoing(count, ff_ref, new_y, new_rhs, link_ref, low, up), out_first, out_second)


def inner_base(count, mid_ref, pm_ref, rm_ref, base_ref):
    for i in range(count):
        cut = pm_ref.shape[1]
        v = mid_ref[i].astype(BF16)
        base_ref[i, :cut] = dot(pm_ref[i], v)
        base_ref[i, cut:] = dot(rm_ref[i], v)


def shares(count, ff_ref, rf_ref, link_ref, mass_ref, share_ref):
    face = ff_ref.shape[1] // 2
    mass = []
    for i in range(count):
        total = jnp.sum(ff_ref[i].astype(F32), axis=0, keepdims=True)
        total += jnp.sum(rf_ref[i].astype(F32), axis=0, keepdims=True)
        width = 2 * face + rf_ref.shape[1]
        mass.append(jnp.broadcast_to(total / width, (8, 2 * face)))
        for k in range(2):
            line = mass[i][:1, k * face : (k + 1) * face]
            mass_ref[i, k * face : (k + 1) * face] = transpose(jnp.broadcast_to(line, (face, face)))
    for k, (outer, other) in enumerate(((0, 1), (count - 1, count - 2))):
        here, there = slice(k * face, (k + 1) * face), pl.ds((1 - k) * face, face)
        line = transpose(link_ref[2 * outer + k])[:8]
        inner_line = transpose(link_ref[2 * other + k])[:8]
        one = mass[outer][:, here] * line
        operator = ff_ref[outer, there, here].astype(F32)
        two = dot(mass[other][:, here] * inner_line, operator, precision=HIGH) * line
        share_ref[k] = jnp.where(iota(one.shape, 0) == 0, one, two)


def end_mean(count, mid_ref, rm_ref, y_ref, near_share_ref, out_ref, column_ref):
    face = y_ref.shape[1] // 2
    for k in range(2):
        for j in range(2):
            line = jnp.broadcast_to(near_share_ref[k, j : j + 1], (face, face))
            column_ref[2 * k + j] = transpose(line)
    for i in range(count):
        inner = dot(rm_ref[i], mid_ref[i].astype(BF16))
        total = jnp.sum(y_ref[i], axis=0, keepdims=True) + jnp.sum(inner, axis=0, keepdims=True)
        out_ref[i : i + 1] = total / (2 * face + rm_ref.shape[1])


def means_payload(count, ff_ref, y_ref, rhs_ref, link_ref, faces_ref, near_ref, near_link_ref,
                  column_ref, mass_ref, base_mean_ref, mean_ref, op_ref, parts_ref):
    low, up = load_faces(count, faces_ref)
    zero = jnp.zeros_like(low[0])
    last = count - 1
    next_below = dot(near_ref[0], (near_link_ref[0] * low[0]).astype(BF16))
    next_above = dot(near_ref[1], (near_link_ref[1] * up[last]).astype(BF16))
    _, next_low, next_up = face_sweep(count, ff_ref, y_ref, rhs_ref, link_ref, low, up, zero, zero)
    rows = []
    for i in range(count):
        v = jnp.concatenate(
            face_vector(i, count, rhs_ref, link_ref, next_low, next_up, next_below, next_above), axis=0
        )
        rows.append(base_mean_ref[i : i + 1] + weighted(mass_ref[i], v.astype(F32)))
    rows += [mean_ref[i : i + 1] for i in range(count)]
    for k, (two, one) in ((1, (up[last], next_up[last])), (0, (low[0], next_low[0]))):
        rows.append(weighted(column_ref[2 * k], one))
        rows.append(weighted(column_ref[2 * k + 1], two))
    rows += [zero[:1]] * (payload_rows(count) - len(rows))
    parts_ref[...] = dot(op_ref[...], jnp.concatenate(rows, axis=0), precision=HIGH)


def weighted(column, x):
    return jnp.sum(column * x, axis=0, keepdims=True)


def payload_rows(count):
    return -(-(2 * count + 4) // 8) * 8


def last_window(count, first_ref, second_ref, ff_ref, rhs_hbm, link_ref, faces_hbm, near_ref,
                near_link_ref, rf_ref, mid_hbm, fm_ref, rm_ref, start_hbm, end_ref, out_hbm,
                y_ref, rhs_ref, faces_ref, mid_ref, start_ref, sems, out_sems):
    copies = read_all((mid_hbm, rhs_hbm, faces_hbm, start_hbm), (mid_ref, rhs_ref, faces_ref, start_ref), sems)
    copies[0].wait()
    face = faces_ref.shape[1] // 2
    width = end_ref.shape[1]
    for i in range(count):
        v = mid_ref[i].astype(BF16)
        y_ref[i] = dot(fm_ref[i], v)
        end_ref[i, face : width - face] = dot(rm_ref[i], v)
    for copy in copies[1:]:
        copy.wait()
    vectors, low, up = window(
        count, first_ref, second_ref, ff_ref, y_ref, rhs_ref, link_ref, faces_ref, near_ref, near_link_ref
    )
    later = lax.axis_index("cuts") > 0
    copies = []
    for i in range(count):
        end_ref[i, :face] = low[i]
        end_ref[i, face : width - face] += dot(rf_ref[i], vectors[i])
        end_ref[i, width - face :] = up[i]
        start_ref[i] = jnp.where(later, end_ref[i], start_ref[i])
        copies.append(pltpu.make_async_copy(start_ref.at[i], out_hbm.at[i], out_sems.at[i]))
        copies[i].start()
    for copy in copies:
        copy.wait()


def coarse_operator(count, slices, partner_hbm, cond_hbm, out_ref, partner_ref, cond_ref, sems):
    copies = [
        pltpu.make_async_copy(partner_hbm, partner_ref, sems.at[0]),
        pltpu.make_async_copy(cond_hbm, cond_ref, sems.at[1]),
    ]
    for copy in copies:
        copy.start()
    for copy in copies:
        copy.wait()
    n = partner_ref.shape[0]
    row, col = iota((n, n), 0), iota((n, n), 1)
    weights = (jnp.abs(row - col) == 1).astype(F32)
    for b in range(n):
        to, cond = partner_ref[b], cond_ref[b]
        weights += jnp.where((row == b) & (col == to), cond, 0.0)
        weights += jnp.where((col == b) & (row == to), cond, 0.0)
    eye = (row == col).astype(F32)
    m = eye + eye * jnp.sum(weights, axis=1, keepdims=True) - weights
    for i in range(n):
        pivot = 1.0 / m[i : i + 1, i : i + 1]
        line = m[i : i + 1, :] * pivot
        column = m[:, i : i + 1]
        inner = jnp.where(col == i, -column * pivot, m - column * line)
        m = jnp.where(row == i, jnp.where(col == i, pivot, line), inner)
    here, me = lax.axis_index("cuts"), lax.axis_index("sub")
    shape = (n, out_ref.shape[1])
    block, item = iota(shape, 0) - me * count, iota(shape, 1)
    own = (item < count) & (block == item)
    above = (item >= 2 * count) & (item < 2 * count + 2) & (block == item - count)
    below = (item >= 2 * count + 2) & (item < 2 * count + 4) & (block == 2 * count + 1 - item)
    end = (own | above | below).astype(F32)
    start = ((item >= count) & (item < 2 * count) & (block == item - count)).astype(F32)
    ends, starts = [], []
    for _ in range(1, slices - 1):
        end, start = dot(m, end, precision=HIGH), dot(m, start, precision=HIGH)
        ends.append(end)
        starts.append(start)
    for s in range(slices):
        total = jnp.zeros(shape, F32)
        for k in range(1, slices - 1):
            if s - 1 - k >= 0:
                total += jnp.where(here == s - 1 - k, ends[k - 1], 0.0)
            if s - k >= 1:
                total -= jnp.where(here == s - k, starts[k - 1], 0.0)
        out_ref[s * n : (s + 1) * n] = total


def correct(count, pieces, parts_ref, previous_ref, early_hbm, out_hbm, out_ref, sems):
    @pl.when(lax.axis_index("cuts") > 1)
    def _():
        mine = jnp.sum(parts_ref[...], axis=0)
        size = out_ref.shape[1] // pieces
        copies = []
        for i in range(count):
            for k in range(pieces):
                rows = pl.ds(k * size, size)
                out_ref[i, rows] = previous_ref[i, rows] + mine[i : i + 1]
                copies.append(
                    pltpu.make_async_copy(out_ref.at[i, rows], out_hbm.at[i, rows], sems.at[i * pieces + k])
                )
                copies[-1].start()
        for copy in copies:
            copy.wait()


def exchange(first, second, ahead=0):
    size, slices = lax.axis_size("sub"), lax.axis_size("cuts")
    pairs, other = [], []
    for c in range(slices):
        d = (c + ahead) % slices
        for i in range(size):
            pairs.append((c * size + i, d * size + (i ^ 1)))
            j = i + (1 if i % 2 else -1)
            if 0 <= j < size:
                other.append((c * size + i, d * size + j))
            elif ahead:
                other.append((c * size + i, d * size + i))
            else:
                other.append((c * size + i, (c ^ 1 if c ^ 1 < slices else c) * size + i))
    far = lax.ppermute(second, ("cuts", "sub"), other)
    near = lax.ppermute(first, ("cuts", "sub"), pairs)
    return near, far


def on_device(slices, start_states, source, block_inverse, face_map, transmissibility, partner, fracture_cond):
    start = start_states[0]
    count, width, scenarios = start.shape
    face = face_map.shape[-1]
    inner = width - 2 * face
    sub = lax.axis_size("sub")
    sds = jax.ShapeDtypeStruct
    message = sds((2 * face, scenarios), F32)
    opening = sds((3 * face + 8, scenarios), F32)
    sharing = sds((2 * face + 8, scenarios), F32)
    share_shape = sds((2, 8, face), F32)
    per = payload_rows(count)
    faces_shape = sds((count, 2 * face, scenarios), F32)
    rhs_shape = sds((count, width, scenarios), F32)
    held = [
        pltpu.with_memory_space_constraint(a, pltpu.HBM)
        for a in (start, source, block_inverse, face_map, transmissibility)
    ]
    buffers = [pltpu.VMEM(a.shape, a.dtype) for a in (start, source)]
    row = pltpu.VMEM((face, width), BF16)
    tables = [pltpu.VMEM(a.shape, a.dtype) for a in (face_map, transmissibility)]
    mid_shape = sds((count, inner, scenarios), F32)
    rhs, link, faces, first, second = call(
        functools.partial(prepare, count),
        [faces_shape, sds((2 * count, face, scenarios), F32), faces_shape, opening, opening],
        held,
        stay=range(5),
        scratch=buffers + [row, row] + tables + [pltpu.SemaphoreType.DMA((6,))],
    )
    ff, fm, pf, rf, pm, rm, mid, wells, y, mean = call(
        functools.partial(prepare_rest, count),
        [
            sds((count, 2 * face, 2 * face), BF16),
            sds((count, 2 * face, inner), BF16),
            sds((count, 2 * face, 2 * face), BF16),
            sds((count, inner, 2 * face), BF16),
            sds((count, 2 * face, inner), BF16),
            sds((count, inner, inner), BF16),
            mid_shape,
            rhs_shape,
            faces_shape,
            sds((count, scenarios), F32),
        ],
        held[:4],
        stay=range(4),
        scratch=buffers
        + [pltpu.VMEM(block_inverse.shape, BF16), tables[0], pltpu.SemaphoreType.DMA((4,))],
    )
    blocks = partner.shape[0]
    (op,) = call(
        functools.partial(coarse_operator, count, slices),
        [sds((slices * blocks, per), F32)],
        [pltpu.with_memory_space_constraint(v, pltpu.HBM) for v in (partner, fracture_cond)],
        stay=range(2),
        scratch=[
            pltpu.SMEM((blocks,), jnp.int32),
            pltpu.SMEM((blocks,), F32),
            pltpu.SemaphoreType.DMA((2,)),
        ],
    )
    mass, share = call(
        functools.partial(shares, count),
        [faces_shape, share_shape],
        (ff, rf, link),
    )
    near = near_link = None
    ring = [(i, (i + 1) % slices) for i in range(slices)]
    for step in range(FINE_STEPS):
        final = step == FINE_STEPS - 1
        if final:
            taken_mid = lax.ppermute(mid, "cuts", ring)
            taken_rhs = lax.ppermute(rhs, "cuts", ring)
            base_mean, near_column = call(
                functools.partial(end_mean, count),
                [sds((count, scenarios), F32), sds((4, face, scenarios), F32)],
                (mid, rm, y, near_share),
            )
        else:
            (base,) = call(functools.partial(inner_base, count), [rhs_shape], (mid, pm, rm))
        for turn in range(0, SWEEPS, 2):
            ending = final and turn == SWEEPS - 2
            first, second = exchange(first, second, 1 if ending else 0)
            common = (first, second, ff, y, rhs, link, faces)
            if turn < SWEEPS - 2:
                if near is None:
                    faces, first, second, near, near_link = call(
                        functools.partial(middle_window, count, True),
                        [faces_shape, sharing, sharing, sds((2, face, face), BF16), sds((2, face, scenarios), F32)],
                        common + (share,),
                    )
                else:
                    faces, first, second = call(
                        functools.partial(middle_window, count, False),
                        [faces_shape, message, message],
                        common + (near, near_link),
                    )
            elif not ending:
                outs = [faces_shape, message, message, faces_shape, mid_shape, faces_shape]
                outs = call(
                    functools.partial(step_window, count, step == 0),
                    outs + [share_shape] if step == 0 else outs,
                    common + (near, near_link, fm, pf, rf, base, wells),
                )
                faces, first, second, rhs, mid, y = outs[:6]
                if step == 0:
                    near_share = outs[6]
    taken_faces = lax.ppermute(faces, "cuts", ring)
    (parts,) = call(
        functools.partial(means_payload, count),
        [sds((slices * blocks, scenarios), F32)],
        (ff, y, rhs, link, faces, near, near_link, near_column, mass, base_mean, mean, op),
    )
    parts = parts.reshape(slices * sub, count, scenarios)
    parts = lax.all_to_all(parts, ("cuts", "sub"), 0, 0, tiled=True)
    taken_rhs, taken_faces, taken_mid = (
        pltpu.with_memory_space_constraint(v, pltpu.HBM) for v in (taken_rhs, taken_faces, taken_mid)
    )
    previous, early = call(
        functools.partial(last_window, count),
        [rhs_shape, rhs_shape],
        (first, second, ff, taken_rhs, link, taken_faces, near, near_link, rf, taken_mid, fm, rm, held[0]),
        stay=(3, 5, 9, 12),
        stay_out=(1,),
        scratch=[pltpu.VMEM(faces_shape.shape, F32)] * 3
        + [
            pltpu.VMEM(mid_shape.shape, F32),
            pltpu.VMEM(rhs_shape.shape, F32),
            pltpu.SemaphoreType.DMA((4,)),
            pltpu.SemaphoreType.DMA((count,)),
        ],
    )
    pieces = 2
    (result,) = call(
        functools.partial(correct, count, pieces),
        [rhs_shape],
        (parts, previous, early),
        stay=(2,),
        stay_out=(0,),
        scratch=[pltpu.VMEM(rhs_shape.shape, F32), pltpu.SemaphoreType.DMA((count * pieces,))],
        aliases={2: 0},
    )
    return result[None]


def solution(mesh):
    slices = mesh.shape["cuts"]

    def body(*args):
        return on_device(slices, *args)

    in_specs = (
        P("cuts", "sub", None, None),
        P("sub", None, None),
        P("sub", None, None),
        P("sub", None, None),
        P("sub", None, None),
        P(),
        P(),
    )
    return jax.shard_map(
        body,
        mesh=mesh,
        in_specs=in_specs,
        out_specs=P("cuts", "sub", None, None),
        check_vma=False,
    )
```

```python
import functools

import jax
import jax.numpy as jnp
from jax import lax
from jax.experimental import pallas as pl
from jax.experimental.pallas import tpu as pltpu
from jax.sharding import PartitionSpec as P


FINE_STEPS = 4
SWEEPS = 4
F32 = jnp.float32
BF16 = jnp.bfloat16
HIGH = lax.Precision.HIGHEST


def dot(a, b, dims=((1,), (0,)), precision=None):
    return lax.dot_general(a, b, (dims, ((), ())), precision=precision, preferred_element_type=F32)


def transpose(x):
    return jnp.transpose(x, (1, 0))


def iota(shape, axis):
    return lax.broadcasted_iota(jnp.int32, shape, axis)


def call(body, out_shape, args, flops=1 << 28, stay=(), stay_out=(), scratch=(), aliases=None):
    size = sum(a.size * a.dtype.itemsize for a in list(args) + list(out_shape))
    vmem = pl.BlockSpec(memory_space=pltpu.VMEM)
    hbm = pl.BlockSpec(memory_space=pltpu.HBM)
    return pl.pallas_call(
        body,
        out_shape=out_shape,
        in_specs=[hbm if k in stay else vmem for k in range(len(args))],
        out_specs=[hbm if k in stay_out else vmem for k in range(len(out_shape))],
        scratch_shapes=list(scratch),
        input_output_aliases=aliases or {},
        compiler_params=pltpu.CompilerParams(vmem_limit_bytes=24 << 20),
        cost_estimate=pl.CostEstimate(flops=flops, bytes_accessed=size, transcendentals=0),
    )(*args)


def face_vector(i, count, rhs_ref, link_ref, low, up, below, above):
    face = low[0].shape[0]
    under = below if i == 0 else up[i - 1]
    over = above if i == count - 1 else low[i + 1]
    v_low = rhs_ref[i, :face] + link_ref[2 * i] * under
    v_up = rhs_ref[i, face : 2 * face] + link_ref[2 * i + 1] * over
    return v_low.astype(BF16), v_up.astype(BF16)


def face_sweep(count, ff_ref, y_ref, rhs_ref, link_ref, low, up, below, above):
    face = low[0].shape[0]
    vectors, new_low, new_up = [], [], []
    for i in range(count):
        v = jnp.concatenate(face_vector(i, count, rhs_ref, link_ref, low, up, below, above), axis=0)
        x = y_ref[i] + dot(ff_ref[i], v)
        vectors.append(v)
        new_low.append(x[:face])
        new_up.append(x[face:])
    return vectors, new_low, new_up


def outgoing(count, ff_ref, y_ref, rhs_ref, link_ref, low, up):
    face = low[0].shape[0]
    last = count - 1
    zero = jnp.zeros_like(low[0])
    v = jnp.concatenate(face_vector(last, count, rhs_ref, link_ref, low, up, zero, zero), axis=0)
    next_up = y_ref[last, face:] + dot(ff_ref[last, face:], v)
    v = jnp.concatenate(face_vector(0, count, rhs_ref, link_ref, low, up, zero, zero), axis=0)
    next_low = y_ref[0, :face] + dot(ff_ref[0, :face], v)
    return (up[last], next_up), (low[0], next_low)


def store_messages(upward, downward, first_ref, second_ref):
    even = lax.rem(lax.axis_index("sub"), 2) == 0
    at = 0
    for one, other in zip(upward, downward):
        rows = pl.ds(at, one.shape[0])
        first_ref[rows] = jnp.where(even, one, other)
        second_ref[rows] = jnp.where(even, other, one)
        at += one.shape[0]


def received(first_ref, second_ref, rows):
    even = lax.rem(lax.axis_index("sub"), 2) == 0
    first, second = first_ref[rows], second_ref[rows]
    return jnp.where(even, second, first), jnp.where(even, first, second)


def read_all(sources, targets, sems):
    copies = [pltpu.make_async_copy(a, b, sems.at[k]) for k, (a, b) in enumerate(zip(sources, targets))]
    for copy in copies:
        copy.start()
    return copies


def face_rows(side, face, width):
    return slice(0, face) if side == 0 else slice(width - face, width)


def permutation(i, side, map_ref):
    face = map_ref.shape[2]
    return iota((face, face), 0) == map_ref[i, side : side + 1, :]


def as_bf16(mask):
    return mask.astype(F32).astype(BF16)


def prepare(count, start_hbm, source_hbm, inverse_hbm, map_hbm, trans_hbm,
            rhs_ref, link_ref, faces_ref, first_ref, second_ref,
            start_ref, source_ref, low_ref, up_ref, map_ref, trans_ref, sems):
    width = start_ref.shape[1]
    face = map_ref.shape[2]
    last = count - 1
    copies = read_all(
        (map_hbm, trans_hbm, start_hbm, source_hbm,
         inverse_hbm.at[0, pl.ds(0, face)], inverse_hbm.at[last, pl.ds(width - face, face)]),
        (map_ref, trans_ref, start_ref, source_ref, low_ref, up_ref),
        sems,
    )
    me, size = lax.axis_index("sub"), lax.axis_size("sub")
    copies[0].wait()
    copies[1].wait()
    perms = []
    for i in range(count):
        for side in range(2):
            linked = permutation(i, side, map_ref)
            column = jnp.sum(
                jnp.where(linked, trans_ref[i, side : side + 1, :], 0.0), axis=1, keepdims=True
            )
            if i == 0 and side == 0:
                column = jnp.where(me == 0, 0.0, column)
            if i == last and side == 1:
                column = jnp.where(me == size - 1, 0.0, column)
            link_ref[2 * i + side] = jnp.broadcast_to(column, (face, start_ref.shape[2]))
            perms.append(as_bf16(linked))
    for copy in copies[2:]:
        copy.wait()
    low, up = [], []
    for i in range(count):
        for side in range(2):
            rows = face_rows(side, face, width)
            to = slice(side * face, (side + 1) * face)
            value = start_ref[i, rows]
            high = value.astype(BF16)
            rest = value - high.astype(F32)
            mid = rest.astype(BF16)
            tail = (rest - mid.astype(F32)).astype(BF16)
            perm = perms[2 * i + side]
            parts = dot(perm, jnp.concatenate([high, mid, tail, source_ref[i, rows]], axis=1))
            cut = value.shape[1]
            parts = [parts[:, k * cut : (k + 1) * cut] for k in range(4)]
            rhs_ref[i, to] = parts[0] + parts[1] + parts[2] + parts[3]
            faces_ref[i, to] = value
            (up if side else low).append(value)
    zero = jnp.zeros_like(low[0])
    inner = slice(face, width - face)
    ahead, operators = [], []
    for i, matrix, at in ((last, up_ref, 1), (0, low_ref, 0)):
        columns = [
            dot(matrix[:, face_rows(side, face, width)], perms[2 * i + side], ((1,), (1,))).astype(BF16)
            for side in range(2)
        ]
        middle = (start_ref[i, inner] + source_ref[i, inner].astype(F32)).astype(BF16)
        v = jnp.concatenate(face_vector(i, count, rhs_ref, link_ref, low, up, zero, zero), axis=0)
        ahead.append(dot(matrix[:, inner], middle) + dot(jnp.concatenate(columns, axis=1), v))
        operators.append(columns[at].astype(F32))
    upward = (up[last], ahead[0], operators[0], transpose(link_ref[2 * last + 1])[:8])
    downward = (low[0], ahead[1], operators[1], transpose(link_ref[0])[:8])
    store_messages(upward, downward, first_ref, second_ref)


def prepare_rest(count, start_hbm, source_hbm, inverse_hbm, map_hbm,
                 ff_ref, fm_ref, pf_ref, rf_ref, pm_ref, rm_ref, mid_ref, wells_ref, y_ref, mean_ref,
                 start_ref, source_ref, inverse_ref, map_ref, sems):
    for copy in read_all(
        (start_hbm, source_hbm, inverse_hbm, map_hbm), (start_ref, source_ref, inverse_ref, map_ref), sems
    ):
        copy.wait()
    width = start_ref.shape[1]
    face = map_ref.shape[2]
    inner = slice(face, width - face)
    for i in range(count):
        perms = [as_bf16(permutation(i, side, map_ref)) for side in range(2)]
        for side in range(2):
            to = slice(side * face, (side + 1) * face)
            rows = face_rows(side, face, width)
            columns = dot(inverse_ref[i, :, rows], perms[side], ((1,), (1,))).astype(BF16)
            ff_ref[i, :face, to] = columns[:face]
            ff_ref[i, face:, to] = columns[width - face :]
            rf_ref[i, :, to] = columns[inner]
            wells_ref[i, to] = dot(perms[side], source_ref[i, rows])
            fm_ref[i, to] = inverse_ref[i, rows, inner]
        for side in range(2):
            to = slice(side * face, (side + 1) * face)
            pf_ref[i, to] = dot(perms[side], ff_ref[i, to]).astype(BF16)
            pm_ref[i, to] = dot(perms[side], fm_ref[i, to]).astype(BF16)
        rm_ref[i] = inverse_ref[i, inner, inner]
        wells = source_ref[i, inner].astype(F32)
        mid_ref[i] = start_ref[i, inner] + wells
        wells_ref[i, 2 * face :] = wells
        mean_ref[i : i + 1] = jnp.sum(start_ref[i], axis=0, keepdims=True) / width
        y_ref[i] = dot(fm_ref[i], mid_ref[i].astype(BF16))


def load_faces(count, faces_ref):
    face = faces_ref.shape[1] // 2
    return [faces_ref[i, :face] for i in range(count)], [faces_ref[i, face:] for i in range(count)]


def window(count, first_ref, second_ref, ff_ref, y_ref, rhs_ref, link_ref, faces_ref, near_ref, near_link_ref):
    low, up = load_faces(count, faces_ref)
    face = low[0].shape[0]
    below, above = received(first_ref, second_ref, slice(0, face))
    next_below, next_above = received(first_ref, second_ref, slice(face, 2 * face))
    next_below += dot(near_ref[0], (near_link_ref[0] * low[0]).astype(BF16))
    next_above += dot(near_ref[1], (near_link_ref[1] * up[count - 1]).astype(BF16))
    _, low, up = face_sweep(count, ff_ref, y_ref, rhs_ref, link_ref, low, up, below, above)
    return face_sweep(count, ff_ref, y_ref, rhs_ref, link_ref, low, up, next_below, next_above)


def middle_window(count, opening, *refs):
    if opening:
        (first_ref, second_ref, ff_ref, y_ref, rhs_ref, link_ref, faces_ref, share_ref,
         new_faces, out_first, out_second, near_ref, near_link_ref) = refs
        face = faces_ref.shape[1] // 2
        for k, part in enumerate(received(first_ref, second_ref, slice(2 * face, 3 * face))):
            near_ref[k] = part.astype(BF16)
        for k, part in enumerate(received(first_ref, second_ref, slice(3 * face, 3 * face + 8))):
            near_link_ref[k] = transpose(jnp.broadcast_to(part[:1], (face, face)))
    else:
        (first_ref, second_ref, ff_ref, y_ref, rhs_ref, link_ref, faces_ref, near_ref, near_link_ref,
         new_faces, out_first, out_second, *next_faces) = refs
        face = faces_ref.shape[1] // 2
    _, low, up = window(
        count, first_ref, second_ref, ff_ref, y_ref, rhs_ref, link_ref, faces_ref, near_ref, near_link_ref
    )
    for i in range(count):
        new_faces[i, :face] = low[i]
        new_faces[i, face:] = up[i]
    if not opening and next_faces:
        zero = jnp.zeros_like(low[0])
        _, next_low, next_up = face_sweep(count, ff_ref, y_ref, rhs_ref, link_ref, low, up, zero, zero)
        for i in range(count):
            next_faces[0][i, :face] = next_low[i]
            next_faces[0][i, face:] = next_up[i]
        upward, downward = (up[-1], next_up[-1]), (low[0], next_low[0])
    else:
        upward, downward = outgoing(count, ff_ref, y_ref, rhs_ref, link_ref, low, up)
    if opening:
        upward += (share_ref[1],)
        downward += (share_ref[0],)
    store_messages(upward, downward, out_first, out_second)


def step_window(count, opening, first_ref, second_ref, ff_ref, y_ref, rhs_ref, link_ref, faces_ref, near_ref,
                near_link_ref, fm_ref, pf_ref, rf_ref, base_ref, source_ref,
                new_faces, out_first, out_second, new_rhs, new_mid, new_y, *near_share):
    face = faces_ref.shape[1] // 2
    if opening:
        for k, part in enumerate(received(first_ref, second_ref, slice(2 * face, 2 * face + 8))):
            near_share[0][k] = part
    vectors, low, up = window(
        count, first_ref, second_ref, ff_ref, y_ref, rhs_ref, link_ref, faces_ref, near_ref, near_link_ref
    )
    for i in range(count):
        new_faces[i, :face] = low[i]
        new_faces[i, face:] = up[i]
        cut = 2 * face
        new_rhs[i] = base_ref[i, :cut] + dot(pf_ref[i], vectors[i]) + source_ref[i, :cut]
        rhs = base_ref[i, cut:] + dot(rf_ref[i], vectors[i]) + source_ref[i, cut:]
        new_mid[i] = rhs
        new_y[i] = dot(fm_ref[i], rhs.astype(BF16))
    store_messages(*outgoing(count, ff_ref, new_y, new_rhs, link_ref, low, up), out_first, out_second)


def inner_base(count, mid_ref, pm_ref, rm_ref, base_ref):
    for i in range(count):
        cut = pm_ref.shape[1]
        v = mid_ref[i].astype(BF16)
        base_ref[i, :cut] = dot(pm_ref[i], v)
        base_ref[i, cut:] = dot(rm_ref[i], v)


def shares(count, ff_ref, rf_ref, link_ref, mass_ref, share_ref):
    face = ff_ref.shape[1] // 2
    mass = []
    for i in range(count):
        total = jnp.sum(ff_ref[i].astype(F32), axis=0, keepdims=True)
        total += jnp.sum(rf_ref[i].astype(F32), axis=0, keepdims=True)
        width = 2 * face + rf_ref.shape[1]
        mass.append(jnp.broadcast_to(total / width, (8, 2 * face)))
        for k in range(2):
            line = mass[i][:1, k * face : (k + 1) * face]
            mass_ref[i, k * face : (k + 1) * face] = transpose(jnp.broadcast_to(line, (face, face)))
    for k, (outer, other) in enumerate(((0, 1), (count - 1, count - 2))):
        here, there = slice(k * face, (k + 1) * face), pl.ds((1 - k) * face, face)
        line = transpose(link_ref[2 * outer + k])[:8]
        inner_line = transpose(link_ref[2 * other + k])[:8]
        one = mass[outer][:, here] * line
        operator = ff_ref[outer, there, here].astype(F32)
        two = dot(mass[other][:, here] * inner_line, operator, precision=HIGH) * line
        share_ref[k] = jnp.where(iota(one.shape, 0) == 0, one, two)


def end_mean(count, mid_ref, rm_ref, y_ref, near_share_ref, out_ref, column_ref):
    face = y_ref.shape[1] // 2
    for k in range(2):
        for j in range(2):
            line = jnp.broadcast_to(near_share_ref[k, j : j + 1], (face, face))
            column_ref[2 * k + j] = transpose(line)
    for i in range(count):
        inner = dot(rm_ref[i], mid_ref[i].astype(BF16))
        total = jnp.sum(y_ref[i], axis=0, keepdims=True) + jnp.sum(inner, axis=0, keepdims=True)
        out_ref[i : i + 1] = total / (2 * face + rm_ref.shape[1])


def means_payload(count, rhs_ref, link_ref, faces_ref, next_ref, near_ref, near_link_ref,
                  column_ref, mass_ref, base_mean_ref, mean_ref, op_ref, parts_ref):
    low, up = load_faces(count, faces_ref)
    next_low, next_up = load_faces(count, next_ref)
    last = count - 1
    next_below = dot(near_ref[0], (near_link_ref[0] * low[0]).astype(BF16))
    next_above = dot(near_ref[1], (near_link_ref[1] * up[last]).astype(BF16))
    rows = []
    for i in range(count):
        v_low, v_up = face_vector(i, count, rhs_ref, link_ref, next_low, next_up, next_below, next_above)
        face = v_low.shape[0]
        own = weighted(mass_ref[i, :face], v_low.astype(F32)) + weighted(mass_ref[i, face:], v_up.astype(F32))
        rows.append(base_mean_ref[i : i + 1] + own)
    rows += [mean_ref[i : i + 1] for i in range(count)]
    for k, (two, one) in ((1, (up[last], next_up[last])), (0, (low[0], next_low[0]))):
        rows.append(weighted(column_ref[2 * k], one))
        rows.append(weighted(column_ref[2 * k + 1], two))
    total = op_ref[0] * rows[0]
    for k in range(1, len(rows)):
        total += op_ref[k] * rows[k]
    parts_ref[...] = total


def weighted(column, x):
    return jnp.sum(column * x, axis=0, keepdims=True)


def payload_rows(count):
    return -(-(2 * count + 4) // 8) * 8


def last_window(count, first_ref, second_ref, ff_ref, rhs_hbm, link_ref, faces_hbm, near_ref,
                near_link_ref, rf_ref, mid_hbm, fm_ref, rm_ref, start_hbm, end_ref, out_hbm,
                y_ref, rhs_ref, faces_ref, mid_ref, start_ref, sems, out_sems):
    copies = read_all((mid_hbm, rhs_hbm, faces_hbm, start_hbm), (mid_ref, rhs_ref, faces_ref, start_ref), sems)
    copies[0].wait()
    face = faces_ref.shape[1] // 2
    width = end_ref.shape[1]
    for i in range(count):
        v = mid_ref[i].astype(BF16)
        y_ref[i] = dot(fm_ref[i], v)
        end_ref[i, face : width - face] = dot(rm_ref[i], v)
    for copy in copies[1:]:
        copy.wait()
    vectors, low, up = window(
        count, first_ref, second_ref, ff_ref, y_ref, rhs_ref, link_ref, faces_ref, near_ref, near_link_ref
    )
    later = lax.axis_index("cuts") > 0
    copies = []
    for i in range(count):
        end_ref[i, :face] = low[i]
        end_ref[i, face : width - face] += dot(rf_ref[i], vectors[i])
        end_ref[i, width - face :] = up[i]
        start_ref[i] = jnp.where(later, end_ref[i], start_ref[i])
        copies.append(pltpu.make_async_copy(start_ref.at[i], out_hbm.at[i], out_sems.at[i]))
        copies[i].start()
    for copy in copies:
        copy.wait()


def coarse_operator(count, slices, partner_hbm, cond_hbm, out_ref, partner_ref, cond_ref, sems):
    copies = [
        pltpu.make_async_copy(partner_hbm, partner_ref, sems.at[0]),
        pltpu.make_async_copy(cond_hbm, cond_ref, sems.at[1]),
    ]
    for copy in copies:
        copy.start()
    for copy in copies:
        copy.wait()
    n = partner_ref.shape[0]
    row, col = iota((n, n), 0), iota((n, n), 1)
    weights = (jnp.abs(row - col) == 1).astype(F32)
    for b in range(n):
        to, cond = partner_ref[b], cond_ref[b]
        weights += jnp.where((row == b) & (col == to), cond, 0.0)
        weights += jnp.where((col == b) & (row == to), cond, 0.0)
    eye = (row == col).astype(F32)
    m = eye + eye * jnp.sum(weights, axis=1, keepdims=True) - weights
    for i in range(n):
        pivot = 1.0 / m[i : i + 1, i : i + 1]
        line = m[i : i + 1, :] * pivot
        column = m[:, i : i + 1]
        inner = jnp.where(col == i, -column * pivot, m - column * line)
        m = jnp.where(row == i, jnp.where(col == i, pivot, line), inner)
    here, me = lax.axis_index("cuts"), lax.axis_index("sub")
    shape = (n, payload_rows(count))
    block, item = iota(shape, 0) - me * count, iota(shape, 1)
    own = (item < count) & (block == item)
    above = (item >= 2 * count) & (item < 2 * count + 2) & (block == item - count)
    below = (item >= 2 * count + 2) & (item < 2 * count + 4) & (block == 2 * count + 1 - item)
    end = (own | above | below).astype(F32)
    start = ((item >= count) & (item < 2 * count) & (block == item - count)).astype(F32)
    ends, starts = [], []
    for _ in range(1, slices - 1):
        end, start = dot(m, end, precision=HIGH), dot(m, start, precision=HIGH)
        ends.append(end)
        starts.append(start)
    for s in range(slices):
        total = jnp.zeros(shape, F32)
        for k in range(1, slices - 1):
            if s - 1 - k >= 0:
                total += jnp.where(here == s - 1 - k, ends[k - 1], 0.0)
            if s - k >= 1:
                total -= jnp.where(here == s - k, starts[k - 1], 0.0)
        for k in range(out_ref.shape[0]):
            out_ref[k, s * n : (s + 1) * n] = jnp.broadcast_to(total[:, k : k + 1], (n, out_ref.shape[2]))


def correct(count, pieces, parts_ref, previous_ref, early_hbm, out_hbm, out_ref, sems):
    @pl.when(lax.axis_index("cuts") > 1)
    def _():
        mine = jnp.sum(parts_ref[...], axis=0)
        size = out_ref.shape[1] // pieces
        copies = []
        for i in range(count):
            for k in range(pieces):
                rows = pl.ds(k * size, size)
                out_ref[i, rows] = previous_ref[i, rows] + mine[i : i + 1]
                copies.append(
                    pltpu.make_async_copy(out_ref.at[i, rows], out_hbm.at[i, rows], sems.at[i * pieces + k])
                )
                copies[-1].start()
        for copy in copies:
            copy.wait()


def exchange(first, second, ahead=0):
    size, slices = lax.axis_size("sub"), lax.axis_size("cuts")
    pairs, other = [], []
    for c in range(slices):
        d = (c + ahead) % slices
        for i in range(size):
            pairs.append((c * size + i, d * size + (i ^ 1)))
            j = i + (1 if i % 2 else -1)
            if 0 <= j < size:
                other.append((c * size + i, d * size + j))
            elif ahead:
                other.append((c * size + i, d * size + i))
            else:
                other.append((c * size + i, (c ^ 1 if c ^ 1 < slices else c) * size + i))
    far = lax.ppermute(second, ("cuts", "sub"), other)
    near = lax.ppermute(first, ("cuts", "sub"), pairs)
    return near, far


def on_device(slices, start_states, source, block_inverse, face_map, transmissibility, partner, fracture_cond):
    start = start_states[0]
    count, width, scenarios = start.shape
    face = face_map.shape[-1]
    inner = width - 2 * face
    sub = lax.axis_size("sub")
    sds = jax.ShapeDtypeStruct
    message = sds((2 * face, scenarios), F32)
    opening = sds((3 * face + 8, scenarios), F32)
    sharing = sds((2 * face + 8, scenarios), F32)
    share_shape = sds((2, 8, face), F32)
    faces_shape = sds((count, 2 * face, scenarios), F32)
    rhs_shape = sds((count, width, scenarios), F32)
    held = [
        pltpu.with_memory_space_constraint(a, pltpu.HBM)
        for a in (start, source, block_inverse, face_map, transmissibility)
    ]
    buffers = [pltpu.VMEM(a.shape, a.dtype) for a in (start, source)]
    row = pltpu.VMEM((face, width), BF16)
    tables = [pltpu.VMEM(a.shape, a.dtype) for a in (face_map, transmissibility)]
    mid_shape = sds((count, inner, scenarios), F32)
    rhs, link, faces, first, second = call(
        functools.partial(prepare, count),
        [faces_shape, sds((2 * count, face, scenarios), F32), faces_shape, opening, opening],
        held,
        stay=range(5),
        scratch=buffers + [row, row] + tables + [pltpu.SemaphoreType.DMA((6,))],
    )
    ff, fm, pf, rf, pm, rm, mid, wells, y, mean = call(
        functools.partial(prepare_rest, count),
        [
            sds((count, 2 * face, 2 * face), BF16),
            sds((count, 2 * face, inner), BF16),
            sds((count, 2 * face, 2 * face), BF16),
            sds((count, inner, 2 * face), BF16),
            sds((count, 2 * face, inner), BF16),
            sds((count, inner, inner), BF16),
            mid_shape,
            rhs_shape,
            faces_shape,
            sds((count, scenarios), F32),
        ],
        held[:4],
        stay=range(4),
        scratch=buffers
        + [pltpu.VMEM(block_inverse.shape, BF16), tables[0], pltpu.SemaphoreType.DMA((4,))],
    )
    blocks = partner.shape[0]
    (op,) = call(
        functools.partial(coarse_operator, count, slices),
        [sds((2 * count + 4, slices * blocks, scenarios), F32)],
        [pltpu.with_memory_space_constraint(v, pltpu.HBM) for v in (partner, fracture_cond)],
        stay=range(2),
        scratch=[
            pltpu.SMEM((blocks,), jnp.int32),
            pltpu.SMEM((blocks,), F32),
            pltpu.SemaphoreType.DMA((2,)),
        ],
    )
    mass, share = call(
        functools.partial(shares, count),
        [faces_shape, share_shape],
        (ff, rf, link),
    )
    near = near_link = None
    ring = [(i, (i + 1) % slices) for i in range(slices)]
    for step in range(FINE_STEPS):
        final = step == FINE_STEPS - 1
        if final:
            taken_mid = lax.ppermute(mid, "cuts", ring)
            taken_rhs = lax.ppermute(rhs, "cuts", ring)
            base_mean, near_column = call(
                functools.partial(end_mean, count),
                [sds((count, scenarios), F32), sds((4, face, scenarios), F32)],
                (mid, rm, y, near_share),
            )
        else:
            (base,) = call(functools.partial(inner_base, count), [rhs_shape], (mid, pm, rm))
        for turn in range(0, SWEEPS, 2):
            ending = final and turn == SWEEPS - 2
            first, second = exchange(first, second, 1 if ending else 0)
            common = (first, second, ff, y, rhs, link, faces)
            if turn < SWEEPS - 2:
                if near is None:
                    faces, first, second, near, near_link = call(
                        functools.partial(middle_window, count, True),
                        [faces_shape, sharing, sharing, sds((2, face, face), BF16), sds((2, face, scenarios), F32)],
                        common + (share,),
                    )
                else:
                    faces, first, second, *ahead = call(
                        functools.partial(middle_window, count, False),
                        [faces_shape, message, message] + [faces_shape] * final,
                        common + (near, near_link),
                    )
            elif not ending:
                outs = [faces_shape, message, message, faces_shape, mid_shape, faces_shape]
                outs = call(
                    functools.partial(step_window, count, step == 0),
                    outs + [share_shape] if step == 0 else outs,
                    common + (near, near_link, fm, pf, rf, base, wells),
                )
                faces, first, second, rhs, mid, y = outs[:6]
                if step == 0:
                    near_share = outs[6]
    taken_faces = lax.ppermute(faces, "cuts", ring)
    (parts,) = call(
        functools.partial(means_payload, count),
        [sds((slices * blocks, scenarios), F32)],
        (rhs, link, faces, ahead[0], near, near_link, near_column, mass, base_mean, mean, op),
    )
    parts = parts.reshape(slices * sub, count, scenarios)
    parts = lax.all_to_all(parts, ("cuts", "sub"), 0, 0, tiled=True)
    taken_rhs, taken_faces, taken_mid = (
        pltpu.with_memory_space_constraint(v, pltpu.HBM) for v in (taken_rhs, taken_faces, taken_mid)
    )
    previous, early = call(
        functools.partial(last_window, count),
        [rhs_shape, rhs_shape],
        (first, second, ff, taken_rhs, link, taken_faces, near, near_link, rf, taken_mid, fm, rm, held[0]),
        stay=(3, 5, 9, 12),
        stay_out=(1,),
        scratch=[pltpu.VMEM(faces_shape.shape, F32)] * 3
        + [
            pltpu.VMEM(mid_shape.shape, F32),
            pltpu.VMEM(rhs_shape.shape, F32),
            pltpu.SemaphoreType.DMA((4,)),
            pltpu.SemaphoreType.DMA((count,)),
        ],
    )
    pieces = 2
    (result,) = call(
        functools.partial(correct, count, pieces),
        [rhs_shape],
        (parts, previous, early),
        stay=(2,),
        stay_out=(0,),
        scratch=[pltpu.VMEM(rhs_shape.shape, F32), pltpu.SemaphoreType.DMA((count * pieces,))],
        aliases={2: 0},
    )
    return result[None]


def solution(mesh):
    slices = mesh.shape["cuts"]

    def body(*args):
        return on_device(slices, *args)

    in_specs = (
        P("cuts", "sub", None, None),
        P("sub", None, None),
        P("sub", None, None),
        P("sub", None, None),
        P("sub", None, None),
        P(),
        P(),
    )
    return jax.shard_map(
        body,
        mesh=mesh,
        in_specs=in_specs,
        out_specs=P("cuts", "sub", None, None),
        check_vma=False,
    )
```

```python
import functools

import jax
import jax.numpy as jnp
from jax import lax
from jax.experimental import pallas as pl
from jax.experimental.pallas import tpu as pltpu
from jax.sharding import PartitionSpec as P


FINE_STEPS = 4
SWEEPS = 4
F32 = jnp.float32
BF16 = jnp.bfloat16
HIGH = lax.Precision.HIGHEST


def dot(a, b, dims=((1,), (0,)), precision=None):
    return lax.dot_general(a, b, (dims, ((), ())), precision=precision, preferred_element_type=F32)


def transpose(x):
    return jnp.transpose(x, (1, 0))


def iota(shape, axis):
    return lax.broadcasted_iota(jnp.int32, shape, axis)


def call(body, out_shape, args, flops=1 << 28, stay=(), stay_out=(), scratch=(), aliases=None):
    size = sum(a.size * a.dtype.itemsize for a in list(args) + list(out_shape))
    vmem = pl.BlockSpec(memory_space=pltpu.VMEM)
    hbm = pl.BlockSpec(memory_space=pltpu.HBM)
    return pl.pallas_call(
        body,
        out_shape=out_shape,
        in_specs=[hbm if k in stay else vmem for k in range(len(args))],
        out_specs=[hbm if k in stay_out else vmem for k in range(len(out_shape))],
        scratch_shapes=list(scratch),
        input_output_aliases=aliases or {},
        compiler_params=pltpu.CompilerParams(vmem_limit_bytes=24 << 20),
        cost_estimate=pl.CostEstimate(flops=flops, bytes_accessed=size, transcendentals=0),
    )(*args)


def face_vector(i, count, rhs_ref, link_ref, low, up, below, above):
    face = low[0].shape[0]
    under = below if i == 0 else up[i - 1]
    over = above if i == count - 1 else low[i + 1]
    v_low = rhs_ref[i, :face] + link_ref[2 * i] * under
    v_up = rhs_ref[i, face : 2 * face] + link_ref[2 * i + 1] * over
    return v_low.astype(BF16), v_up.astype(BF16)


def face_sweep(count, ff_ref, y_ref, rhs_ref, link_ref, low, up, below, above):
    face = low[0].shape[0]
    vectors, new_low, new_up = [], [], []
    for i in range(count):
        v = jnp.concatenate(face_vector(i, count, rhs_ref, link_ref, low, up, below, above), axis=0)
        x = y_ref[i] + dot(ff_ref[i], v)
        vectors.append(v)
        new_low.append(x[:face])
        new_up.append(x[face:])
    return vectors, new_low, new_up


def outgoing(count, ff_ref, y_low, y_up, rhs_ref, link_ref, low, up):
    face = low[0].shape[0]
    last = count - 1
    zero = jnp.zeros_like(low[0])
    v = jnp.concatenate(face_vector(last, count, rhs_ref, link_ref, low, up, zero, zero), axis=0)
    next_up = y_up + dot(ff_ref[last, face:], v)
    v = jnp.concatenate(face_vector(0, count, rhs_ref, link_ref, low, up, zero, zero), axis=0)
    next_low = y_low + dot(ff_ref[0, :face], v)
    return (up[last], next_up), (low[0], next_low)


def store_messages(upward, downward, first_ref, second_ref):
    even = lax.rem(lax.axis_index("sub"), 2) == 0
    at = 0
    for one, other in zip(upward, downward):
        rows = pl.ds(at, one.shape[0])
        first_ref[rows] = jnp.where(even, one, other)
        second_ref[rows] = jnp.where(even, other, one)
        at += one.shape[0]


def received(first_ref, second_ref, rows):
    even = lax.rem(lax.axis_index("sub"), 2) == 0
    first, second = first_ref[rows], second_ref[rows]
    return jnp.where(even, second, first), jnp.where(even, first, second)


def read_all(sources, targets, sems):
    copies = [pltpu.make_async_copy(a, b, sems.at[k]) for k, (a, b) in enumerate(zip(sources, targets))]
    for copy in copies:
        copy.start()
    return copies


def face_rows(side, face, width):
    return slice(0, face) if side == 0 else slice(width - face, width)


def permutation(i, side, map_ref):
    face = map_ref.shape[2]
    return iota((face, face), 0) == map_ref[i, side : side + 1, :]


def as_bf16(mask):
    return mask.astype(F32).astype(BF16)


def prepare(count, start_hbm, source_hbm, inverse_hbm, map_hbm, trans_hbm,
            rhs_ref, link_ref, faces_ref, first_ref, second_ref,
            start_ref, source_ref, low_ref, up_ref, map_ref, trans_ref, sems):
    width = start_ref.shape[1]
    face = map_ref.shape[2]
    last = count - 1
    copies = read_all(
        (map_hbm, trans_hbm, start_hbm, source_hbm,
         inverse_hbm.at[0, pl.ds(0, face)], inverse_hbm.at[last, pl.ds(width - face, face)]),
        (map_ref, trans_ref, start_ref, source_ref, low_ref, up_ref),
        sems,
    )
    me, size = lax.axis_index("sub"), lax.axis_size("sub")
    copies[0].wait()
    copies[1].wait()
    perms = []
    for i in range(count):
        for side in range(2):
            linked = permutation(i, side, map_ref)
            column = jnp.sum(
                jnp.where(linked, trans_ref[i, side : side + 1, :], 0.0), axis=1, keepdims=True
            )
            if i == 0 and side == 0:
                column = jnp.where(me == 0, 0.0, column)
            if i == last and side == 1:
                column = jnp.where(me == size - 1, 0.0, column)
            link_ref[2 * i + side] = jnp.broadcast_to(column, (face, start_ref.shape[2]))
            perms.append(as_bf16(linked))
    for copy in copies[2:]:
        copy.wait()
    low, up = [], []
    for i in range(count):
        for side in range(2):
            rows = face_rows(side, face, width)
            to = slice(side * face, (side + 1) * face)
            value = start_ref[i, rows]
            high = value.astype(BF16)
            rest = value - high.astype(F32)
            mid = rest.astype(BF16)
            tail = (rest - mid.astype(F32)).astype(BF16)
            perm = perms[2 * i + side]
            parts = dot(perm, jnp.concatenate([high, mid, tail, source_ref[i, rows]], axis=1))
            cut = value.shape[1]
            parts = [parts[:, k * cut : (k + 1) * cut] for k in range(4)]
            rhs_ref[i, to] = parts[0] + parts[1] + parts[2] + parts[3]
            faces_ref[i, to] = value
            (up if side else low).append(value)
    zero = jnp.zeros_like(low[0])
    inner = slice(face, width - face)
    ahead, operators = [], []
    for i, matrix, at in ((last, up_ref, 1), (0, low_ref, 0)):
        columns = [
            dot(matrix[:, face_rows(side, face, width)], perms[2 * i + side], ((1,), (1,))).astype(BF16)
            for side in range(2)
        ]
        middle = (start_ref[i, inner] + source_ref[i, inner].astype(F32)).astype(BF16)
        v = jnp.concatenate(face_vector(i, count, rhs_ref, link_ref, low, up, zero, zero), axis=0)
        ahead.append(dot(matrix[:, inner], middle) + dot(jnp.concatenate(columns, axis=1), v))
        operators.append(columns[at].astype(F32))
    upward = (up[last], ahead[0], operators[0], transpose(link_ref[2 * last + 1])[:8])
    downward = (low[0], ahead[1], operators[1], transpose(link_ref[0])[:8])
    store_messages(upward, downward, first_ref, second_ref)


def prepare_rest(count, start_hbm, source_hbm, inverse_hbm, map_hbm,
                 ff_ref, fm_ref, pf_ref, rf_ref, pm_ref, rm_ref, mid_ref, wells_ref, mean_ref,
                 start_ref, source_ref, inverse_ref, map_ref, sems):
    for copy in read_all(
        (start_hbm, source_hbm, inverse_hbm, map_hbm), (start_ref, source_ref, inverse_ref, map_ref), sems
    ):
        copy.wait()
    width = start_ref.shape[1]
    face = map_ref.shape[2]
    inner = slice(face, width - face)
    for i in range(count):
        perms = [as_bf16(permutation(i, side, map_ref)) for side in range(2)]
        for side in range(2):
            to = slice(side * face, (side + 1) * face)
            rows = face_rows(side, face, width)
            columns = dot(inverse_ref[i, :, rows], perms[side], ((1,), (1,))).astype(BF16)
            ff_ref[i, :face, to] = columns[:face]
            ff_ref[i, face:, to] = columns[width - face :]
            rf_ref[i, :, to] = columns[inner]
            wells_ref[i, to] = dot(perms[side], source_ref[i, rows])
            fm_ref[i, to] = inverse_ref[i, rows, inner]
        for side in range(2):
            to = slice(side * face, (side + 1) * face)
            pf_ref[i, to] = dot(perms[side], ff_ref[i, to]).astype(BF16)
            pm_ref[i, to] = dot(perms[side], fm_ref[i, to]).astype(BF16)
        rm_ref[i] = inverse_ref[i, inner, inner]
        wells = source_ref[i, inner].astype(F32)
        mid_ref[i] = start_ref[i, inner] + wells
        wells_ref[i, 2 * face :] = wells
        mean_ref[i : i + 1] = jnp.sum(start_ref[i], axis=0, keepdims=True) / width


def load_faces(count, faces_ref):
    face = faces_ref.shape[1] // 2
    return [faces_ref[i, :face] for i in range(count)], [faces_ref[i, face:] for i in range(count)]


def window(count, first_ref, second_ref, ff_ref, y_ref, rhs_ref, link_ref, faces_ref, near_ref, near_link_ref):
    low, up = load_faces(count, faces_ref)
    face = low[0].shape[0]
    below, above = received(first_ref, second_ref, slice(0, face))
    next_below, next_above = received(first_ref, second_ref, slice(face, 2 * face))
    next_below += dot(near_ref[0], (near_link_ref[0] * low[0]).astype(BF16))
    next_above += dot(near_ref[1], (near_link_ref[1] * up[count - 1]).astype(BF16))
    _, low, up = face_sweep(count, ff_ref, y_ref, rhs_ref, link_ref, low, up, below, above)
    return face_sweep(count, ff_ref, y_ref, rhs_ref, link_ref, low, up, next_below, next_above)


def middle_window(count, opening, *refs):
    if opening:
        (first_ref, second_ref, ff_ref, y_ref, rhs_ref, link_ref, faces_ref, share_ref,
         new_faces, out_first, out_second, near_ref, near_link_ref) = refs
        face = faces_ref.shape[1] // 2
        for k, part in enumerate(received(first_ref, second_ref, slice(2 * face, 3 * face))):
            near_ref[k] = part.astype(BF16)
        for k, part in enumerate(received(first_ref, second_ref, slice(3 * face, 3 * face + 8))):
            near_link_ref[k] = transpose(jnp.broadcast_to(part[:1], (face, face)))
    else:
        (first_ref, second_ref, ff_ref, y_ref, rhs_ref, link_ref, faces_ref, near_ref, near_link_ref,
         new_faces, out_first, out_second, *next_faces) = refs
        face = faces_ref.shape[1] // 2
    _, low, up = window(
        count, first_ref, second_ref, ff_ref, y_ref, rhs_ref, link_ref, faces_ref, near_ref, near_link_ref
    )
    for i in range(count):
        new_faces[i, :face] = low[i]
        new_faces[i, face:] = up[i]
    if not opening and next_faces:
        zero = jnp.zeros_like(low[0])
        _, next_low, next_up = face_sweep(count, ff_ref, y_ref, rhs_ref, link_ref, low, up, zero, zero)
        for i in range(count):
            next_faces[0][i, :face] = next_low[i]
            next_faces[0][i, face:] = next_up[i]
        upward, downward = (up[-1], next_up[-1]), (low[0], next_low[0])
    else:
        upward, downward = outgoing(count, ff_ref, y_ref[0, :face], y_ref[count - 1, face:], rhs_ref, link_ref, low, up)
    if opening:
        upward += (share_ref[1],)
        downward += (share_ref[0],)
    store_messages(upward, downward, out_first, out_second)


def step_window(count, opening, first_ref, second_ref, ff_ref, y_ref, rhs_ref, link_ref, faces_ref, near_ref,
                near_link_ref, fm_ref, pf_ref, rf_ref, base_ref, source_ref,
                new_faces, out_first, out_second, new_rhs, new_mid, *near_share):
    face = faces_ref.shape[1] // 2
    if opening:
        for k, part in enumerate(received(first_ref, second_ref, slice(2 * face, 2 * face + 8))):
            near_share[0][k] = part
    vectors, low, up = window(
        count, first_ref, second_ref, ff_ref, y_ref, rhs_ref, link_ref, faces_ref, near_ref, near_link_ref
    )
    for i in range(count):
        new_faces[i, :face] = low[i]
        new_faces[i, face:] = up[i]
        cut = 2 * face
        new_rhs[i] = base_ref[i, :cut] + dot(pf_ref[i], vectors[i]) + source_ref[i, :cut]
        rhs = base_ref[i, cut:] + dot(rf_ref[i], vectors[i]) + source_ref[i, cut:]
        new_mid[i] = rhs
        if i == 0:
            y_low = dot(fm_ref[i, :face], rhs.astype(BF16))
        if i == count - 1:
            y_up = dot(fm_ref[i, face:], rhs.astype(BF16))
    store_messages(*outgoing(count, ff_ref, y_low, y_up, new_rhs, link_ref, low, up), out_first, out_second)


def inner_base(count, mid_ref, pm_ref, rm_ref, fm_ref, base_ref, y_ref):
    for i in range(count):
        cut = pm_ref.shape[1]
        v = mid_ref[i].astype(BF16)
        base_ref[i, :cut] = dot(pm_ref[i], v)
        base_ref[i, cut:] = dot(rm_ref[i], v)
        y_ref[i] = dot(fm_ref[i], v)


def shares(count, ff_ref, rf_ref, link_ref, mass_ref, share_ref):
    face = ff_ref.shape[1] // 2
    mass = []
    for i in range(count):
        total = jnp.sum(ff_ref[i].astype(F32), axis=0, keepdims=True)
        total += jnp.sum(rf_ref[i].astype(F32), axis=0, keepdims=True)
        width = 2 * face + rf_ref.shape[1]
        mass.append(jnp.broadcast_to(total / width, (8, 2 * face)))
        for k in range(2):
            line = mass[i][:1, k * face : (k + 1) * face]
            mass_ref[i, k * face : (k + 1) * face] = transpose(jnp.broadcast_to(line, (face, face)))
    for k, (outer, other) in enumerate(((0, 1), (count - 1, count - 2))):
        here, there = slice(k * face, (k + 1) * face), pl.ds((1 - k) * face, face)
        line = transpose(link_ref[2 * outer + k])[:8]
        inner_line = transpose(link_ref[2 * other + k])[:8]
        one = mass[outer][:, here] * line
        operator = ff_ref[outer, there, here].astype(F32)
        two = dot(mass[other][:, here] * inner_line, operator, precision=HIGH) * line
        share_ref[k] = jnp.where(iota(one.shape, 0) == 0, one, two)


def end_mean(count, mid_ref, rm_ref, fm_ref, near_share_ref, out_ref, column_ref, y_ref):
    face = y_ref.shape[1] // 2
    for k in range(2):
        for j in range(2):
            line = jnp.broadcast_to(near_share_ref[k, j : j + 1], (face, face))
            column_ref[2 * k + j] = transpose(line)
    for i in range(count):
        v = mid_ref[i].astype(BF16)
        y = dot(fm_ref[i], v)
        y_ref[i] = y
        inner = dot(rm_ref[i], v)
        total = jnp.sum(y, axis=0, keepdims=True) + jnp.sum(inner, axis=0, keepdims=True)
        out_ref[i : i + 1] = total / (2 * face + rm_ref.shape[1])


def means_payload(count, rhs_ref, link_ref, faces_ref, next_ref, near_ref, near_link_ref,
                  column_ref, mass_ref, base_mean_ref, mean_ref, op_ref, parts_ref):
    low, up = load_faces(count, faces_ref)
    next_low, next_up = load_faces(count, next_ref)
    last = count - 1
    next_below = dot(near_ref[0], (near_link_ref[0] * low[0]).astype(BF16))
    next_above = dot(near_ref[1], (near_link_ref[1] * up[last]).astype(BF16))
    rows = []
    for i in range(count):
        v_low, v_up = face_vector(i, count, rhs_ref, link_ref, next_low, next_up, next_below, next_above)
        face = v_low.shape[0]
        own = weighted(mass_ref[i, :face], v_low.astype(F32)) + weighted(mass_ref[i, face:], v_up.astype(F32))
        rows.append(base_mean_ref[i : i + 1] + own)
    rows += [mean_ref[i : i + 1] for i in range(count)]
    for k, (two, one) in ((1, (up[last], next_up[last])), (0, (low[0], next_low[0]))):
        rows.append(weighted(column_ref[2 * k], one))
        rows.append(weighted(column_ref[2 * k + 1], two))
    total = op_ref[0] * rows[0]
    for k in range(1, len(rows)):
        total += op_ref[k] * rows[k]
    parts_ref[...] = total


def weighted(column, x):
    return jnp.sum(column * x, axis=0, keepdims=True)


def payload_rows(count):
    return -(-(2 * count + 4) // 8) * 8


def last_window(count, first_ref, second_ref, ff_ref, rhs_hbm, link_ref, faces_hbm, near_ref,
                near_link_ref, rf_ref, mid_hbm, fm_ref, rm_ref, start_hbm, end_ref, out_hbm,
                y_ref, rhs_ref, faces_ref, mid_ref, start_ref, sems, out_sems):
    copies = read_all((mid_hbm, rhs_hbm, faces_hbm, start_hbm), (mid_ref, rhs_ref, faces_ref, start_ref), sems)
    copies[0].wait()
    face = faces_ref.shape[1] // 2
    width = end_ref.shape[1]
    for i in range(count):
        v = mid_ref[i].astype(BF16)
        y_ref[i] = dot(fm_ref[i], v)
        end_ref[i, face : width - face] = dot(rm_ref[i], v)
    for copy in copies[1:]:
        copy.wait()
    vectors, low, up = window(
        count, first_ref, second_ref, ff_ref, y_ref, rhs_ref, link_ref, faces_ref, near_ref, near_link_ref
    )
    later = lax.axis_index("cuts") > 0
    copies = []
    for i in range(count):
        end_ref[i, :face] = low[i]
        end_ref[i, face : width - face] += dot(rf_ref[i], vectors[i])
        end_ref[i, width - face :] = up[i]
        start_ref[i] = jnp.where(later, end_ref[i], start_ref[i])
        copies.append(pltpu.make_async_copy(start_ref.at[i], out_hbm.at[i], out_sems.at[i]))
        copies[i].start()
    for copy in copies:
        copy.wait()


def coarse_operator(count, slices, partner_hbm, cond_hbm, out_ref, partner_ref, cond_ref, sems):
    copies = [
        pltpu.make_async_copy(partner_hbm, partner_ref, sems.at[0]),
        pltpu.make_async_copy(cond_hbm, cond_ref, sems.at[1]),
    ]
    for copy in copies:
        copy.start()
    for copy in copies:
        copy.wait()
    n = partner_ref.shape[0]
    row, col = iota((n, n), 0), iota((n, n), 1)
    weights = (jnp.abs(row - col) == 1).astype(F32)
    for b in range(n):
        to, cond = partner_ref[b], cond_ref[b]
        weights += jnp.where((row == b) & (col == to), cond, 0.0)
        weights += jnp.where((col == b) & (row == to), cond, 0.0)
    eye = (row == col).astype(F32)
    m = eye + eye * jnp.sum(weights, axis=1, keepdims=True) - weights
    for i in range(n):
        pivot = 1.0 / m[i : i + 1, i : i + 1]
        line = m[i : i + 1, :] * pivot
        column = m[:, i : i + 1]
        inner = jnp.where(col == i, -column * pivot, m - column * line)
        m = jnp.where(row == i, jnp.where(col == i, pivot, line), inner)
    here, me = lax.axis_index("cuts"), lax.axis_index("sub")
    shape = (n, payload_rows(count))
    block, item = iota(shape, 0) - me * count, iota(shape, 1)
    own = (item < count) & (block == item)
    above = (item >= 2 * count) & (item < 2 * count + 2) & (block == item - count)
    below = (item >= 2 * count + 2) & (item < 2 * count + 4) & (block == 2 * count + 1 - item)
    end = (own | above | below).astype(F32)
    start = ((item >= count) & (item < 2 * count) & (block == item - count)).astype(F32)
    ends, starts = [], []
    for _ in range(1, slices - 1):
        end, start = dot(m, end, precision=HIGH), dot(m, start, precision=HIGH)
        ends.append(end)
        starts.append(start)
    for s in range(slices):
        total = jnp.zeros(shape, F32)
        for k in range(1, slices - 1):
            if s - 1 - k >= 0:
                total += jnp.where(here == s - 1 - k, ends[k - 1], 0.0)
            if s - k >= 1:
                total -= jnp.where(here == s - k, starts[k - 1], 0.0)
        for k in range(out_ref.shape[0]):
            out_ref[k, s * n : (s + 1) * n] = jnp.broadcast_to(total[:, k : k + 1], (n, out_ref.shape[2]))


def correct(count, pieces, parts_ref, previous_ref, early_hbm, out_hbm, out_ref, sems):
    @pl.when(lax.axis_index("cuts") > 1)
    def _():
        mine = jnp.sum(parts_ref[...], axis=0)
        size = out_ref.shape[1] // pieces
        copies = []
        for i in range(count):
            for k in range(pieces):
                rows = pl.ds(k * size, size)
                out_ref[i, rows] = previous_ref[i, rows] + mine[i : i + 1]
                copies.append(
                    pltpu.make_async_copy(out_ref.at[i, rows], out_hbm.at[i, rows], sems.at[i * pieces + k])
                )
                copies[-1].start()
        for copy in copies:
            copy.wait()


def exchange(first, second, ahead=0):
    size, slices = lax.axis_size("sub"), lax.axis_size("cuts")
    pairs, other = [], []
    for c in range(slices):
        d = (c + ahead) % slices
        for i in range(size):
            pairs.append((c * size + i, d * size + (i ^ 1)))
            j = i + (1 if i % 2 else -1)
            if 0 <= j < size:
                other.append((c * size + i, d * size + j))
            elif ahead:
                other.append((c * size + i, d * size + i))
            else:
                other.append((c * size + i, (c ^ 1 if c ^ 1 < slices else c) * size + i))
    far = lax.ppermute(second, ("cuts", "sub"), other)
    near = lax.ppermute(first, ("cuts", "sub"), pairs)
    return near, far


def on_device(slices, start_states, source, block_inverse, face_map, transmissibility, partner, fracture_cond):
    start = start_states[0]
    count, width, scenarios = start.shape
    face = face_map.shape[-1]
    inner = width - 2 * face
    sub = lax.axis_size("sub")
    sds = jax.ShapeDtypeStruct
    message = sds((2 * face, scenarios), F32)
    opening = sds((3 * face + 8, scenarios), F32)
    sharing = sds((2 * face + 8, scenarios), F32)
    share_shape = sds((2, 8, face), F32)
    faces_shape = sds((count, 2 * face, scenarios), F32)
    rhs_shape = sds((count, width, scenarios), F32)
    held = [
        pltpu.with_memory_space_constraint(a, pltpu.HBM)
        for a in (start, source, block_inverse, face_map, transmissibility)
    ]
    buffers = [pltpu.VMEM(a.shape, a.dtype) for a in (start, source)]
    row = pltpu.VMEM((face, width), BF16)
    tables = [pltpu.VMEM(a.shape, a.dtype) for a in (face_map, transmissibility)]
    mid_shape = sds((count, inner, scenarios), F32)
    rhs, link, faces, first, second = call(
        functools.partial(prepare, count),
        [faces_shape, sds((2 * count, face, scenarios), F32), faces_shape, opening, opening],
        held,
        stay=range(5),
        scratch=buffers + [row, row] + tables + [pltpu.SemaphoreType.DMA((6,))],
    )
    ff, fm, pf, rf, pm, rm, mid, wells, mean = call(
        functools.partial(prepare_rest, count),
        [
            sds((count, 2 * face, 2 * face), BF16),
            sds((count, 2 * face, inner), BF16),
            sds((count, 2 * face, 2 * face), BF16),
            sds((count, inner, 2 * face), BF16),
            sds((count, 2 * face, inner), BF16),
            sds((count, inner, inner), BF16),
            mid_shape,
            rhs_shape,
            sds((count, scenarios), F32),
        ],
        held[:4],
        stay=range(4),
        scratch=buffers
        + [pltpu.VMEM(block_inverse.shape, BF16), tables[0], pltpu.SemaphoreType.DMA((4,))],
    )
    blocks = partner.shape[0]
    (op,) = call(
        functools.partial(coarse_operator, count, slices),
        [sds((2 * count + 4, slices * blocks, scenarios), F32)],
        [pltpu.with_memory_space_constraint(v, pltpu.HBM) for v in (partner, fracture_cond)],
        stay=range(2),
        scratch=[
            pltpu.SMEM((blocks,), jnp.int32),
            pltpu.SMEM((blocks,), F32),
            pltpu.SemaphoreType.DMA((2,)),
        ],
    )
    mass, share = call(
        functools.partial(shares, count),
        [faces_shape, share_shape],
        (ff, rf, link),
    )
    near = near_link = None
    ring = [(i, (i + 1) % slices) for i in range(slices)]
    for step in range(FINE_STEPS):
        final = step == FINE_STEPS - 1
        if final:
            taken_mid = lax.ppermute(mid, "cuts", ring)
            taken_rhs = lax.ppermute(rhs, "cuts", ring)
            base_mean, near_column, y = call(
                functools.partial(end_mean, count),
                [sds((count, scenarios), F32), sds((4, face, scenarios), F32), faces_shape],
                (mid, rm, fm, near_share),
            )
        else:
            base, y = call(functools.partial(inner_base, count), [rhs_shape, faces_shape], (mid, pm, rm, fm))
        for turn in range(0, SWEEPS, 2):
            ending = final and turn == SWEEPS - 2
            first, second = exchange(first, second, 1 if ending else 0)
            common = (first, second, ff, y, rhs, link, faces)
            if turn < SWEEPS - 2:
                if near is None:
                    faces, first, second, near, near_link = call(
                        functools.partial(middle_window, count, True),
                        [faces_shape, sharing, sharing, sds((2, face, face), BF16), sds((2, face, scenarios), F32)],
                        common + (share,),
                    )
                else:
                    faces, first, second, *ahead = call(
                        functools.partial(middle_window, count, False),
                        [faces_shape, message, message] + [faces_shape] * final,
                        common + (near, near_link),
                    )
            elif not ending:
                outs = [faces_shape, message, message, faces_shape, mid_shape]
                outs = call(
                    functools.partial(step_window, count, step == 0),
                    outs + [share_shape] if step == 0 else outs,
                    common + (near, near_link, fm, pf, rf, base, wells),
                )
                faces, first, second, rhs, mid = outs[:5]
                if step == 0:
                    near_share = outs[5]
    taken_faces = lax.ppermute(faces, "cuts", ring)
    (parts,) = call(
        functools.partial(means_payload, count),
        [sds((slices * blocks, scenarios), F32)],
        (rhs, link, faces, ahead[0], near, near_link, near_column, mass, base_mean, mean, op),
    )
    parts = parts.reshape(slices * sub, count, scenarios)
    parts = lax.all_to_all(parts, ("cuts", "sub"), 0, 0, tiled=True)
    taken_rhs, taken_faces, taken_mid = (
        pltpu.with_memory_space_constraint(v, pltpu.HBM) for v in (taken_rhs, taken_faces, taken_mid)
    )
    previous, early = call(
        functools.partial(last_window, count),
        [rhs_shape, rhs_shape],
        (first, second, ff, taken_rhs, link, taken_faces, near, near_link, rf, taken_mid, fm, rm, held[0]),
        stay=(3, 5, 9, 12),
        stay_out=(1,),
        scratch=[pltpu.VMEM(faces_shape.shape, F32)] * 3
        + [
            pltpu.VMEM(mid_shape.shape, F32),
            pltpu.VMEM(rhs_shape.shape, F32),
            pltpu.SemaphoreType.DMA((4,)),
            pltpu.SemaphoreType.DMA((count,)),
        ],
    )
    pieces = 2
    (result,) = call(
        functools.partial(correct, count, pieces),
        [rhs_shape],
        (parts, previous, early),
        stay=(2,),
        stay_out=(0,),
        scratch=[pltpu.VMEM(rhs_shape.shape, F32), pltpu.SemaphoreType.DMA((count * pieces,))],
        aliases={2: 0},
    )
    return result[None]


def solution(mesh):
    slices = mesh.shape["cuts"]

    def body(*args):
        return on_device(slices, *args)

    in_specs = (
        P("cuts", "sub", None, None),
        P("sub", None, None),
        P("sub", None, None),
        P("sub", None, None),
        P("sub", None, None),
        P(),
        P(),
    )
    return jax.shard_map(
        body,
        mesh=mesh,
        in_specs=in_specs,
        out_specs=P("cuts", "sub", None, None),
        check_vma=False,
    )
```

```python
import functools

import jax
import jax.numpy as jnp
from jax import lax
from jax.experimental import pallas as pl
from jax.experimental.pallas import tpu as pltpu
from jax.sharding import PartitionSpec as P


FINE_STEPS = 4
SWEEPS = 4
F32 = jnp.float32
BF16 = jnp.bfloat16
HIGH = lax.Precision.HIGHEST


def dot(a, b, dims=((1,), (0,)), precision=None):
    return lax.dot_general(a, b, (dims, ((), ())), precision=precision, preferred_element_type=F32)


def transpose(x):
    return jnp.transpose(x, (1, 0))


def iota(shape, axis):
    return lax.broadcasted_iota(jnp.int32, shape, axis)


def call(body, out_shape, args, flops=1 << 28, stay=(), stay_out=(), scratch=(), aliases=None):
    size = sum(a.size * a.dtype.itemsize for a in list(args) + list(out_shape))
    vmem = pl.BlockSpec(memory_space=pltpu.VMEM)
    hbm = pl.BlockSpec(memory_space=pltpu.HBM)
    return pl.pallas_call(
        body,
        out_shape=out_shape,
        in_specs=[hbm if k in stay else vmem for k in range(len(args))],
        out_specs=[hbm if k in stay_out else vmem for k in range(len(out_shape))],
        scratch_shapes=list(scratch),
        input_output_aliases=aliases or {},
        compiler_params=pltpu.CompilerParams(vmem_limit_bytes=24 << 20),
        cost_estimate=pl.CostEstimate(flops=flops, bytes_accessed=size, transcendentals=0),
    )(*args)


def face_vector(i, count, rhs_ref, link_ref, low, up, below, above):
    face = low[0].shape[0]
    under = below if i == 0 else up[i - 1]
    over = above if i == count - 1 else low[i + 1]
    v_low = rhs_ref[i, :face] + link_ref[2 * i] * under
    v_up = rhs_ref[i, face : 2 * face] + link_ref[2 * i + 1] * over
    return v_low.astype(BF16), v_up.astype(BF16)


def face_sweep(count, ff_ref, y_ref, rhs_ref, link_ref, low, up, below, above):
    face = low[0].shape[0]
    vectors, new_low, new_up = [], [], []
    for i in range(count):
        v = jnp.concatenate(face_vector(i, count, rhs_ref, link_ref, low, up, below, above), axis=0)
        x = y_ref[i] + dot(ff_ref[i], v)
        vectors.append(v)
        new_low.append(x[:face])
        new_up.append(x[face:])
    return vectors, new_low, new_up


def outgoing(count, ff_ref, y_low, y_up, rhs_ref, link_ref, low, up):
    face = low[0].shape[0]
    last = count - 1
    zero = jnp.zeros_like(low[0])
    v = jnp.concatenate(face_vector(last, count, rhs_ref, link_ref, low, up, zero, zero), axis=0)
    next_up = y_up + dot(ff_ref[last, face:], v)
    v = jnp.concatenate(face_vector(0, count, rhs_ref, link_ref, low, up, zero, zero), axis=0)
    next_low = y_low + dot(ff_ref[0, :face], v)
    return (up[last], next_up), (low[0], next_low)


def store_messages(upward, downward, first_ref, second_ref):
    even = lax.rem(lax.axis_index("sub"), 2) == 0
    at = 0
    for one, other in zip(upward, downward):
        rows = pl.ds(at, one.shape[0])
        first_ref[rows] = jnp.where(even, one, other)
        second_ref[rows] = jnp.where(even, other, one)
        at += one.shape[0]


def received(first_ref, second_ref, rows):
    even = lax.rem(lax.axis_index("sub"), 2) == 0
    first, second = first_ref[rows], second_ref[rows]
    return jnp.where(even, second, first), jnp.where(even, first, second)


def read_all(sources, targets, sems):
    copies = [pltpu.make_async_copy(a, b, sems.at[k]) for k, (a, b) in enumerate(zip(sources, targets))]
    for copy in copies:
        copy.start()
    return copies


def face_rows(side, face, width):
    return slice(0, face) if side == 0 else slice(width - face, width)


def permutation(i, side, map_ref):
    face = map_ref.shape[2]
    return iota((face, face), 0) == map_ref[i, side : side + 1, :]


def as_bf16(mask):
    return mask.astype(F32).astype(BF16)


def prepare(count, start_hbm, source_hbm, inverse_hbm, map_hbm, trans_hbm,
            rhs_ref, link_ref, faces_ref, first_ref, second_ref,
            start_ref, source_ref, low_ref, up_ref, map_ref, trans_ref, sems):
    width = start_ref.shape[1]
    face = map_ref.shape[2]
    last = count - 1
    copies = read_all(
        (map_hbm, trans_hbm, start_hbm, source_hbm,
         inverse_hbm.at[0, pl.ds(0, face)], inverse_hbm.at[last, pl.ds(width - face, face)]),
        (map_ref, trans_ref, start_ref, source_ref, low_ref, up_ref),
        sems,
    )
    me, size = lax.axis_index("sub"), lax.axis_size("sub")
    copies[0].wait()
    copies[1].wait()
    perms = []
    for i in range(count):
        for side in range(2):
            linked = permutation(i, side, map_ref)
            column = jnp.sum(
                jnp.where(linked, trans_ref[i, side : side + 1, :], 0.0), axis=1, keepdims=True
            )
            if i == 0 and side == 0:
                column = jnp.where(me == 0, 0.0, column)
            if i == last and side == 1:
                column = jnp.where(me == size - 1, 0.0, column)
            link_ref[2 * i + side] = jnp.broadcast_to(column, (face, start_ref.shape[2]))
            perms.append(as_bf16(linked))
    for copy in copies[2:]:
        copy.wait()
    low, up = [], []
    for i in range(count):
        for side in range(2):
            rows = face_rows(side, face, width)
            to = slice(side * face, (side + 1) * face)
            value = start_ref[i, rows]
            high = value.astype(BF16)
            rest = value - high.astype(F32)
            mid = rest.astype(BF16)
            tail = (rest - mid.astype(F32)).astype(BF16)
            perm = perms[2 * i + side]
            parts = dot(perm, jnp.concatenate([high, mid, tail, source_ref[i, rows]], axis=1))
            cut = value.shape[1]
            parts = [parts[:, k * cut : (k + 1) * cut] for k in range(4)]
            rhs_ref[i, to] = parts[0] + parts[1] + parts[2] + parts[3]
            faces_ref[i, to] = value
            (up if side else low).append(value)
    zero = jnp.zeros_like(low[0])
    inner = slice(face, width - face)
    ahead, operators = [], []
    for i, matrix, at in ((last, up_ref, 1), (0, low_ref, 0)):
        columns = [
            dot(matrix[:, face_rows(side, face, width)], perms[2 * i + side], ((1,), (1,))).astype(BF16)
            for side in range(2)
        ]
        middle = (start_ref[i, inner] + source_ref[i, inner].astype(F32)).astype(BF16)
        v = jnp.concatenate(face_vector(i, count, rhs_ref, link_ref, low, up, zero, zero), axis=0)
        ahead.append(dot(matrix[:, inner], middle) + dot(jnp.concatenate(columns, axis=1), v))
        operators.append(columns[at].astype(F32))
    upward = (up[last], ahead[0], operators[0], transpose(link_ref[2 * last + 1])[:8])
    downward = (low[0], ahead[1], operators[1], transpose(link_ref[0])[:8])
    store_messages(upward, downward, first_ref, second_ref)


def prepare_rest(count, start_hbm, source_hbm, inverse_hbm, map_hbm,
                 ff_ref, fm_ref, pf_ref, rf_ref, pm_ref, rm_ref, mid_ref, wells_ref, mean_ref,
                 start_ref, source_ref, inverse_ref, map_ref, sems):
    for copy in read_all(
        (start_hbm, source_hbm, inverse_hbm, map_hbm), (start_ref, source_ref, inverse_ref, map_ref), sems
    ):
        copy.wait()
    width = start_ref.shape[1]
    face = map_ref.shape[2]
    inner = slice(face, width - face)
    for i in range(count):
        perms = [as_bf16(permutation(i, side, map_ref)) for side in range(2)]
        for side in range(2):
            to = slice(side * face, (side + 1) * face)
            rows = face_rows(side, face, width)
            columns = dot(inverse_ref[i, :, rows], perms[side], ((1,), (1,))).astype(BF16)
            ff_ref[i, :face, to] = columns[:face]
            ff_ref[i, face:, to] = columns[width - face :]
            rf_ref[i, :, to] = columns[inner]
            wells_ref[i, to] = dot(perms[side], source_ref[i, rows])
            fm_ref[i, to] = inverse_ref[i, rows, inner]
        for side in range(2):
            to = slice(side * face, (side + 1) * face)
            pf_ref[i, to] = dot(perms[side], ff_ref[i, to]).astype(BF16)
            pm_ref[i, to] = dot(perms[side], fm_ref[i, to]).astype(BF16)
        rm_ref[i] = inverse_ref[i, inner, inner]
        wells = source_ref[i, inner].astype(F32)
        mid_ref[i] = start_ref[i, inner] + wells
        wells_ref[i, 2 * face :] = wells
        mean_ref[i : i + 1] = jnp.sum(start_ref[i], axis=0, keepdims=True) / width


def load_faces(count, faces_ref):
    face = faces_ref.shape[1] // 2
    return [faces_ref[i, :face] for i in range(count)], [faces_ref[i, face:] for i in range(count)]


def window(count, first_ref, second_ref, ff_ref, y_ref, rhs_ref, link_ref, faces_ref, near_ref, near_link_ref):
    low, up = load_faces(count, faces_ref)
    face = low[0].shape[0]
    below, above = received(first_ref, second_ref, slice(0, face))
    next_below, next_above = received(first_ref, second_ref, slice(face, 2 * face))
    next_below += dot(near_ref[0], (near_link_ref[0] * low[0]).astype(BF16))
    next_above += dot(near_ref[1], (near_link_ref[1] * up[count - 1]).astype(BF16))
    _, low, up = face_sweep(count, ff_ref, y_ref, rhs_ref, link_ref, low, up, below, above)
    return face_sweep(count, ff_ref, y_ref, rhs_ref, link_ref, low, up, next_below, next_above)


def middle_window(count, opening, *refs):
    if opening:
        (first_ref, second_ref, ff_ref, y_ref, rhs_ref, link_ref, faces_ref, share_ref,
         new_faces, out_first, out_second, near_ref, near_link_ref) = refs
        face = faces_ref.shape[1] // 2
        for k, part in enumerate(received(first_ref, second_ref, slice(2 * face, 3 * face))):
            near_ref[k] = part.astype(BF16)
        for k, part in enumerate(received(first_ref, second_ref, slice(3 * face, 3 * face + 8))):
            near_link_ref[k] = transpose(jnp.broadcast_to(part[:1], (face, face)))
    else:
        (first_ref, second_ref, ff_ref, y_ref, rhs_ref, link_ref, faces_ref, near_ref, near_link_ref,
         new_faces, out_first, out_second, *next_faces) = refs
        face = faces_ref.shape[1] // 2
    _, low, up = window(
        count, first_ref, second_ref, ff_ref, y_ref, rhs_ref, link_ref, faces_ref, near_ref, near_link_ref
    )
    for i in range(count):
        new_faces[i, :face] = low[i]
        new_faces[i, face:] = up[i]
    if not opening and next_faces:
        zero = jnp.zeros_like(low[0])
        _, next_low, next_up = face_sweep(count, ff_ref, y_ref, rhs_ref, link_ref, low, up, zero, zero)
        for i in range(count):
            next_faces[0][i, :face] = next_low[i]
            next_faces[0][i, face:] = next_up[i]
        upward, downward = (up[-1], next_up[-1]), (low[0], next_low[0])
    else:
        upward, downward = outgoing(count, ff_ref, y_ref[0, :face], y_ref[count - 1, face:], rhs_ref, link_ref, low, up)
    if opening:
        upward += (share_ref[1],)
        downward += (share_ref[0],)
    store_messages(upward, downward, out_first, out_second)


def step_window(count, opening, first_ref, second_ref, ff_ref, y_ref, rhs_ref, link_ref, faces_ref, near_ref,
                near_link_ref, fm_ref, pf_ref, rf_ref, base_ref, source_ref,
                new_faces, out_first, out_second, new_rhs, new_mid, *near_share):
    face = faces_ref.shape[1] // 2
    if opening:
        for k, part in enumerate(received(first_ref, second_ref, slice(2 * face, 2 * face + 8))):
            near_share[0][k] = part
    vectors, low, up = window(
        count, first_ref, second_ref, ff_ref, y_ref, rhs_ref, link_ref, faces_ref, near_ref, near_link_ref
    )
    for i in range(count):
        new_faces[i, :face] = low[i]
        new_faces[i, face:] = up[i]
        cut = 2 * face
        new_rhs[i] = base_ref[i, :cut] + dot(pf_ref[i], vectors[i]) + source_ref[i, :cut]
        rhs = base_ref[i, cut:] + dot(rf_ref[i], vectors[i]) + source_ref[i, cut:]
        new_mid[i] = rhs
        if i == 0:
            y_low = dot(fm_ref[i, :face], rhs.astype(BF16))
        if i == count - 1:
            y_up = dot(fm_ref[i, face:], rhs.astype(BF16))
    store_messages(*outgoing(count, ff_ref, y_low, y_up, new_rhs, link_ref, low, up), out_first, out_second)


def inner_base(count, mid_ref, pm_ref, rm_ref, fm_ref, base_ref, y_ref):
    for i in range(count):
        cut = pm_ref.shape[1]
        v = mid_ref[i].astype(BF16)
        base_ref[i, :cut] = dot(pm_ref[i], v)
        base_ref[i, cut:] = dot(rm_ref[i], v)
        y_ref[i] = dot(fm_ref[i], v)


def shares(count, ff_ref, rf_ref, link_ref, mass_ref, share_ref):
    face = ff_ref.shape[1] // 2
    mass = []
    for i in range(count):
        total = jnp.sum(ff_ref[i].astype(F32), axis=0, keepdims=True)
        total += jnp.sum(rf_ref[i].astype(F32), axis=0, keepdims=True)
        width = 2 * face + rf_ref.shape[1]
        mass.append(jnp.broadcast_to(total / width, (8, 2 * face)))
        for k in range(2):
            line = mass[i][:1, k * face : (k + 1) * face]
            mass_ref[i, k * face : (k + 1) * face] = transpose(jnp.broadcast_to(line, (face, face)))
    for k, (outer, other) in enumerate(((0, 1), (count - 1, count - 2))):
        here, there = slice(k * face, (k + 1) * face), pl.ds((1 - k) * face, face)
        line = transpose(link_ref[2 * outer + k])[:8]
        inner_line = transpose(link_ref[2 * other + k])[:8]
        one = mass[outer][:, here] * line
        operator = ff_ref[outer, there, here].astype(F32)
        two = dot(mass[other][:, here] * inner_line, operator, precision=HIGH) * line
        share_ref[k] = jnp.where(iota(one.shape, 0) == 0, one, two)


def end_mean(count, mid_ref, rm_ref, fm_ref, near_share_ref, out_ref, column_ref, y_ref):
    face = y_ref.shape[1] // 2
    for k in range(2):
        for j in range(2):
            line = jnp.broadcast_to(near_share_ref[k, j : j + 1], (face, face))
            column_ref[2 * k + j] = transpose(line)
    for i in range(count):
        v = mid_ref[i].astype(BF16)
        y = dot(fm_ref[i], v)
        y_ref[i] = y
        inner = dot(rm_ref[i], v)
        total = jnp.sum(y, axis=0, keepdims=True) + jnp.sum(inner, axis=0, keepdims=True)
        out_ref[i : i + 1] = total / (2 * face + rm_ref.shape[1])


def means_payload(count, rhs_ref, link_ref, faces_ref, next_ref, near_ref, near_link_ref,
                  column_ref, mass_ref, base_mean_ref, mean_ref, op_ref, parts_ref):
    low, up = load_faces(count, faces_ref)
    next_low, next_up = load_faces(count, next_ref)
    last = count - 1
    next_below = dot(near_ref[0], (near_link_ref[0] * low[0]).astype(BF16))
    next_above = dot(near_ref[1], (near_link_ref[1] * up[last]).astype(BF16))
    rows = []
    for i in range(count):
        v_low, v_up = face_vector(i, count, rhs_ref, link_ref, next_low, next_up, next_below, next_above)
        face = v_low.shape[0]
        own = weighted(mass_ref[i, :face], v_low.astype(F32)) + weighted(mass_ref[i, face:], v_up.astype(F32))
        rows.append(base_mean_ref[i : i + 1] + own)
    rows += [mean_ref[i : i + 1] for i in range(count)]
    for k, (two, one) in ((1, (up[last], next_up[last])), (0, (low[0], next_low[0]))):
        rows.append(weighted(column_ref[2 * k], one))
        rows.append(weighted(column_ref[2 * k + 1], two))
    total = op_ref[0] * rows[0]
    for k in range(1, len(rows)):
        total += op_ref[k] * rows[k]
    parts_ref[...] = total


def weighted(column, x):
    return jnp.sum(column * x, axis=0, keepdims=True)


def payload_rows(count):
    return -(-(2 * count + 4) // 8) * 8


def last_window(count, first_ref, second_ref, ff_ref, rhs_hbm, link_ref, faces_hbm, near_ref,
                near_link_ref, rf_ref, mid_hbm, fm_ref, rm_ref, start_hbm, end_ref, out_hbm,
                y_ref, rhs_ref, faces_ref, mid_ref, start_ref, sems, out_sems):
    copies = read_all((mid_hbm, rhs_hbm, faces_hbm, start_hbm), (mid_ref, rhs_ref, faces_ref, start_ref), sems)
    copies[0].wait()
    face = faces_ref.shape[1] // 2
    width = end_ref.shape[1]
    for i in range(count):
        v = mid_ref[i].astype(BF16)
        y_ref[i] = dot(fm_ref[i], v)
        end_ref[i, face : width - face] = dot(rm_ref[i], v)
    for copy in copies[1:]:
        copy.wait()
    vectors, low, up = window(
        count, first_ref, second_ref, ff_ref, y_ref, rhs_ref, link_ref, faces_ref, near_ref, near_link_ref
    )
    later = lax.axis_index("cuts") > 0
    copies = []
    for i in range(count):
        end_ref[i, :face] = low[i]
        end_ref[i, face : width - face] += dot(rf_ref[i], vectors[i])
        end_ref[i, width - face :] = up[i]
        start_ref[i] = jnp.where(later, end_ref[i], start_ref[i])
    for i in range(count):
        copies.append(pltpu.make_async_copy(start_ref.at[i], out_hbm.at[i], out_sems.at[i]))
        copies[i].start()
    for copy in copies:
        copy.wait()


def coarse_operator(count, slices, partner_hbm, cond_hbm, out_ref, partner_ref, cond_ref, sems):
    copies = [
        pltpu.make_async_copy(partner_hbm, partner_ref, sems.at[0]),
        pltpu.make_async_copy(cond_hbm, cond_ref, sems.at[1]),
    ]
    for copy in copies:
        copy.start()
    for copy in copies:
        copy.wait()
    n = partner_ref.shape[0]
    row, col = iota((n, n), 0), iota((n, n), 1)
    weights = (jnp.abs(row - col) == 1).astype(F32)
    for b in range(n):
        to, cond = partner_ref[b], cond_ref[b]
        weights += jnp.where((row == b) & (col == to), cond, 0.0)
        weights += jnp.where((col == b) & (row == to), cond, 0.0)
    eye = (row == col).astype(F32)
    m = eye + eye * jnp.sum(weights, axis=1, keepdims=True) - weights
    for i in range(n):
        pivot = 1.0 / m[i : i + 1, i : i + 1]
        line = m[i : i + 1, :] * pivot
        column = m[:, i : i + 1]
        inner = jnp.where(col == i, -column * pivot, m - column * line)
        m = jnp.where(row == i, jnp.where(col == i, pivot, line), inner)
    here, me = lax.axis_index("cuts"), lax.axis_index("sub")
    shape = (n, payload_rows(count))
    block, item = iota(shape, 0) - me * count, iota(shape, 1)
    own = (item < count) & (block == item)
    above = (item >= 2 * count) & (item < 2 * count + 2) & (block == item - count)
    below = (item >= 2 * count + 2) & (item < 2 * count + 4) & (block == 2 * count + 1 - item)
    end = (own | above | below).astype(F32)
    start = ((item >= count) & (item < 2 * count) & (block == item - count)).astype(F32)
    ends, starts = [], []
    for _ in range(1, slices - 1):
        end, start = dot(m, end, precision=HIGH), dot(m, start, precision=HIGH)
        ends.append(end)
        starts.append(start)
    for s in range(slices):
        total = jnp.zeros(shape, F32)
        for k in range(1, slices - 1):
            if s - 1 - k >= 0:
                total += jnp.where(here == s - 1 - k, ends[k - 1], 0.0)
            if s - k >= 1:
                total -= jnp.where(here == s - k, starts[k - 1], 0.0)
        for k in range(out_ref.shape[0]):
            out_ref[k, s * n : (s + 1) * n] = jnp.broadcast_to(total[:, k : k + 1], (n, out_ref.shape[2]))


def correct(count, parts_ref, previous_ref, early_hbm, out_hbm, out_ref, sems):
    @pl.when(lax.axis_index("cuts") > 1)
    def _():
        mine = jnp.sum(parts_ref[...], axis=0)
        for i in range(count):
            out_ref[i] = previous_ref[i] + mine[i : i + 1]
        copies = [pltpu.make_async_copy(out_ref.at[i], out_hbm.at[i], sems.at[i]) for i in range(count)]
        for copy in copies:
            copy.start()
        for copy in copies:
            copy.wait()


def exchange(first, second, ahead=0):
    size, slices = lax.axis_size("sub"), lax.axis_size("cuts")
    pairs, other = [], []
    for c in range(slices):
        d = (c + ahead) % slices
        for i in range(size):
            pairs.append((c * size + i, d * size + (i ^ 1)))
            j = i + (1 if i % 2 else -1)
            if 0 <= j < size:
                other.append((c * size + i, d * size + j))
            elif ahead:
                other.append((c * size + i, d * size + i))
            else:
                other.append((c * size + i, (c ^ 1 if c ^ 1 < slices else c) * size + i))
    far = lax.ppermute(second, ("cuts", "sub"), other)
    near = lax.ppermute(first, ("cuts", "sub"), pairs)
    return near, far


def on_device(slices, start_states, source, block_inverse, face_map, transmissibility, partner, fracture_cond):
    start = start_states[0]
    count, width, scenarios = start.shape
    face = face_map.shape[-1]
    inner = width - 2 * face
    sub = lax.axis_size("sub")
    sds = jax.ShapeDtypeStruct
    message = sds((2 * face, scenarios), F32)
    opening = sds((3 * face + 8, scenarios), F32)
    sharing = sds((2 * face + 8, scenarios), F32)
    share_shape = sds((2, 8, face), F32)
    faces_shape = sds((count, 2 * face, scenarios), F32)
    rhs_shape = sds((count, width, scenarios), F32)
    held = [
        pltpu.with_memory_space_constraint(a, pltpu.HBM)
        for a in (start, source, block_inverse, face_map, transmissibility)
    ]
    buffers = [pltpu.VMEM(a.shape, a.dtype) for a in (start, source)]
    row = pltpu.VMEM((face, width), BF16)
    tables = [pltpu.VMEM(a.shape, a.dtype) for a in (face_map, transmissibility)]
    mid_shape = sds((count, inner, scenarios), F32)
    rhs, link, faces, first, second = call(
        functools.partial(prepare, count),
        [faces_shape, sds((2 * count, face, scenarios), F32), faces_shape, opening, opening],
        held,
        stay=range(5),
        scratch=buffers + [row, row] + tables + [pltpu.SemaphoreType.DMA((6,))],
    )
    ff, fm, pf, rf, pm, rm, mid, wells, mean = call(
        functools.partial(prepare_rest, count),
        [
            sds((count, 2 * face, 2 * face), BF16),
            sds((count, 2 * face, inner), BF16),
            sds((count, 2 * face, 2 * face), BF16),
            sds((count, inner, 2 * face), BF16),
            sds((count, 2 * face, inner), BF16),
            sds((count, inner, inner), BF16),
            mid_shape,
            rhs_shape,
            sds((count, scenarios), F32),
        ],
        held[:4],
        stay=range(4),
        scratch=buffers
        + [pltpu.VMEM(block_inverse.shape, BF16), tables[0], pltpu.SemaphoreType.DMA((4,))],
    )
    blocks = partner.shape[0]
    (op,) = call(
        functools.partial(coarse_operator, count, slices),
        [sds((2 * count + 4, slices * blocks, scenarios), F32)],
        [pltpu.with_memory_space_constraint(v, pltpu.HBM) for v in (partner, fracture_cond)],
        stay=range(2),
        scratch=[
            pltpu.SMEM((blocks,), jnp.int32),
            pltpu.SMEM((blocks,), F32),
            pltpu.SemaphoreType.DMA((2,)),
        ],
    )
    mass, share = call(
        functools.partial(shares, count),
        [faces_shape, share_shape],
        (ff, rf, link),
    )
    near = near_link = None
    ring = [(i, (i + 1) % slices) for i in range(slices)]
    for step in range(FINE_STEPS):
        final = step == FINE_STEPS - 1
        if final:
            taken_mid = lax.ppermute(mid, "cuts", ring)
            taken_rhs = lax.ppermute(rhs, "cuts", ring)
            base_mean, near_column, y = call(
                functools.partial(end_mean, count),
                [sds((count, scenarios), F32), sds((4, face, scenarios), F32), faces_shape],
                (mid, rm, fm, near_share),
            )
        else:
            base, y = call(functools.partial(inner_base, count), [rhs_shape, faces_shape], (mid, pm, rm, fm))
        for turn in range(0, SWEEPS, 2):
            ending = final and turn == SWEEPS - 2
            first, second = exchange(first, second, 1 if ending else 0)
            common = (first, second, ff, y, rhs, link, faces)
            if turn < SWEEPS - 2:
                if near is None:
                    faces, first, second, near, near_link = call(
                        functools.partial(middle_window, count, True),
                        [faces_shape, sharing, sharing, sds((2, face, face), BF16), sds((2, face, scenarios), F32)],
                        common + (share,),
                    )
                else:
                    faces, first, second, *ahead = call(
                        functools.partial(middle_window, count, False),
                        [faces_shape, message, message] + [faces_shape] * final,
                        common + (near, near_link),
                    )
            elif not ending:
                outs = [faces_shape, message, message, faces_shape, mid_shape]
                outs = call(
                    functools.partial(step_window, count, step == 0),
                    outs + [share_shape] if step == 0 else outs,
                    common + (near, near_link, fm, pf, rf, base, wells),
                )
                faces, first, second, rhs, mid = outs[:5]
                if step == 0:
                    near_share = outs[5]
    taken_faces = lax.ppermute(faces, "cuts", ring)
    (parts,) = call(
        functools.partial(means_payload, count),
        [sds((slices * blocks, scenarios), F32)],
        (rhs, link, faces, ahead[0], near, near_link, near_column, mass, base_mean, mean, op),
    )
    parts = parts.reshape(slices * sub, count, scenarios)
    parts = lax.all_to_all(parts, ("cuts", "sub"), 0, 0, tiled=True)
    taken_rhs, taken_faces, taken_mid = (
        pltpu.with_memory_space_constraint(v, pltpu.HBM) for v in (taken_rhs, taken_faces, taken_mid)
    )
    previous, early = call(
        functools.partial(last_window, count),
        [rhs_shape, rhs_shape],
        (first, second, ff, taken_rhs, link, taken_faces, near, near_link, rf, taken_mid, fm, rm, held[0]),
        stay=(3, 5, 9, 12),
        stay_out=(1,),
        scratch=[pltpu.VMEM(faces_shape.shape, F32)] * 3
        + [
            pltpu.VMEM(mid_shape.shape, F32),
            pltpu.VMEM(rhs_shape.shape, F32),
            pltpu.SemaphoreType.DMA((4,)),
            pltpu.SemaphoreType.DMA((count,)),
        ],
    )
    (result,) = call(
        functools.partial(correct, count),
        [rhs_shape],
        (parts, previous, early),
        stay=(2,),
        stay_out=(0,),
        scratch=[pltpu.VMEM(rhs_shape.shape, F32), pltpu.SemaphoreType.DMA((count,))],
        aliases={2: 0},
    )
    return result[None]


def solution(mesh):
    slices = mesh.shape["cuts"]

    def body(*args):
        return on_device(slices, *args)

    in_specs = (
        P("cuts", "sub", None, None),
        P("sub", None, None),
        P("sub", None, None),
        P("sub", None, None),
        P("sub", None, None),
        P(),
        P(),
    )
    return jax.shard_map(
        body,
        mesh=mesh,
        in_specs=in_specs,
        out_specs=P("cuts", "sub", None, None),
        check_vma=False,
    )
```

```python
import functools

import jax
import jax.numpy as jnp
from jax import lax
from jax.experimental import pallas as pl
from jax.experimental.pallas import tpu as pltpu
from jax.sharding import PartitionSpec as P


FINE_STEPS = 4
SWEEPS = 4
F32 = jnp.float32
BF16 = jnp.bfloat16
HIGH = lax.Precision.HIGHEST


def dot(a, b, dims=((1,), (0,)), precision=None):
    return lax.dot_general(a, b, (dims, ((), ())), precision=precision, preferred_element_type=F32)


def transpose(x):
    return jnp.transpose(x, (1, 0))


def iota(shape, axis):
    return lax.broadcasted_iota(jnp.int32, shape, axis)


def call(body, out_shape, args, flops=1 << 28, stay=(), stay_out=(), scratch=(), aliases=None):
    size = sum(a.size * a.dtype.itemsize for a in list(args) + list(out_shape))
    vmem = pl.BlockSpec(memory_space=pltpu.VMEM)
    hbm = pl.BlockSpec(memory_space=pltpu.HBM)
    return pl.pallas_call(
        body,
        out_shape=out_shape,
        in_specs=[hbm if k in stay else vmem for k in range(len(args))],
        out_specs=[hbm if k in stay_out else vmem for k in range(len(out_shape))],
        scratch_shapes=list(scratch),
        input_output_aliases=aliases or {},
        compiler_params=pltpu.CompilerParams(vmem_limit_bytes=24 << 20),
        cost_estimate=pl.CostEstimate(flops=flops, bytes_accessed=size, transcendentals=0),
    )(*args)


def face_vector(i, count, rhs_ref, link_ref, low, up, below, above):
    face = low[0].shape[0]
    under = below if i == 0 else up[i - 1]
    over = above if i == count - 1 else low[i + 1]
    v_low = rhs_ref[i, :face] + link_ref[2 * i] * under
    v_up = rhs_ref[i, face : 2 * face] + link_ref[2 * i + 1] * over
    return v_low.astype(BF16), v_up.astype(BF16)


def face_sweep(count, ff_ref, y_ref, rhs_ref, link_ref, low, up, below, above):
    face = low[0].shape[0]
    vectors, new_low, new_up = [], [], []
    for i in range(count):
        v = jnp.concatenate(face_vector(i, count, rhs_ref, link_ref, low, up, below, above), axis=0)
        x = y_ref[i] + dot(ff_ref[i], v)
        vectors.append(v)
        new_low.append(x[:face])
        new_up.append(x[face:])
    return vectors, new_low, new_up


def outgoing(count, ff_ref, y_low, y_up, rhs_ref, link_ref, low, up):
    face = low[0].shape[0]
    last = count - 1
    zero = jnp.zeros_like(low[0])
    v = jnp.concatenate(face_vector(last, count, rhs_ref, link_ref, low, up, zero, zero), axis=0)
    next_up = y_up + dot(ff_ref[last, face:], v)
    v = jnp.concatenate(face_vector(0, count, rhs_ref, link_ref, low, up, zero, zero), axis=0)
    next_low = y_low + dot(ff_ref[0, :face], v)
    return (up[last], next_up), (low[0], next_low)


def store_messages(upward, downward, first_ref, second_ref):
    even = lax.rem(lax.axis_index("sub"), 2) == 0
    at = 0
    for one, other in zip(upward, downward):
        rows = pl.ds(at, one.shape[0])
        first_ref[rows] = jnp.where(even, one, other)
        second_ref[rows] = jnp.where(even, other, one)
        at += one.shape[0]


def received(first_ref, second_ref, rows):
    even = lax.rem(lax.axis_index("sub"), 2) == 0
    first, second = first_ref[rows], second_ref[rows]
    return jnp.where(even, second, first), jnp.where(even, first, second)


def read_all(sources, targets, sems):
    copies = [pltpu.make_async_copy(a, b, sems.at[k]) for k, (a, b) in enumerate(zip(sources, targets))]
    for copy in copies:
        copy.start()
    return copies


def face_rows(side, face, width):
    return slice(0, face) if side == 0 else slice(width - face, width)


def permutation(i, side, map_ref):
    face = map_ref.shape[2]
    return iota((face, face), 0) == map_ref[i, side : side + 1, :]


def as_bf16(mask):
    return mask.astype(F32).astype(BF16)


def prepare(count, start_hbm, source_hbm, inverse_hbm, map_hbm, trans_hbm,
            rhs_ref, link_ref, faces_ref, first_ref, second_ref,
            start_ref, source_ref, low_ref, up_ref, map_ref, trans_ref, sems):
    width = start_ref.shape[1]
    face = map_ref.shape[2]
    last = count - 1
    copies = read_all(
        (map_hbm, trans_hbm, start_hbm, source_hbm,
         inverse_hbm.at[0, pl.ds(0, face)], inverse_hbm.at[last, pl.ds(width - face, face)]),
        (map_ref, trans_ref, start_ref, source_ref, low_ref, up_ref),
        sems,
    )
    me, size = lax.axis_index("sub"), lax.axis_size("sub")
    copies[0].wait()
    copies[1].wait()
    perms = []
    for i in range(count):
        for side in range(2):
            linked = permutation(i, side, map_ref)
            column = jnp.sum(
                jnp.where(linked, trans_ref[i, side : side + 1, :], 0.0), axis=1, keepdims=True
            )
            if i == 0 and side == 0:
                column = jnp.where(me == 0, 0.0, column)
            if i == last and side == 1:
                column = jnp.where(me == size - 1, 0.0, column)
            link_ref[2 * i + side] = jnp.broadcast_to(column, (face, start_ref.shape[2]))
            perms.append(as_bf16(linked))
    for copy in copies[2:]:
        copy.wait()
    low, up = [], []
    for i in range(count):
        for side in range(2):
            rows = face_rows(side, face, width)
            to = slice(side * face, (side + 1) * face)
            value = start_ref[i, rows]
            high = value.astype(BF16)
            rest = value - high.astype(F32)
            mid = rest.astype(BF16)
            tail = (rest - mid.astype(F32)).astype(BF16)
            perm = perms[2 * i + side]
            parts = dot(perm, jnp.concatenate([high, mid, tail, source_ref[i, rows]], axis=1))
            cut = value.shape[1]
            parts = [parts[:, k * cut : (k + 1) * cut] for k in range(4)]
            rhs_ref[i, to] = parts[0] + parts[1] + parts[2] + parts[3]
            faces_ref[i, to] = value
            (up if side else low).append(value)
    zero = jnp.zeros_like(low[0])
    inner = slice(face, width - face)
    ahead, operators = [], []
    for i, matrix, at in ((last, up_ref, 1), (0, low_ref, 0)):
        columns = [
            dot(matrix[:, face_rows(side, face, width)], perms[2 * i + side], ((1,), (1,))).astype(BF16)
            for side in range(2)
        ]
        middle = (start_ref[i, inner] + source_ref[i, inner].astype(F32)).astype(BF16)
        v = jnp.concatenate(face_vector(i, count, rhs_ref, link_ref, low, up, zero, zero), axis=0)
        ahead.append(dot(matrix[:, inner], middle) + dot(jnp.concatenate(columns, axis=1), v))
        operators.append(columns[at].astype(F32))
    upward = (up[last], ahead[0], operators[0], transpose(link_ref[2 * last + 1])[:8])
    downward = (low[0], ahead[1], operators[1], transpose(link_ref[0])[:8])
    store_messages(upward, downward, first_ref, second_ref)


def prepare_rest(count, start_hbm, source_hbm, inverse_hbm, map_hbm,
                 ff_ref, fm_ref, pf_ref, rf_ref, pm_ref, rm_ref, mid_ref, wells_ref, mean_ref,
                 start_ref, source_ref, inverse_ref, map_ref, sems):
    for copy in read_all(
        (start_hbm, source_hbm, inverse_hbm, map_hbm), (start_ref, source_ref, inverse_ref, map_ref), sems
    ):
        copy.wait()
    width = start_ref.shape[1]
    face = map_ref.shape[2]
    inner = slice(face, width - face)
    for i in range(count):
        perms = [as_bf16(permutation(i, side, map_ref)) for side in range(2)]
        for side in range(2):
            to = slice(side * face, (side + 1) * face)
            rows = face_rows(side, face, width)
            columns = dot(inverse_ref[i, :, rows], perms[side], ((1,), (1,))).astype(BF16)
            ff_ref[i, :face, to] = columns[:face]
            ff_ref[i, face:, to] = columns[width - face :]
            rf_ref[i, :, to] = columns[inner]
            wells_ref[i, to] = dot(perms[side], source_ref[i, rows])
            fm_ref[i, to] = inverse_ref[i, rows, inner]
        for side in range(2):
            to = slice(side * face, (side + 1) * face)
            pf_ref[i, to] = dot(perms[side], ff_ref[i, to]).astype(BF16)
            pm_ref[i, to] = dot(perms[side], fm_ref[i, to]).astype(BF16)
        rm_ref[i] = inverse_ref[i, inner, inner]
        wells = source_ref[i, inner].astype(F32)
        mid_ref[i] = start_ref[i, inner] + wells
        wells_ref[i, 2 * face :] = wells
        mean_ref[i : i + 1] = jnp.sum(start_ref[i], axis=0, keepdims=True) / width


def load_faces(count, faces_ref):
    face = faces_ref.shape[1] // 2
    return [faces_ref[i, :face] for i in range(count)], [faces_ref[i, face:] for i in range(count)]


def window(count, first_ref, second_ref, ff_ref, y_ref, rhs_ref, link_ref, faces_ref, near_ref, near_link_ref):
    low, up = load_faces(count, faces_ref)
    face = low[0].shape[0]
    below, above = received(first_ref, second_ref, slice(0, face))
    next_below, next_above = received(first_ref, second_ref, slice(face, 2 * face))
    next_below += dot(near_ref[0], (near_link_ref[0] * low[0]).astype(BF16))
    next_above += dot(near_ref[1], (near_link_ref[1] * up[count - 1]).astype(BF16))
    _, low, up = face_sweep(count, ff_ref, y_ref, rhs_ref, link_ref, low, up, below, above)
    return face_sweep(count, ff_ref, y_ref, rhs_ref, link_ref, low, up, next_below, next_above)


def middle_window(count, opening, *refs):
    if opening:
        (first_ref, second_ref, ff_ref, y_ref, rhs_ref, link_ref, faces_ref, share_ref,
         new_faces, out_first, out_second, near_ref, near_link_ref) = refs
        face = faces_ref.shape[1] // 2
        for k, part in enumerate(received(first_ref, second_ref, slice(2 * face, 3 * face))):
            near_ref[k] = part.astype(BF16)
        for k, part in enumerate(received(first_ref, second_ref, slice(3 * face, 3 * face + 8))):
            near_link_ref[k] = transpose(jnp.broadcast_to(part[:1], (face, face)))
    else:
        (first_ref, second_ref, ff_ref, y_ref, rhs_ref, link_ref, faces_ref, near_ref, near_link_ref,
         new_faces, out_first, out_second, *next_faces) = refs
        face = faces_ref.shape[1] // 2
    _, low, up = window(
        count, first_ref, second_ref, ff_ref, y_ref, rhs_ref, link_ref, faces_ref, near_ref, near_link_ref
    )
    for i in range(count):
        new_faces[i, :face] = low[i]
        new_faces[i, face:] = up[i]
    if not opening and next_faces:
        zero = jnp.zeros_like(low[0])
        _, next_low, next_up = face_sweep(count, ff_ref, y_ref, rhs_ref, link_ref, low, up, zero, zero)
        for i in range(count):
            next_faces[0][i, :face] = next_low[i]
            next_faces[0][i, face:] = next_up[i]
        next_faces[1][0] = dot(near_ref[0], (near_link_ref[0] * low[0]).astype(BF16))
        next_faces[1][1] = dot(near_ref[1], (near_link_ref[1] * up[-1]).astype(BF16))
        upward, downward = (up[-1], next_up[-1]), (low[0], next_low[0])
    else:
        upward, downward = outgoing(count, ff_ref, y_ref[0, :face], y_ref[count - 1, face:], rhs_ref, link_ref, low, up)
    if opening:
        upward += (share_ref[1],)
        downward += (share_ref[0],)
    store_messages(upward, downward, out_first, out_second)


def step_window(count, opening, first_ref, second_ref, ff_ref, y_ref, rhs_ref, link_ref, faces_ref, near_ref,
                near_link_ref, fm_ref, pf_ref, rf_ref, base_ref, source_ref,
                new_faces, out_first, out_second, new_rhs, new_mid, *near_share):
    face = faces_ref.shape[1] // 2
    if opening:
        for k, part in enumerate(received(first_ref, second_ref, slice(2 * face, 2 * face + 8))):
            near_share[0][k] = part
    vectors, low, up = window(
        count, first_ref, second_ref, ff_ref, y_ref, rhs_ref, link_ref, faces_ref, near_ref, near_link_ref
    )
    for i in range(count):
        new_faces[i, :face] = low[i]
        new_faces[i, face:] = up[i]
        cut = 2 * face
        new_rhs[i] = base_ref[i, :cut] + dot(pf_ref[i], vectors[i]) + source_ref[i, :cut]
        rhs = base_ref[i, cut:] + dot(rf_ref[i], vectors[i]) + source_ref[i, cut:]
        new_mid[i] = rhs
        if i == 0:
            y_low = dot(fm_ref[i, :face], rhs.astype(BF16))
        if i == count - 1:
            y_up = dot(fm_ref[i, face:], rhs.astype(BF16))
    store_messages(*outgoing(count, ff_ref, y_low, y_up, new_rhs, link_ref, low, up), out_first, out_second)


def inner_base(count, mid_ref, pm_ref, rm_ref, fm_ref, base_ref, y_ref):
    for i in range(count):
        cut = pm_ref.shape[1]
        v = mid_ref[i].astype(BF16)
        base_ref[i, :cut] = dot(pm_ref[i], v)
        base_ref[i, cut:] = dot(rm_ref[i], v)
        y_ref[i] = dot(fm_ref[i], v)


def shares(count, ff_ref, rf_ref, link_ref, mass_ref, share_ref):
    face = ff_ref.shape[1] // 2
    mass = []
    for i in range(count):
        total = jnp.sum(ff_ref[i].astype(F32), axis=0, keepdims=True)
        total += jnp.sum(rf_ref[i].astype(F32), axis=0, keepdims=True)
        width = 2 * face + rf_ref.shape[1]
        mass.append(jnp.broadcast_to(total / width, (8, 2 * face)))
        for k in range(2):
            line = mass[i][:1, k * face : (k + 1) * face]
            mass_ref[i, k * face : (k + 1) * face] = transpose(jnp.broadcast_to(line, (face, face)))
    for k, (outer, other) in enumerate(((0, 1), (count - 1, count - 2))):
        here, there = slice(k * face, (k + 1) * face), pl.ds((1 - k) * face, face)
        line = transpose(link_ref[2 * outer + k])[:8]
        inner_line = transpose(link_ref[2 * other + k])[:8]
        one = mass[outer][:, here] * line
        operator = ff_ref[outer, there, here].astype(F32)
        two = dot(mass[other][:, here] * inner_line, operator, precision=HIGH) * line
        share_ref[k] = jnp.where(iota(one.shape, 0) == 0, one, two)


def end_mean(count, mid_ref, rm_ref, fm_ref, near_share_ref, out_ref, column_ref, y_ref):
    face = y_ref.shape[1] // 2
    for k in range(2):
        for j in range(2):
            line = jnp.broadcast_to(near_share_ref[k, j : j + 1], (face, face))
            column_ref[2 * k + j] = transpose(line)
    for i in range(count):
        v = mid_ref[i].astype(BF16)
        y = dot(fm_ref[i], v)
        y_ref[i] = y
        inner = dot(rm_ref[i], v)
        total = jnp.sum(y, axis=0, keepdims=True) + jnp.sum(inner, axis=0, keepdims=True)
        out_ref[i : i + 1] = total / (2 * face + rm_ref.shape[1])


def means_payload(count, rhs_ref, link_ref, faces_ref, next_ref, outer_ref,
                  column_ref, mass_ref, base_mean_ref, mean_ref, op_ref, parts_ref):
    low, up = load_faces(count, faces_ref)
    next_low, next_up = load_faces(count, next_ref)
    last = count - 1
    next_below, next_above = outer_ref[0], outer_ref[1]
    rows = []
    for i in range(count):
        v_low, v_up = face_vector(i, count, rhs_ref, link_ref, next_low, next_up, next_below, next_above)
        face = v_low.shape[0]
        own = weighted(mass_ref[i, :face], v_low.astype(F32)) + weighted(mass_ref[i, face:], v_up.astype(F32))
        rows.append(base_mean_ref[i : i + 1] + own)
    rows += [mean_ref[i : i + 1] for i in range(count)]
    for k, (two, one) in ((1, (up[last], next_up[last])), (0, (low[0], next_low[0]))):
        rows.append(weighted(column_ref[2 * k], one))
        rows.append(weighted(column_ref[2 * k + 1], two))
    total = op_ref[0] * rows[0]
    for k in range(1, len(rows)):
        total += op_ref[k] * rows[k]
    parts_ref[...] = total


def weighted(column, x):
    return jnp.sum(column * x, axis=0, keepdims=True)


def payload_rows(count):
    return -(-(2 * count + 4) // 8) * 8


def last_window(count, first_ref, second_ref, ff_ref, rhs_hbm, link_ref, faces_hbm, near_ref,
                near_link_ref, rf_ref, mid_hbm, fm_ref, rm_ref, start_hbm, end_ref, out_hbm,
                y_ref, rhs_ref, faces_ref, mid_ref, start_ref, sems, out_sems):
    copies = read_all((mid_hbm, rhs_hbm, faces_hbm, start_hbm), (mid_ref, rhs_ref, faces_ref, start_ref), sems)
    copies[0].wait()
    face = faces_ref.shape[1] // 2
    width = end_ref.shape[1]
    for i in range(count):
        v = mid_ref[i].astype(BF16)
        y_ref[i] = dot(fm_ref[i], v)
        end_ref[i, face : width - face] = dot(rm_ref[i], v)
    for copy in copies[1:]:
        copy.wait()
    vectors, low, up = window(
        count, first_ref, second_ref, ff_ref, y_ref, rhs_ref, link_ref, faces_ref, near_ref, near_link_ref
    )
    later = lax.axis_index("cuts") > 0
    copies = []
    for i in range(count):
        end_ref[i, :face] = low[i]
        end_ref[i, face : width - face] += dot(rf_ref[i], vectors[i])
        end_ref[i, width - face :] = up[i]
        start_ref[i] = jnp.where(later, end_ref[i], start_ref[i])
    for i in range(count):
        copies.append(pltpu.make_async_copy(start_ref.at[i], out_hbm.at[i], out_sems.at[i]))
        copies[i].start()
    for copy in copies:
        copy.wait()


def coarse_operator(count, slices, partner_hbm, cond_hbm, out_ref, partner_ref, cond_ref, sems):
    copies = [
        pltpu.make_async_copy(partner_hbm, partner_ref, sems.at[0]),
        pltpu.make_async_copy(cond_hbm, cond_ref, sems.at[1]),
    ]
    for copy in copies:
        copy.start()
    for copy in copies:
        copy.wait()
    n = partner_ref.shape[0]
    row, col = iota((n, n), 0), iota((n, n), 1)
    weights = (jnp.abs(row - col) == 1).astype(F32)
    for b in range(n):
        to, cond = partner_ref[b], cond_ref[b]
        weights += jnp.where((row == b) & (col == to), cond, 0.0)
        weights += jnp.where((col == b) & (row == to), cond, 0.0)
    eye = (row == col).astype(F32)
    m = eye + eye * jnp.sum(weights, axis=1, keepdims=True) - weights
    for i in range(n):
        pivot = 1.0 / m[i : i + 1, i : i + 1]
        line = m[i : i + 1, :] * pivot
        column = m[:, i : i + 1]
        inner = jnp.where(col == i, -column * pivot, m - column * line)
        m = jnp.where(row == i, jnp.where(col == i, pivot, line), inner)
    here, me = lax.axis_index("cuts"), lax.axis_index("sub")
    shape = (n, payload_rows(count))
    block, item = iota(shape, 0) - me * count, iota(shape, 1)
    own = (item < count) & (block == item)
    above = (item >= 2 * count) & (item < 2 * count + 2) & (block == item - count)
    below = (item >= 2 * count + 2) & (item < 2 * count + 4) & (block == 2 * count + 1 - item)
    end = (own | above | below).astype(F32)
    start = ((item >= count) & (item < 2 * count) & (block == item - count)).astype(F32)
    ends, starts = [], []
    for _ in range(1, slices - 1):
        end, start = dot(m, end, precision=HIGH), dot(m, start, precision=HIGH)
        ends.append(end)
        starts.append(start)
    for s in range(slices):
        total = jnp.zeros(shape, F32)
        for k in range(1, slices - 1):
            if s - 1 - k >= 0:
                total += jnp.where(here == s - 1 - k, ends[k - 1], 0.0)
            if s - k >= 1:
                total -= jnp.where(here == s - k, starts[k - 1], 0.0)
        for k in range(out_ref.shape[0]):
            out_ref[k, s * n : (s + 1) * n] = jnp.broadcast_to(total[:, k : k + 1], (n, out_ref.shape[2]))


def correct(count, parts_ref, previous_ref, early_hbm, out_hbm, out_ref, sems):
    @pl.when(lax.axis_index("cuts") > 1)
    def _():
        mine = jnp.sum(parts_ref[...], axis=0)
        for i in range(count):
            out_ref[i] = previous_ref[i] + mine[i : i + 1]
        copies = [pltpu.make_async_copy(out_ref.at[i], out_hbm.at[i], sems.at[i]) for i in range(count)]
        for copy in copies:
            copy.start()
        for copy in copies:
            copy.wait()


def exchange(first, second, ahead=0):
    size, slices = lax.axis_size("sub"), lax.axis_size("cuts")
    pairs, other = [], []
    for c in range(slices):
        d = (c + ahead) % slices
        for i in range(size):
            pairs.append((c * size + i, d * size + (i ^ 1)))
            j = i + (1 if i % 2 else -1)
            if 0 <= j < size:
                other.append((c * size + i, d * size + j))
            elif ahead:
                other.append((c * size + i, d * size + i))
            else:
                other.append((c * size + i, (c ^ 1 if c ^ 1 < slices else c) * size + i))
    far = lax.ppermute(second, ("cuts", "sub"), other)
    near = lax.ppermute(first, ("cuts", "sub"), pairs)
    return near, far


def on_device(slices, start_states, source, block_inverse, face_map, transmissibility, partner, fracture_cond):
    start = start_states[0]
    count, width, scenarios = start.shape
    face = face_map.shape[-1]
    inner = width - 2 * face
    sub = lax.axis_size("sub")
    sds = jax.ShapeDtypeStruct
    message = sds((2 * face, scenarios), F32)
    opening = sds((3 * face + 8, scenarios), F32)
    sharing = sds((2 * face + 8, scenarios), F32)
    share_shape = sds((2, 8, face), F32)
    faces_shape = sds((count, 2 * face, scenarios), F32)
    rhs_shape = sds((count, width, scenarios), F32)
    held = [
        pltpu.with_memory_space_constraint(a, pltpu.HBM)
        for a in (start, source, block_inverse, face_map, transmissibility)
    ]
    buffers = [pltpu.VMEM(a.shape, a.dtype) for a in (start, source)]
    row = pltpu.VMEM((face, width), BF16)
    tables = [pltpu.VMEM(a.shape, a.dtype) for a in (face_map, transmissibility)]
    mid_shape = sds((count, inner, scenarios), F32)
    rhs, link, faces, first, second = call(
        functools.partial(prepare, count),
        [faces_shape, sds((2 * count, face, scenarios), F32), faces_shape, opening, opening],
        held,
        stay=range(5),
        scratch=buffers + [row, row] + tables + [pltpu.SemaphoreType.DMA((6,))],
    )
    ff, fm, pf, rf, pm, rm, mid, wells, mean = call(
        functools.partial(prepare_rest, count),
        [
            sds((count, 2 * face, 2 * face), BF16),
            sds((count, 2 * face, inner), BF16),
            sds((count, 2 * face, 2 * face), BF16),
            sds((count, inner, 2 * face), BF16),
            sds((count, 2 * face, inner), BF16),
            sds((count, inner, inner), BF16),
            mid_shape,
            rhs_shape,
            sds((count, scenarios), F32),
        ],
        held[:4],
        stay=range(4),
        scratch=buffers
        + [pltpu.VMEM(block_inverse.shape, BF16), tables[0], pltpu.SemaphoreType.DMA((4,))],
    )
    blocks = partner.shape[0]
    (op,) = call(
        functools.partial(coarse_operator, count, slices),
        [sds((2 * count + 4, slices * blocks, scenarios), F32)],
        [pltpu.with_memory_space_constraint(v, pltpu.HBM) for v in (partner, fracture_cond)],
        stay=range(2),
        scratch=[
            pltpu.SMEM((blocks,), jnp.int32),
            pltpu.SMEM((blocks,), F32),
            pltpu.SemaphoreType.DMA((2,)),
        ],
    )
    mass, share = call(
        functools.partial(shares, count),
        [faces_shape, share_shape],
        (ff, rf, link),
    )
    near = near_link = None
    ring = [(i, (i + 1) % slices) for i in range(slices)]
    for step in range(FINE_STEPS):
        final = step == FINE_STEPS - 1
        if final:
            taken_mid = lax.ppermute(mid, "cuts", ring)
            taken_rhs = lax.ppermute(rhs, "cuts", ring)
            base_mean, near_column, y = call(
                functools.partial(end_mean, count),
                [sds((count, scenarios), F32), sds((4, face, scenarios), F32), faces_shape],
                (mid, rm, fm, near_share),
            )
        else:
            base, y = call(functools.partial(inner_base, count), [rhs_shape, faces_shape], (mid, pm, rm, fm))
        for turn in range(0, SWEEPS, 2):
            ending = final and turn == SWEEPS - 2
            first, second = exchange(first, second, 1 if ending else 0)
            common = (first, second, ff, y, rhs, link, faces)
            if turn < SWEEPS - 2:
                if near is None:
                    faces, first, second, near, near_link = call(
                        functools.partial(middle_window, count, True),
                        [faces_shape, sharing, sharing, sds((2, face, face), BF16), sds((2, face, scenarios), F32)],
                        common + (share,),
                    )
                else:
                    faces, first, second, *ahead = call(
                        functools.partial(middle_window, count, False),
                        [faces_shape, message, message]
                        + [faces_shape, sds((2, face, scenarios), F32)] * final,
                        common + (near, near_link),
                    )
            elif not ending:
                outs = [faces_shape, message, message, faces_shape, mid_shape]
                outs = call(
                    functools.partial(step_window, count, step == 0),
                    outs + [share_shape] if step == 0 else outs,
                    common + (near, near_link, fm, pf, rf, base, wells),
                )
                faces, first, second, rhs, mid = outs[:5]
                if step == 0:
                    near_share = outs[5]
    taken_faces = lax.ppermute(faces, "cuts", ring)
    (parts,) = call(
        functools.partial(means_payload, count),
        [sds((slices * blocks, scenarios), F32)],
        (rhs, link, faces, *ahead, near_column, mass, base_mean, mean, op),
    )
    parts = parts.reshape(slices * sub, count, scenarios)
    parts = lax.all_to_all(parts, ("cuts", "sub"), 0, 0, tiled=True)
    taken_rhs, taken_faces, taken_mid = (
        pltpu.with_memory_space_constraint(v, pltpu.HBM) for v in (taken_rhs, taken_faces, taken_mid)
    )
    previous, early = call(
        functools.partial(last_window, count),
        [rhs_shape, rhs_shape],
        (first, second, ff, taken_rhs, link, taken_faces, near, near_link, rf, taken_mid, fm, rm, held[0]),
        stay=(3, 5, 9, 12),
        stay_out=(1,),
        scratch=[pltpu.VMEM(faces_shape.shape, F32)] * 3
        + [
            pltpu.VMEM(mid_shape.shape, F32),
            pltpu.VMEM(rhs_shape.shape, F32),
            pltpu.SemaphoreType.DMA((4,)),
            pltpu.SemaphoreType.DMA((count,)),
        ],
    )
    (result,) = call(
        functools.partial(correct, count),
        [rhs_shape],
        (parts, previous, early),
        stay=(2,),
        stay_out=(0,),
        scratch=[pltpu.VMEM(rhs_shape.shape, F32), pltpu.SemaphoreType.DMA((count,))],
        aliases={2: 0},
    )
    return result[None]


def solution(mesh):
    slices = mesh.shape["cuts"]

    def body(*args):
        return on_device(slices, *args)

    in_specs = (
        P("cuts", "sub", None, None),
        P("sub", None, None),
        P("sub", None, None),
        P("sub", None, None),
        P("sub", None, None),
        P(),
        P(),
    )
    return jax.shard_map(
        body,
        mesh=mesh,
        in_specs=in_specs,
        out_specs=P("cuts", "sub", None, None),
        check_vma=False,
    )
```
